256 devices in a mesh: slab: 64 (over z, x, core), view: 4 (over y).
Axes of the slice: x: 4, y: 4, z: 8, core: 2. Of those that a mesh axis runs over, the one named last changes fastest.
Arguments:
- activity: float32 [2048, 32, 1024], P('slab'), may hold values from 0.5 to 2
- sensitivity: float32 [2048, 32, 1024], P('slab'), may hold values from 1 to 8
- psf_width: float32 [2048], P('slab'), may hold values from 0.05 to 0.3
- measured: bfloat16 [4, 4096, 32, 128], P('view', 'slab'), may hold values from 0.25 to 4
- block_slab: int32 [4, 4096, 1], P('view', 'slab'), may hold values from 0 to 63; in each aligned block of 64 rows (0 to 63, 64 to 127, ..., all dimensions but the last counted through in order) at most 2 rows name the same one
- block_line: int32 [4, 4096], P('view', 'slab'), may hold values from 0 to 31
- block_angle: int32 [4, 4096], P('view', 'slab'), may hold values from 0 to 7
- subset_views: int32 [4, 8], P('view'), may hold values from 0 to 335
Outputs:
- updated: float32 [2048, 32, 1024], P('slab')
The draws below stay inside these ranges and needn't reach their ends.
Inputs may be any that keep to these rules, and one draw needn't show every extreme that they name: `block_slab`: among the 64 blocks of one device (aligned blocks of 64 rows) no slab is named more than 2 times, a bound that some block reaches.
All inputs are finite; a program needn't handle non-finite values.
Results may differ from the reference program's by a relative error of at most 0.0014.
Values may be sent and summed in bfloat16 or wider, within the bound.
A program may use at most 64 MiB of HBM per device.

```python
import math
import jax
import jax.numpy as jnp
import numpy as np
from jax import lax

ZS = 32
LINES = 32
VL = 1024
BINS = 128
ANG = 8
VIEWS_ALL = 336
NB = 64
Z = 2048
BLOCKS = 4096
CAP = 2
N_SLAB = 64
N_VIEW = 4


def touch_ends(drawn, own_key, least, high):
    longest = drawn.shape.index(max(drawn.shape))
    spots = []
    for shift in (0, 1):
        where = [jax.random.randint(jax.random.fold_in(own_key, axis), (), 0, length) for axis, length in enumerate(drawn.shape)]
        where[longest] = (where[longest] + shift) % drawn.shape[longest]
        spots.append(tuple(where))
    return drawn.at[spots[0]].set(least).at[spots[1]].set(high)


def block_levels(own_key, shape, pieces, least, top_value):
    def one(axis_at, blocks):
        heights = jax.random.uniform(jax.random.fold_in(jax.random.fold_in(own_key, 6), axis_at), (blocks,), jnp.float32, least / len(pieces), top_value / len(pieces))
        return jnp.repeat(jnp.exp(heights), shape[axis_at] // blocks).reshape((-1,) + (1,) * (len(shape) - axis_at - 1))

    factor_of = one(*pieces[0])
    for cut in pieces[1:]:
        factor_of = factor_of * one(*cut)
    return factor_of


def deal_out(rng, own, number, rows, count, top, reach, slope):
    order = jax.random.permutation(rng, count)
    heavy_load, ordinary = portions_of(count, rows * top, reach, slope, True), portions_of(count, rows * top, reach, slope, False)
    places = jnp.arange(count)

    def named(sizes, turn):
        used = int((sizes > 0).sum())
        fixed = max(1, used // 4)
        passed = fixed + (places - fixed + turn * (used - fixed)) % max(1, count - fixed)
        return jnp.zeros((count,), jnp.int32).at[order[jnp.where(places < fixed, places, passed)]].set(jnp.asarray(sizes, jnp.int32))

    sizes = jnp.where(number % 4 == 0, named(heavy_load, number // 4), named(ordinary, number - number // 4 - 1))
    mixed = jax.random.permutation(jax.random.fold_in(own, 3), count)
    donor, taker = mixed[0:count // 2 * 2:2], mixed[1:count // 2 * 2:2]
    slack = jnp.minimum(sizes[donor] - 1, reach - sizes[taker]) // 2
    slack = jnp.where((donor == order[0]) | (taker == order[0]) | (sizes[taker] == 0), 0, jnp.maximum(slack, 0))
    passed = jax.random.randint(jax.random.fold_in(own, 4), (count // 2,), 0, 1 << 20) % (slack + 1)
    sizes = sizes.at[donor].add(-passed).at[taker].add(passed)
    labels = jnp.searchsorted(jnp.cumsum(sizes), jnp.arange(rows * top), side="right").astype(jnp.int32)
    listing = labels.reshape(top, rows).T
    listing = listing[jax.random.permutation(jax.random.fold_in(own, 1), rows)]
    turn = jax.random.randint(jax.random.fold_in(own, 2), (rows, 1), 0, top)
    return jnp.take_along_axis(listing, (jnp.arange(top)[None, :] + turn) % top, axis=1)


def portions_of(count, total, limit, lean, full):
    portions = [(1 << 20) // math.isqrt(standing ** lean) + 1 for standing in range(1, count + 1)]
    largest = limit if full else min(limit, max(-(-total // count), total * portions[0] // sum(portions)))
    least = 1 if total - largest >= count - 1 else 0
    counts, rest = [largest] + [least] * (count - 1), total - largest - least * (count - 1)
    while rest > 0:
        candidates = [i for i in range(1, count) if counts[i] < largest] or [i for i in range(1, count) if counts[i] < limit]
        mass, left = sum([portions[i] for i in candidates]), rest
        for i in candidates:
            extra = min(limit - counts[i], max(1, left * portions[i] // mass), rest)
            counts[i] = counts[i] + extra
            rest = rest - extra
    return np.array(counts)


def setup_inputs(seed: int = 0) -> dict:
    arg_keys = jax.random.split(jax.random.key(seed), 9)
    activity = jnp.clip(jnp.exp(math.log(2.0) - 1.3862944 * jax.random.uniform(arg_keys[0], (Z, LINES, VL), jnp.float32) ** block_levels(arg_keys[0], (Z, LINES, VL), ((0, 64),), -0.2, 0.2)), 0.5, 2.0)
    sensitivity = jnp.clip(jnp.exp(math.log(8.0) - 2.0794415 * jax.random.uniform(arg_keys[1], (Z, LINES, VL), jnp.float32) ** block_levels(arg_keys[1], (Z, LINES, VL), ((0, 64),), -0.2, 0.2)), 1.0, 8.0)
    psf_width = jnp.clip(0.05 + 0.25 * jax.random.uniform(arg_keys[2], (Z,), jnp.float32) ** block_levels(arg_keys[2], (Z,), ((0, 64),), -0.2, 0.2), 0.05, 0.3)
    measured = jnp.clip(jnp.exp(math.log(4.0) - 2.7725887 * jax.random.uniform(arg_keys[3], (N_VIEW, BLOCKS, ZS, BINS), jnp.float32) ** block_levels(arg_keys[3], (N_VIEW, BLOCKS, ZS, BINS), ((0, 4), (1, 64)), -0.2, 0.2)), 0.25, 4.0).astype(jnp.bfloat16)
    block_slab_keys = jax.random.split(jax.random.fold_in(arg_keys[4], 1), N_VIEW * BLOCKS // NB)
    block_slab_turns = jax.random.permutation(jax.random.fold_in(arg_keys[4], 3), N_VIEW * BLOCKS // NB)
    block_slab = jax.vmap(lambda own, number: deal_out(jax.random.fold_in(arg_keys[4], 2), own, number, NB, N_SLAB, 1, CAP, 2))(block_slab_keys, block_slab_turns).reshape((N_VIEW, BLOCKS, 1))
    block_line = touch_ends(jax.random.randint(arg_keys[5], (N_VIEW, BLOCKS), 0, LINES), jax.random.fold_in(arg_keys[5], 1), 0, LINES - 1).astype(jnp.int32)
    block_angle = touch_ends(jax.random.randint(arg_keys[6], (N_VIEW, BLOCKS), 0, ANG), jax.random.fold_in(arg_keys[6], 1), 0, ANG - 1).astype(jnp.int32)
    subset_views = touch_ends(jax.random.randint(arg_keys[7], (N_VIEW, ANG), 0, VIEWS_ALL), jax.random.fold_in(arg_keys[7], 1), 0, VIEWS_ALL - 1).astype(jnp.int32)
    return {"activity": activity, "sensitivity": sensitivity, "psf_width": psf_width, "measured": measured, "block_slab": block_slab, "block_line": block_line, "block_angle": block_angle, "subset_views": subset_views}


BACKGROUND = 0.05

def kernels(angles, bins, length):
    view_angle = math.pi * angles.astype(jnp.float32) / VIEWS_ALL
    step_width = length / bins
    deviation = 0.25 * step_width
    spacing = step_width * (0.75 + 0.25 * jnp.cos(2.0 * view_angle))
    offset = 1.5 * step_width * jnp.sin(view_angle)
    centres = (jnp.arange(bins, dtype=jnp.float32) + 0.5 - bins / 2)[None, :] * spacing[:, None] + offset[:, None]
    voxel_pos = jnp.arange(length, dtype=jnp.float32) + 0.5 - length / 2
    distance = voxel_pos[None, None, :] - centres[:, :, None]
    values = jnp.exp(-distance * distance / (2.0 * deviation * deviation)) / (deviation * math.sqrt(2.0 * math.pi))
    return values.astype(jnp.bfloat16)

def blur_forward(field, weight):
    padded = jnp.pad(field, ((1, 1), (0, 0), (0, 0)))
    wide = weight[:, None, None]
    return (1.0 - 2.0 * wide) * field + wide * (padded[:-2] + padded[2:])

def blur_adjoint(field, weight):
    wide = weight[:, None, None]
    padded = jnp.pad(wide * field, ((1, 1), (0, 0), (0, 0)))
    return (1.0 - 2.0 * wide) * field + padded[:-2] + padded[2:]

def reference(activity, sensitivity, psf_width, measured, block_slab, block_line, block_angle, subset_views):
    blurred = blur_forward(activity, psf_width).astype(jnp.bfloat16)
    planes = blurred.reshape(N_SLAB, ZS, LINES, VL)
    total = jnp.zeros((N_SLAB, ZS, LINES, VL), jnp.float32)
    for group in range(N_VIEW):
        tof_kernel = kernels(subset_views[group], BINS, VL)
        targets = block_slab[group, :, 0]
        line_ids = block_line[group]
        angle_ids = block_angle[group]

        def project(packed):
            slab_ids, line_part, angle_part = packed
            tiles = planes[slab_ids, :, line_part, :]
            chosen = tof_kernel[angle_part]
            return jnp.einsum('bzv,btv->bzt', tiles.astype(jnp.float32), chosen.astype(jnp.float32))
        estimate = lax.map(project, (targets.reshape(-1, 32), line_ids.reshape(-1, 32), angle_ids.reshape(-1, 32)))
        estimate = estimate.reshape(BLOCKS, ZS, BINS)
        ratios = measured[group].astype(jnp.float32) / (estimate + BACKGROUND)
        segment = (targets * ANG + angle_ids) * LINES + line_ids
        sums = jax.ops.segment_sum(ratios, segment, num_segments=N_SLAB * ANG * LINES)
        rounded = sums.astype(jnp.bfloat16).reshape(N_SLAB, ANG, LINES, ZS, BINS)
        total = total + jnp.einsum('salzt,atv->szlv', rounded.astype(jnp.float32), tof_kernel.astype(jnp.float32))
    smoothed = blur_adjoint(total.reshape(Z, LINES, VL), psf_width)
    return activity * smoothed / sensitivity
```

```python
import math

import jax
import jax.numpy as jnp
from jax import lax
from jax.sharding import PartitionSpec as P

VIEWS_ALL = 336


BACKGROUND = 0.05


def with_halo(value, sides, width):
    for axis, dim in sides:
        size, length = (lax.axis_size(axis), value.shape[dim])
        up = [(i, (i + 1) % size) for i in range(size - 1)]
        down = [(j, i) for i, j in up]
        last = lax.slice_in_dim(value, length - width, length, axis=dim)
        leading = lax.slice_in_dim(value, 0, width, axis=dim)
        before = lax.ppermute(last, axis, up)
        after = lax.ppermute(leading, axis, down)
        value = jnp.concatenate([before, value, after], axis=dim)
    return value


def kernels(angles, bins, length):
    view_angle = math.pi * angles.astype(jnp.float32) / VIEWS_ALL
    step_width = length / bins
    deviation = 0.25 * step_width
    spacing = step_width * (0.75 + 0.25 * jnp.cos(2.0 * view_angle))
    offset = 1.5 * step_width * jnp.sin(view_angle)
    centres = (jnp.arange(bins, dtype=jnp.float32) + 0.5 - bins / 2)[None, :] * spacing[
        :, None
    ] + offset[:, None]
    voxel_pos = jnp.arange(length, dtype=jnp.float32) + 0.5 - length / 2
    distance = voxel_pos[None, None, :] - centres[:, :, None]
    values = jnp.exp(-distance * distance / (2.0 * deviation * deviation)) / (
        deviation * math.sqrt(2.0 * math.pi)
    )
    return values.astype(jnp.bfloat16)


def on_device(
    activity, sensitivity, psf_width, measured, block_slab, block_line, block_angle, subset_views
):
    weight = psf_width[:, None, None]
    padded = with_halo(activity, (("slab", 0),), 1)
    blurred = ((1.0 - 2.0 * weight) * activity + weight * (padded[:-2] + padded[2:])).astype(
        jnp.bfloat16
    )
    planes, lines_here, length = activity.shape
    bins = measured.shape[3]
    row = planes * bins
    tof_kernel = kernels(subset_views[0], bins, length)
    angle_count = tof_kernel.shape[0]
    pairs = angle_count * lines_here
    projected = jnp.einsum("zlv,atv->alzt", blurred, tof_kernel, preferred_element_type=jnp.float32)
    projected = projected.reshape(pairs, planes, bins)

    slab_count = lax.axis_size("slab")
    block_total = measured.shape[1]
    capacity = 2 * block_total // slab_count
    slots = slab_count * capacity
    targets = block_slab[0, :, 0]
    onehot = (targets[:, None] == jnp.arange(slab_count, dtype=jnp.int32)[None, :]).astype(
        jnp.int32
    )
    slot_pos = jnp.sum((jnp.cumsum(onehot, axis=0) - onehot) * onehot, axis=1)
    flat_slot = targets * capacity + slot_pos
    place = (jnp.arange(slots, dtype=jnp.int32)[:, None] == flat_slot[None, :]).astype(
        jnp.bfloat16
    )
    pair_id = block_angle[0] * lines_here + block_line[0]
    extra = 128
    tag = jnp.broadcast_to(pair_id.astype(jnp.bfloat16)[:, None], (block_total, extra))
    outgoing = jnp.concatenate([measured[0].reshape(block_total, row), tag], axis=1)
    send = jnp.dot(place, outgoing, preferred_element_type=jnp.float32).astype(jnp.bfloat16)
    recv = lax.all_to_all(
        send.reshape(slab_count, capacity, row + extra), "slab", 0, 0, tiled=True
    ).reshape(slots, row + extra)
    index = recv[:, row].astype(jnp.int32)
    rows = recv[:, :row].reshape(slots, planes, bins)
    estimate = projected[index]
    ratios = (rows.astype(jnp.float32) / (estimate + BACKGROUND)).reshape(slots, row)

    same = index[:, None] == index[None, :]
    earlier = jnp.arange(slots)[None, :] < jnp.arange(slots)[:, None]
    first = ~jnp.any(same & earlier, axis=1)
    merge = (same & first[:, None]).astype(jnp.float32)
    merged = jnp.dot(merge, ratios, precision=lax.Precision.HIGHEST).astype(jnp.bfloat16)

    views = subset_views[0]
    info = jnp.zeros((extra,), jnp.float32)
    info = info.at[0:angle_count].set((views // 16).astype(jnp.float32))
    info = info.at[angle_count : 2 * angle_count].set((views % 16).astype(jnp.float32))
    info = jnp.broadcast_to(info[None, :], (slots, extra))
    info = info.at[:, 2 * angle_count].set(index.astype(jnp.float32)).astype(jnp.bfloat16)
    payload = jnp.concatenate([merged, info], axis=1)
    everything = lax.all_gather(payload, "view", axis=0, tiled=False)
    group_count = everything.shape[0]

    dense = []
    kernel_all = []
    for group in range(group_count):
        got = everything[group]
        tail = got[0, row:].astype(jnp.int32)
        views_k = tail[0:angle_count] * 16 + tail[angle_count : 2 * angle_count]
        kernel_all.append(kernels(views_k, bins, length))
        index_k = got[:, row + 2 * angle_count].astype(jnp.int32)
        scatter = (jnp.arange(pairs, dtype=jnp.int32)[:, None] == index_k[None, :]).astype(
            jnp.bfloat16
        )
        dense.append(
            jnp.dot(scatter, got[:, :row], preferred_element_type=jnp.float32).astype(jnp.bfloat16)
        )
    dense = jnp.stack(dense).reshape(group_count, angle_count, lines_here, planes, bins)
    kernel_all = jnp.stack(kernel_all)
    total = jnp.einsum(
        "kalzt,katv->zlv", dense, kernel_all, preferred_element_type=jnp.float32
    )
    edges = with_halo(weight * total, (("slab", 0),), 1)
    smoothed = (1.0 - 2.0 * weight) * total + edges[:-2] + edges[2:]
    return activity * smoothed / sensitivity


def solution(mesh):
    in_specs = (
        P("slab", None, None),
        P("slab", None, None),
        P("slab"),
        P("view", "slab", None, None),
        P("view", "slab", None),
        P("view", "slab"),
        P("view", "slab"),
        P("view", None),
    )
    out_specs = P("slab", None, None)
    return jax.shard_map(
        on_device, mesh=mesh, in_specs=in_specs, out_specs=out_specs, check_vma=False
    )
```

```python
import math

import jax
import jax.numpy as jnp
from jax import lax
from jax.experimental import pallas as pl
from jax.experimental.pallas import tpu as pltpu
from jax.sharding import PartitionSpec as P

MESH = pl.DeviceIdType.MESH

VIEWS_ALL = 336


BACKGROUND = 0.05


def with_halo(value, sides, width):
    for axis, dim in sides:
        size, length = (lax.axis_size(axis), value.shape[dim])
        up = [(i, (i + 1) % size) for i in range(size - 1)]
        down = [(j, i) for i, j in up]
        last = lax.slice_in_dim(value, length - width, length, axis=dim)
        leading = lax.slice_in_dim(value, 0, width, axis=dim)
        before = lax.ppermute(last, axis, up)
        after = lax.ppermute(leading, axis, down)
        value = jnp.concatenate([before, value, after], axis=dim)
    return value


def kernels(angles, bins, length):
    view_angle = math.pi * angles.astype(jnp.float32) / VIEWS_ALL
    step_width = length / bins
    deviation = 0.25 * step_width
    spacing = step_width * (0.75 + 0.25 * jnp.cos(2.0 * view_angle))
    offset = 1.5 * step_width * jnp.sin(view_angle)
    centres = (jnp.arange(bins, dtype=jnp.float32) + 0.5 - bins / 2)[None, :] * spacing[
        :, None
    ] + offset[:, None]
    voxel_pos = jnp.arange(length, dtype=jnp.float32) + 0.5 - length / 2
    distance = voxel_pos[None, None, :] - centres[:, :, None]
    values = jnp.exp(-distance * distance / (2.0 * deviation * deviation)) / (
        deviation * math.sqrt(2.0 * math.pi)
    )
    return values.astype(jnp.bfloat16)


def ring_gather_kernel(payload, out, send_sems, recv_sems):
    count = lax.axis_size("view")
    me = lax.axis_index("view")
    slab = lax.axis_index("slab")
    left = lax.rem(me + count - 1, count)
    right = lax.rem(me + 1, count)
    half = payload.shape[0] // 2

    barrier = pltpu.get_barrier_semaphore()
    for neighbour in (left, right):
        pl.semaphore_signal(barrier, inc=1, device_id=(slab, neighbour), device_id_type=MESH)
    pl.semaphore_wait(barrier, 2)

    to_left = pltpu.make_async_remote_copy(
        src_ref=payload, dst_ref=out.at[1], send_sem=send_sems.at[0], recv_sem=recv_sems.at[1],
        device_id=(slab, left), device_id_type=MESH,
    )
    to_right = pltpu.make_async_remote_copy(
        src_ref=payload, dst_ref=out.at[0], send_sem=send_sems.at[1], recv_sem=recv_sems.at[0],
        device_id=(slab, right), device_id_type=MESH,
    )
    to_left.start()
    to_right.start()
    to_right.wait_recv()
    onward_right = pltpu.make_async_remote_copy(
        src_ref=out.at[0, pl.ds(0, half)], dst_ref=out.at[2, pl.ds(0, half)],
        send_sem=send_sems.at[2], recv_sem=recv_sems.at[2],
        device_id=(slab, right), device_id_type=MESH,
    )
    onward_right.start()
    to_left.wait_recv()
    onward_left = pltpu.make_async_remote_copy(
        src_ref=out.at[1, pl.ds(half, half)], dst_ref=out.at[2, pl.ds(half, half)],
        send_sem=send_sems.at[3], recv_sem=recv_sems.at[3],
        device_id=(slab, left), device_id_type=MESH,
    )
    onward_left.start()
    to_left.wait_send()
    to_right.wait_send()
    onward_right.wait_send()
    onward_left.wait_send()
    onward_right.wait_recv()
    onward_left.wait_recv()


def ring_gather(payload):
    return pl.pallas_call(
        ring_gather_kernel,
        out_shape=jax.ShapeDtypeStruct((3,) + payload.shape, payload.dtype),
        in_specs=[pl.BlockSpec(memory_space=pl.ANY)],
        out_specs=pl.BlockSpec(memory_space=pl.ANY),
        scratch_shapes=[pltpu.SemaphoreType.DMA((4,)), pltpu.SemaphoreType.DMA((4,))],
        compiler_params=pltpu.CompilerParams(collective_id=0, has_side_effects=True),
    )(payload)


def on_device(
    activity, sensitivity, psf_width, measured, block_slab, block_line, block_angle, subset_views
):
    weight = psf_width[:, None, None]
    padded = with_halo(activity, (("slab", 0),), 1)
    blurred = ((1.0 - 2.0 * weight) * activity + weight * (padded[:-2] + padded[2:])).astype(
        jnp.bfloat16
    )
    planes, lines_here, length = activity.shape
    bins = measured.shape[3]
    row = planes * bins
    tof_kernel = kernels(subset_views[0], bins, length)
    angle_count = tof_kernel.shape[0]
    pairs = angle_count * lines_here
    projected = jnp.einsum("zlv,atv->alzt", blurred, tof_kernel, preferred_element_type=jnp.float32)
    projected = projected.reshape(pairs, planes, bins)

    slab_count = lax.axis_size("slab")
    block_total = measured.shape[1]
    capacity = 2 * block_total // slab_count
    slots = slab_count * capacity
    targets = block_slab[0, :, 0]
    onehot = (targets[:, None] == jnp.arange(slab_count, dtype=jnp.int32)[None, :]).astype(
        jnp.int32
    )
    slot_pos = jnp.sum((jnp.cumsum(onehot, axis=0) - onehot) * onehot, axis=1)
    flat_slot = targets * capacity + slot_pos
    place = (jnp.arange(slots, dtype=jnp.int32)[:, None] == flat_slot[None, :]).astype(
        jnp.bfloat16
    )
    pair_id = block_angle[0] * lines_here + block_line[0]
    extra = 128
    tag = jnp.broadcast_to(pair_id.astype(jnp.bfloat16)[:, None], (block_total, extra))
    outgoing = jnp.concatenate([measured[0].reshape(block_total, row), tag], axis=1)
    send = jnp.dot(place, outgoing, preferred_element_type=jnp.float32).astype(jnp.bfloat16)
    recv = lax.all_to_all(
        send.reshape(slab_count, capacity, row + extra), "slab", 0, 0, tiled=True
    ).reshape(slots, row + extra)
    index = recv[:, row].astype(jnp.int32)
    rows = recv[:, :row].reshape(slots, planes, bins)
    estimate = projected[index]
    ratios = (rows.astype(jnp.float32) / (estimate + BACKGROUND)).reshape(slots, row)

    same = index[:, None] == index[None, :]
    earlier = jnp.arange(slots)[None, :] < jnp.arange(slots)[:, None]
    first = ~jnp.any(same & earlier, axis=1)
    merge = (same & first[:, None]).astype(jnp.float32)
    merged = jnp.dot(merge, ratios, precision=lax.Precision.HIGHEST).astype(jnp.bfloat16)

    views = subset_views[0]
    info = jnp.zeros((extra,), jnp.float32)
    info = info.at[0:angle_count].set((views // 16).astype(jnp.float32))
    info = info.at[angle_count : 2 * angle_count].set((views % 16).astype(jnp.float32))
    info = jnp.broadcast_to(info[None, :], (slots, extra))
    info = info.at[:, 2 * angle_count].set(index.astype(jnp.float32)).astype(jnp.bfloat16)
    payload = jnp.concatenate([merged, info], axis=1)
    everything = jnp.concatenate([payload[None], ring_gather(payload)], axis=0)
    group_count = everything.shape[0]

    dense = []
    kernel_all = []
    for group in range(group_count):
        got = everything[group]
        tail = got[0, row:].astype(jnp.int32)
        views_k = tail[0:angle_count] * 16 + tail[angle_count : 2 * angle_count]
        kernel_all.append(kernels(views_k, bins, length))
        index_k = got[:, row + 2 * angle_count].astype(jnp.int32)
        scatter = (jnp.arange(pairs, dtype=jnp.int32)[:, None] == index_k[None, :]).astype(
            jnp.bfloat16
        )
        dense.append(
            jnp.dot(scatter, got[:, :row], preferred_element_type=jnp.float32).astype(jnp.bfloat16)
        )
    dense = jnp.stack(dense).reshape(group_count, angle_count, lines_here, planes, bins)
    kernel_all = jnp.stack(kernel_all)
    total = jnp.einsum(
        "kalzt,katv->zlv", dense, kernel_all, preferred_element_type=jnp.float32
    )
    edges = with_halo(weight * total, (("slab", 0),), 1)
    smoothed = (1.0 - 2.0 * weight) * total + edges[:-2] + edges[2:]
    return activity * smoothed / sensitivity


def solution(mesh):
    in_specs = (
        P("slab", None, None),
        P("slab", None, None),
        P("slab"),
        P("view", "slab", None, None),
        P("view", "slab", None),
        P("view", "slab"),
        P("view", "slab"),
        P("view", None),
    )
    out_specs = P("slab", None, None)
    return jax.shard_map(
        on_device, mesh=mesh, in_specs=in_specs, out_specs=out_specs, check_vma=False
    )
```

```python
import math

import jax
import jax.numpy as jnp
from jax import lax
from jax.experimental import pallas as pl
from jax.experimental.pallas import tpu as pltpu
from jax.sharding import PartitionSpec as P

MESH = pl.DeviceIdType.MESH

VIEWS_ALL = 336


BACKGROUND = 0.05


def with_halo(value, sides, width):
    for axis, dim in sides:
        size, length = (lax.axis_size(axis), value.shape[dim])
        up = [(i, (i + 1) % size) for i in range(size - 1)]
        down = [(j, i) for i, j in up]
        last = lax.slice_in_dim(value, length - width, length, axis=dim)
        leading = lax.slice_in_dim(value, 0, width, axis=dim)
        before = lax.ppermute(last, axis, up)
        after = lax.ppermute(leading, axis, down)
        value = jnp.concatenate([before, value, after], axis=dim)
    return value


def kernels(angles, bins, length):
    view_angle = math.pi * angles.astype(jnp.float32) / VIEWS_ALL
    step_width = length / bins
    deviation = 0.25 * step_width
    spacing = step_width * (0.75 + 0.25 * jnp.cos(2.0 * view_angle))
    offset = 1.5 * step_width * jnp.sin(view_angle)
    centres = (jnp.arange(bins, dtype=jnp.float32) + 0.5 - bins / 2)[None, :] * spacing[
        :, None
    ] + offset[:, None]
    voxel_pos = jnp.arange(length, dtype=jnp.float32) + 0.5 - length / 2
    distance = voxel_pos[None, None, :] - centres[:, :, None]
    values = jnp.exp(-distance * distance / (2.0 * deviation * deviation)) / (
        deviation * math.sqrt(2.0 * math.pi)
    )
    return values.astype(jnp.bfloat16)


def ring_gather_kernel(payload, out, send_sems, recv_sems):
    count = lax.axis_size("view")
    me = lax.axis_index("view")
    slab = lax.axis_index("slab")
    left = lax.rem(me + count - 1, count)
    right = lax.rem(me + 1, count)
    half = payload.shape[0] // 2
    rest = payload.shape[0] - half

    barrier = pltpu.get_barrier_semaphore()
    for neighbour in (left, right):
        pl.semaphore_signal(barrier, inc=1, device_id=(slab, neighbour), device_id_type=MESH)
    pl.semaphore_wait(barrier, 2)

    to_left = pltpu.make_async_remote_copy(
        src_ref=payload, dst_ref=out.at[1], send_sem=send_sems.at[0], recv_sem=recv_sems.at[1],
        device_id=(slab, left), device_id_type=MESH,
    )
    to_right = pltpu.make_async_remote_copy(
        src_ref=payload, dst_ref=out.at[0], send_sem=send_sems.at[1], recv_sem=recv_sems.at[0],
        device_id=(slab, right), device_id_type=MESH,
    )
    to_left.start()
    to_right.start()
    to_right.wait_recv()
    onward_right = pltpu.make_async_remote_copy(
        src_ref=out.at[0, pl.ds(0, half)], dst_ref=out.at[2, pl.ds(0, half)],
        send_sem=send_sems.at[2], recv_sem=recv_sems.at[2],
        device_id=(slab, right), device_id_type=MESH,
    )
    onward_right.start()
    to_left.wait_recv()
    onward_left = pltpu.make_async_remote_copy(
        src_ref=out.at[1, pl.ds(half, rest)], dst_ref=out.at[2, pl.ds(half, rest)],
        send_sem=send_sems.at[3], recv_sem=recv_sems.at[3],
        device_id=(slab, left), device_id_type=MESH,
    )
    onward_left.start()
    to_left.wait_send()
    to_right.wait_send()
    onward_right.wait_send()
    onward_left.wait_send()
    onward_right.wait_recv()
    onward_left.wait_recv()


def ring_gather(payload):
    return pl.pallas_call(
        ring_gather_kernel,
        out_shape=jax.ShapeDtypeStruct((3,) + payload.shape, payload.dtype),
        in_specs=[pl.BlockSpec(memory_space=pl.ANY)],
        out_specs=pl.BlockSpec(memory_space=pl.ANY),
        scratch_shapes=[pltpu.SemaphoreType.DMA((4,)), pltpu.SemaphoreType.DMA((4,))],
        compiler_params=pltpu.CompilerParams(collective_id=0, has_side_effects=True),
    )(payload)


def on_device(
    activity, sensitivity, psf_width, measured, block_slab, block_line, block_angle, subset_views
):
    weight = psf_width[:, None, None]
    padded = with_halo(activity, (("slab", 0),), 1)
    blurred = ((1.0 - 2.0 * weight) * activity + weight * (padded[:-2] + padded[2:])).astype(
        jnp.bfloat16
    )
    planes, lines_here, length = activity.shape
    bins = measured.shape[3]
    row = planes * bins
    tof_kernel = kernels(subset_views[0], bins, length)
    angle_count = tof_kernel.shape[0]
    pairs = angle_count * lines_here
    projected = jnp.einsum("zlv,atv->zlat", blurred, tof_kernel, preferred_element_type=jnp.float32)
    projected = projected.reshape(planes, pairs, bins)

    slab_count = lax.axis_size("slab")
    block_total = measured.shape[1]
    capacity = 2 * block_total // slab_count
    slots = slab_count * capacity
    targets = block_slab[0, :, 0]
    onehot = (targets[:, None] == jnp.arange(slab_count, dtype=jnp.int32)[None, :]).astype(
        jnp.int32
    )
    slot_pos = jnp.sum((jnp.cumsum(onehot, axis=0) - onehot) * onehot, axis=1)
    flat_slot = targets * capacity + slot_pos
    place = (jnp.arange(slots, dtype=jnp.int32)[:, None] == flat_slot[None, :]).astype(
        jnp.bfloat16
    )
    pair_id = block_line[0] * angle_count + block_angle[0]
    extra = 128
    tag = jnp.broadcast_to(pair_id.astype(jnp.bfloat16)[:, None], (block_total, extra))
    outgoing = jnp.concatenate([measured[0].reshape(block_total, row), tag], axis=1)
    send = jnp.dot(place, outgoing, preferred_element_type=jnp.float32).astype(jnp.bfloat16)
    recv = lax.all_to_all(
        send.reshape(slab_count, capacity, row + extra), "slab", 0, 0, tiled=True
    ).reshape(slots, row + extra)
    index = recv[:, row].astype(jnp.int32)
    rows = recv[:, :row].reshape(slots, planes, bins).transpose(1, 0, 2)
    estimate = projected[:, index, :]
    ratios = rows.astype(jnp.float32) / (estimate + BACKGROUND)

    same = index[:, None] == index[None, :]
    earlier = jnp.arange(slots)[None, :] < jnp.arange(slots)[:, None]
    first = ~jnp.any(same & earlier, axis=1)
    merge = jnp.broadcast_to((same & first[:, None]).astype(jnp.float32)[None], (planes, slots, slots))
    merged = jnp.einsum(
        "zij,zjt->zit", merge, ratios, precision=lax.Precision.HIGHEST
    ).astype(jnp.bfloat16)

    views = subset_views[0]
    info = jnp.zeros((slots, bins), jnp.float32)
    info = info.at[:, 0].set(index.astype(jnp.float32))
    info = info.at[:, 1 : 1 + angle_count].set((views // 16).astype(jnp.float32)[None, :])
    info = info.at[:, 1 + angle_count : 1 + 2 * angle_count].set(
        (views % 16).astype(jnp.float32)[None, :]
    )
    payload = jnp.concatenate([merged, info.astype(jnp.bfloat16)[None]], axis=0)
    everything = jnp.concatenate([payload[None], ring_gather(payload)], axis=0)
    group_count = everything.shape[0]

    total = None
    for group in range(group_count):
        got = everything[group]
        tail = got[planes, 0].astype(jnp.int32)
        views_k = tail[1 : 1 + angle_count] * 16 + tail[1 + angle_count : 1 + 2 * angle_count]
        kernel_k = kernels(views_k, bins, length)
        index_k = got[planes, :, 0].astype(jnp.int32)
        scatter = (jnp.arange(pairs, dtype=jnp.int32)[:, None] == index_k[None, :]).astype(
            jnp.bfloat16
        )
        scatter = jnp.broadcast_to(scatter[None], (planes, pairs, slots))
        dense = jnp.einsum(
            "zpi,zit->zpt", scatter, got[:planes], preferred_element_type=jnp.float32
        ).astype(jnp.bfloat16)
        dense = dense.reshape(planes, lines_here, angle_count, bins)
        part = jnp.einsum("zlat,atv->zlv", dense, kernel_k, preferred_element_type=jnp.float32)
        total = part if total is None else total + part
    edges = with_halo(weight * total, (("slab", 0),), 1)
    smoothed = (1.0 - 2.0 * weight) * total + edges[:-2] + edges[2:]
    return activity * smoothed / sensitivity


def solution(mesh):
    in_specs = (
        P("slab", None, None),
        P("slab", None, None),
        P("slab"),
        P("view", "slab", None, None),
        P("view", "slab", None),
        P("view", "slab"),
        P("view", "slab"),
        P("view", None),
    )
    out_specs = P("slab", None, None)
    return jax.shard_map(
        on_device, mesh=mesh, in_specs=in_specs, out_specs=out_specs, check_vma=False
    )
```

```python
import math

import jax
import jax.numpy as jnp
from jax import lax
from jax.experimental import pallas as pl
from jax.experimental.pallas import tpu as pltpu
from jax.sharding import PartitionSpec as P

MESH = pl.DeviceIdType.MESH

VIEWS_ALL = 336


BACKGROUND = 0.05


def with_halo(value, sides, width):
    for axis, dim in sides:
        size, length = (lax.axis_size(axis), value.shape[dim])
        up = [(i, (i + 1) % size) for i in range(size - 1)]
        down = [(j, i) for i, j in up]
        last = lax.slice_in_dim(value, length - width, length, axis=dim)
        leading = lax.slice_in_dim(value, 0, width, axis=dim)
        before = lax.ppermute(last, axis, up)
        after = lax.ppermute(leading, axis, down)
        value = jnp.concatenate([before, value, after], axis=dim)
    return value


def kernels(angles, bins, length):
    view_angle = math.pi * angles.astype(jnp.float32) / VIEWS_ALL
    step_width = length / bins
    deviation = 0.25 * step_width
    spacing = step_width * (0.75 + 0.25 * jnp.cos(2.0 * view_angle))
    offset = 1.5 * step_width * jnp.sin(view_angle)
    centres = (jnp.arange(bins, dtype=jnp.float32) + 0.5 - bins / 2)[None, :] * spacing[
        :, None
    ] + offset[:, None]
    voxel_pos = jnp.arange(length, dtype=jnp.float32) + 0.5 - length / 2
    distance = voxel_pos[None, None, :] - centres[:, :, None]
    values = jnp.exp(-distance * distance / (2.0 * deviation * deviation)) / (
        deviation * math.sqrt(2.0 * math.pi)
    )
    return values.astype(jnp.bfloat16)


def ring_gather_kernel(payload, out, send_sems, recv_sems):
    count = lax.axis_size("view")
    me = lax.axis_index("view")
    slab = lax.axis_index("slab")
    left = lax.rem(me + count - 1, count)
    right = lax.rem(me + 1, count)
    half = payload.shape[0] // 2
    rest = payload.shape[0] - half

    barrier = pltpu.get_barrier_semaphore()
    for neighbour in (left, right):
        pl.semaphore_signal(barrier, inc=1, device_id=(slab, neighbour), device_id_type=MESH)
    pl.semaphore_wait(barrier, 2)

    to_left = pltpu.make_async_remote_copy(
        src_ref=payload, dst_ref=out.at[1], send_sem=send_sems.at[0], recv_sem=recv_sems.at[1],
        device_id=(slab, left), device_id_type=MESH,
    )
    to_right = pltpu.make_async_remote_copy(
        src_ref=payload, dst_ref=out.at[0], send_sem=send_sems.at[1], recv_sem=recv_sems.at[0],
        device_id=(slab, right), device_id_type=MESH,
    )
    to_left.start()
    to_right.start()
    to_right.wait_recv()
    onward_right = pltpu.make_async_remote_copy(
        src_ref=out.at[0, pl.ds(0, half)], dst_ref=out.at[2, pl.ds(0, half)],
        send_sem=send_sems.at[2], recv_sem=recv_sems.at[2],
        device_id=(slab, right), device_id_type=MESH,
    )
    onward_right.start()
    to_left.wait_recv()
    onward_left = pltpu.make_async_remote_copy(
        src_ref=out.at[1, pl.ds(half, rest)], dst_ref=out.at[2, pl.ds(half, rest)],
        send_sem=send_sems.at[3], recv_sem=recv_sems.at[3],
        device_id=(slab, left), device_id_type=MESH,
    )
    onward_left.start()
    to_left.wait_send()
    to_right.wait_send()
    onward_right.wait_send()
    onward_left.wait_send()
    onward_right.wait_recv()
    onward_left.wait_recv()


def ring_gather(payload):
    return pl.pallas_call(
        ring_gather_kernel,
        out_shape=jax.ShapeDtypeStruct((3,) + payload.shape, payload.dtype),
        in_specs=[pl.BlockSpec(memory_space=pl.ANY)],
        out_specs=pl.BlockSpec(memory_space=pl.ANY),
        scratch_shapes=[pltpu.SemaphoreType.DMA((4,)), pltpu.SemaphoreType.DMA((4,))],
        compiler_params=pltpu.CompilerParams(collective_id=0, has_side_effects=True),
    )(payload)


def on_device(
    activity, sensitivity, psf_width, measured, block_slab, block_line, block_angle, subset_views
):
    weight = psf_width[:, None, None]
    padded = with_halo(activity, (("slab", 0),), 1)
    blurred = ((1.0 - 2.0 * weight) * activity + weight * (padded[:-2] + padded[2:])).astype(
        jnp.bfloat16
    )
    planes, lines_here, length = activity.shape
    bins = measured.shape[3]
    row = planes * bins
    tof_kernel = kernels(subset_views[0], bins, length)
    angle_count = tof_kernel.shape[0]
    pairs = angle_count * lines_here
    projected = jnp.einsum("zlv,atv->zalt", blurred, tof_kernel, preferred_element_type=jnp.float32)
    projected = projected.reshape(planes, pairs, bins)

    slab_count = lax.axis_size("slab")
    block_total = measured.shape[1]
    capacity = 2 * block_total // slab_count
    slots = slab_count * capacity
    targets = block_slab[0, :, 0]
    onehot = (targets[:, None] == jnp.arange(slab_count, dtype=jnp.int32)[None, :]).astype(
        jnp.int32
    )
    slot_pos = jnp.sum((jnp.cumsum(onehot, axis=0) - onehot) * onehot, axis=1)
    flat_slot = targets * capacity + slot_pos
    place = (jnp.arange(slots, dtype=jnp.int32)[:, None] == flat_slot[None, :]).astype(
        jnp.bfloat16
    )
    pair_id = block_angle[0] * lines_here + block_line[0]
    extra = 128
    tag = jnp.broadcast_to(pair_id.astype(jnp.bfloat16)[:, None], (block_total, extra))
    outgoing = jnp.concatenate([measured[0].reshape(block_total, row), tag], axis=1)
    send = jnp.dot(place, outgoing, preferred_element_type=jnp.float32).astype(jnp.bfloat16)
    recv = lax.all_to_all(
        send.reshape(slab_count, capacity, row + extra), "slab", 0, 0, tiled=True
    ).reshape(slots, row + extra)
    index = recv[:, row].astype(jnp.int32)
    rows = recv[:, :row].reshape(slots, planes, bins).transpose(1, 0, 2)
    pick = (index[:, None] == jnp.arange(pairs, dtype=jnp.int32)[None, :]).astype(jnp.float32)
    pick = jnp.broadcast_to(pick[None], (planes, slots, pairs))
    estimate = jnp.einsum("zjp,zpt->zjt", pick, projected, precision=lax.Precision.HIGH)
    ratios = rows.astype(jnp.float32) / (estimate + BACKGROUND)

    same = index[:, None] == index[None, :]
    earlier = jnp.arange(slots)[None, :] < jnp.arange(slots)[:, None]
    first = ~jnp.any(same & earlier, axis=1)
    merge = jnp.broadcast_to((same & first[:, None]).astype(jnp.float32)[None], (planes, slots, slots))
    merged = jnp.einsum(
        "zij,zjt->zit", merge, ratios, precision=lax.Precision.HIGH
    ).astype(jnp.bfloat16)

    views = subset_views[0]
    info = jnp.zeros((slots, bins), jnp.float32)
    info = info.at[:, 0].set(index.astype(jnp.float32))
    info = info.at[:, 1 : 1 + angle_count].set((views // 16).astype(jnp.float32)[None, :])
    info = info.at[:, 1 + angle_count : 1 + 2 * angle_count].set(
        (views % 16).astype(jnp.float32)[None, :]
    )
    payload = jnp.concatenate([merged, info.astype(jnp.bfloat16)[None]], axis=0)
    everything = jnp.concatenate([payload[None], ring_gather(payload)], axis=0)
    group_count = everything.shape[0]

    total = None
    for group in range(group_count):
        got = everything[group]
        tail = got[planes, 0].astype(jnp.int32)
        views_k = tail[1 : 1 + angle_count] * 16 + tail[1 + angle_count : 1 + 2 * angle_count]
        kernel_k = kernels(views_k, bins, length)
        index_k = got[planes, :, 0].astype(jnp.int32)
        order = jnp.arange(pairs, dtype=jnp.int32)
        wanted = (order % angle_count) * lines_here + order // angle_count
        scatter = (wanted[:, None] == index_k[None, :]).astype(jnp.bfloat16)
        scatter = jnp.broadcast_to(scatter[None], (planes, pairs, slots))
        dense = jnp.einsum(
            "zpi,zit->zpt", scatter, got[:planes], preferred_element_type=jnp.float32
        ).astype(jnp.bfloat16)
        dense = dense.reshape(planes, lines_here, angle_count, bins)
        parts = [
            jnp.einsum("zlat,atv->zlv", piece, kernel_k, preferred_element_type=jnp.float32)
            for piece in (dense[:1], dense[planes - 1 :], dense[1 : planes - 1])
        ]
        total = parts if total is None else [t + p for t, p in zip(total, parts)]
    low, high, middle = total
    size = lax.axis_size("slab")
    up = [(i, (i + 1) % size) for i in range(size - 1)]
    down = [(j, i) for i, j in up]
    from_below = lax.ppermute(weight[planes - 1 :] * high, "slab", up)
    from_above = lax.ppermute(weight[:1] * low, "slab", down)
    total = jnp.concatenate([low, middle, high], axis=0)
    weighted = weight * total
    below = jnp.concatenate([from_below, weighted[: planes - 1]], axis=0)
    above = jnp.concatenate([weighted[1:], from_above], axis=0)
    smoothed = (1.0 - 2.0 * weight) * total + below + above
    return activity * smoothed / sensitivity


def solution(mesh):
    in_specs = (
        P("slab", None, None),
        P("slab", None, None),
        P("slab"),
        P("view", "slab", None, None),
        P("view", "slab", None),
        P("view", "slab"),
        P("view", "slab"),
        P("view", None),
    )
    out_specs = P("slab", None, None)
    return jax.shard_map(
        on_device, mesh=mesh, in_specs=in_specs, out_specs=out_specs, check_vma=False
    )
```

```python
import math

import jax
import jax.numpy as jnp
from jax import lax
from jax.experimental import pallas as pl
from jax.experimental.pallas import tpu as pltpu
from jax.sharding import PartitionSpec as P

MESH = pl.DeviceIdType.MESH

VIEWS_ALL = 336


BACKGROUND = 0.05


def with_halo(value, sides, width):
    for axis, dim in sides:
        size, length = (lax.axis_size(axis), value.shape[dim])
        up = [(i, (i + 1) % size) for i in range(size - 1)]
        down = [(j, i) for i, j in up]
        last = lax.slice_in_dim(value, length - width, length, axis=dim)
        leading = lax.slice_in_dim(value, 0, width, axis=dim)
        before = lax.ppermute(last, axis, up)
        after = lax.ppermute(leading, axis, down)
        value = jnp.concatenate([before, value, after], axis=dim)
    return value


def kernels(angles, bins, length):
    view_angle = math.pi * angles.astype(jnp.float32) / VIEWS_ALL
    step_width = length / bins
    deviation = 0.25 * step_width
    spacing = step_width * (0.75 + 0.25 * jnp.cos(2.0 * view_angle))
    offset = 1.5 * step_width * jnp.sin(view_angle)
    centres = (jnp.arange(bins, dtype=jnp.float32) + 0.5 - bins / 2)[None, :] * spacing[
        :, None
    ] + offset[:, None]
    voxel_pos = jnp.arange(length, dtype=jnp.float32) + 0.5 - length / 2
    distance = voxel_pos[None, None, :] - centres[:, :, None]
    values = jnp.exp(-distance * distance / (2.0 * deviation * deviation)) / (
        deviation * math.sqrt(2.0 * math.pi)
    )
    return values.astype(jnp.bfloat16)


def ring_gather_kernel(payload, out, send_sems, recv_sems):
    count = lax.axis_size("view")
    me = lax.axis_index("view")
    slab = lax.axis_index("slab")
    left = lax.rem(me + count - 1, count)
    right = lax.rem(me + 1, count)
    half = payload.shape[0] // 2
    rest = payload.shape[0] - half

    barrier = pltpu.get_barrier_semaphore()
    for neighbour in (left, right):
        pl.semaphore_signal(barrier, inc=1, device_id=(slab, neighbour), device_id_type=MESH)
    pl.semaphore_wait(barrier, 2)

    to_left = pltpu.make_async_remote_copy(
        src_ref=payload, dst_ref=out.at[1], send_sem=send_sems.at[0], recv_sem=recv_sems.at[1],
        device_id=(slab, left), device_id_type=MESH,
    )
    to_right = pltpu.make_async_remote_copy(
        src_ref=payload, dst_ref=out.at[0], send_sem=send_sems.at[1], recv_sem=recv_sems.at[0],
        device_id=(slab, right), device_id_type=MESH,
    )
    to_left.start()
    to_right.start()
    to_right.wait_recv()
    onward_right = pltpu.make_async_remote_copy(
        src_ref=out.at[0, pl.ds(0, half)], dst_ref=out.at[2, pl.ds(0, half)],
        send_sem=send_sems.at[2], recv_sem=recv_sems.at[2],
        device_id=(slab, right), device_id_type=MESH,
    )
    onward_right.start()
    to_left.wait_recv()
    onward_left = pltpu.make_async_remote_copy(
        src_ref=out.at[1, pl.ds(half, rest)], dst_ref=out.at[2, pl.ds(half, rest)],
        send_sem=send_sems.at[3], recv_sem=recv_sems.at[3],
        device_id=(slab, left), device_id_type=MESH,
    )
    onward_left.start()
    to_left.wait_send()
    to_right.wait_send()
    onward_right.wait_send()
    onward_left.wait_send()
    onward_right.wait_recv()
    onward_left.wait_recv()


def ring_gather(payload):
    return pl.pallas_call(
        ring_gather_kernel,
        out_shape=jax.ShapeDtypeStruct((3,) + payload.shape, payload.dtype),
        in_specs=[pl.BlockSpec(memory_space=pl.ANY)],
        out_specs=pl.BlockSpec(memory_space=pl.ANY),
        scratch_shapes=[pltpu.SemaphoreType.DMA((4,)), pltpu.SemaphoreType.DMA((4,))],
        compiler_params=pltpu.CompilerParams(collective_id=0, has_side_effects=True),
    )(payload)


def exchange_kernel(send, out, local_sem, send_sems, recv_sems):
    count = lax.axis_size("slab")
    me = lax.axis_index("slab")
    view = lax.axis_index("view")

    barrier = pltpu.get_barrier_semaphore()

    def greet(step, carry):
        peer = lax.rem(me + step, count)
        pl.semaphore_signal(barrier, inc=1, device_id=(peer, view), device_id_type=MESH)
        return carry

    lax.fori_loop(1, count, greet, 0)
    pl.semaphore_wait(barrier, count - 1)

    local = pltpu.make_async_copy(send.at[me], out.at[me], local_sem)
    local.start()

    def copy_to(step):
        peer = lax.rem(me + step, count)
        return pltpu.make_async_remote_copy(
            src_ref=send.at[peer], dst_ref=out.at[me],
            send_sem=send_sems.at[step], recv_sem=recv_sems.at[step],
            device_id=(peer, view), device_id_type=MESH,
        )

    def start(step, carry):
        copy_to(step).start()
        return carry

    def finish(step, carry):
        copy = copy_to(step)
        copy.wait_send()
        copy.wait_recv()
        return carry

    lax.fori_loop(1, count, start, 0)
    lax.fori_loop(1, count, finish, 0)
    local.wait()


def exchange(send):
    count = send.shape[0]
    return pl.pallas_call(
        exchange_kernel,
        out_shape=jax.ShapeDtypeStruct(send.shape, send.dtype),
        in_specs=[pl.BlockSpec(memory_space=pl.ANY)],
        out_specs=pl.BlockSpec(memory_space=pl.ANY),
        scratch_shapes=[
            pltpu.SemaphoreType.DMA(()),
            pltpu.SemaphoreType.DMA((count,)),
            pltpu.SemaphoreType.DMA((count,)),
        ],
        compiler_params=pltpu.CompilerParams(collective_id=1, has_side_effects=True),
    )(send)


def on_device(
    activity, sensitivity, psf_width, measured, block_slab, block_line, block_angle, subset_views
):
    weight = psf_width[:, None, None]
    padded = with_halo(activity, (("slab", 0),), 1)
    blurred = ((1.0 - 2.0 * weight) * activity + weight * (padded[:-2] + padded[2:])).astype(
        jnp.bfloat16
    )
    planes, lines_here, length = activity.shape
    bins = measured.shape[3]
    row = planes * bins
    tof_kernel = kernels(subset_views[0], bins, length)
    angle_count = tof_kernel.shape[0]
    pairs = angle_count * lines_here
    projected = jnp.einsum("zlv,atv->zalt", blurred, tof_kernel, preferred_element_type=jnp.float32)
    projected = projected.reshape(planes, pairs, bins)

    slab_count = lax.axis_size("slab")
    block_total = measured.shape[1]
    capacity = 2 * block_total // slab_count
    slots = slab_count * capacity
    targets = block_slab[0, :, 0]
    onehot = (targets[:, None] == jnp.arange(slab_count, dtype=jnp.int32)[None, :]).astype(
        jnp.int32
    )
    slot_pos = jnp.sum((jnp.cumsum(onehot, axis=0) - onehot) * onehot, axis=1)
    flat_slot = targets * capacity + slot_pos
    place = (jnp.arange(slots, dtype=jnp.int32)[:, None] == flat_slot[None, :]).astype(
        jnp.bfloat16
    )
    pair_id = block_angle[0] * lines_here + block_line[0]
    extra = 128
    tag = jnp.broadcast_to(pair_id.astype(jnp.bfloat16)[:, None], (block_total, extra))
    outgoing = jnp.concatenate([measured[0].reshape(block_total, row), tag], axis=1)
    send = jnp.dot(place, outgoing, preferred_element_type=jnp.float32).astype(jnp.bfloat16)
    recv = exchange(send.reshape(slab_count, capacity, row + extra)).reshape(slots, row + extra)
    index = recv[:, row].astype(jnp.int32)
    rows = recv[:, :row].reshape(slots, planes, bins).transpose(1, 0, 2)
    pick = (index[:, None] == jnp.arange(pairs, dtype=jnp.int32)[None, :]).astype(jnp.float32)
    pick = jnp.broadcast_to(pick[None], (planes, slots, pairs))
    estimate = jnp.einsum("zjp,zpt->zjt", pick, projected, precision=lax.Precision.HIGH)
    ratios = rows.astype(jnp.float32) / (estimate + BACKGROUND)

    same = index[:, None] == index[None, :]
    earlier = jnp.arange(slots)[None, :] < jnp.arange(slots)[:, None]
    first = ~jnp.any(same & earlier, axis=1)
    merge = jnp.broadcast_to((same & first[:, None]).astype(jnp.float32)[None], (planes, slots, slots))
    merged = jnp.einsum(
        "zij,zjt->zit", merge, ratios, precision=lax.Precision.HIGH
    ).astype(jnp.bfloat16)

    views = subset_views[0]
    info = jnp.zeros((slots, bins), jnp.float32)
    info = info.at[:, 0].set(index.astype(jnp.float32))
    info = info.at[:, 1 : 1 + angle_count].set((views // 16).astype(jnp.float32)[None, :])
    info = info.at[:, 1 + angle_count : 1 + 2 * angle_count].set(
        (views % 16).astype(jnp.float32)[None, :]
    )
    payload = jnp.concatenate([merged, info.astype(jnp.bfloat16)[None]], axis=0)
    everything = jnp.concatenate([payload[None], ring_gather(payload)], axis=0)
    group_count = everything.shape[0]

    total = None
    for group in range(group_count):
        got = everything[group]
        tail = got[planes, 0].astype(jnp.int32)
        views_k = tail[1 : 1 + angle_count] * 16 + tail[1 + angle_count : 1 + 2 * angle_count]
        kernel_k = kernels(views_k, bins, length)
        index_k = got[planes, :, 0].astype(jnp.int32)
        order = jnp.arange(pairs, dtype=jnp.int32)
        wanted = (order % angle_count) * lines_here + order // angle_count
        scatter = (wanted[:, None] == index_k[None, :]).astype(jnp.bfloat16)
        scatter = jnp.broadcast_to(scatter[None], (planes, pairs, slots))
        dense = jnp.einsum(
            "zpi,zit->zpt", scatter, got[:planes], preferred_element_type=jnp.float32
        ).astype(jnp.bfloat16)
        dense = dense.reshape(planes, lines_here, angle_count, bins)
        part = jnp.einsum("zlat,atv->zlv", dense, kernel_k, preferred_element_type=jnp.float32)
        total = part if total is None else total + part
    edges = with_halo(weight * total, (("slab", 0),), 1)
    smoothed = (1.0 - 2.0 * weight) * total + edges[:-2] + edges[2:]
    return activity * smoothed / sensitivity


def solution(mesh):
    in_specs = (
        P("slab", None, None),
        P("slab", None, None),
        P("slab"),
        P("view", "slab", None, None),
        P("view", "slab", None),
        P("view", "slab"),
        P("view", "slab"),
        P("view", None),
    )
    out_specs = P("slab", None, None)
    return jax.shard_map(
        on_device, mesh=mesh, in_specs=in_specs, out_specs=out_specs, check_vma=False
    )
```

```python
import math

import jax
import jax.numpy as jnp
from jax import lax
from jax.experimental import pallas as pl
from jax.experimental.pallas import tpu as pltpu
from jax.sharding import PartitionSpec as P

MESH = pl.DeviceIdType.MESH

VIEWS_ALL = 336


BACKGROUND = 0.05


def with_halo(value, sides, width):
    for axis, dim in sides:
        size, length = (lax.axis_size(axis), value.shape[dim])
        up = [(i, (i + 1) % size) for i in range(size - 1)]
        down = [(j, i) for i, j in up]
        last = lax.slice_in_dim(value, length - width, length, axis=dim)
        leading = lax.slice_in_dim(value, 0, width, axis=dim)
        before = lax.ppermute(last, axis, up)
        after = lax.ppermute(leading, axis, down)
        value = jnp.concatenate([before, value, after], axis=dim)
    return value


def kernels(angles, bins, length):
    view_angle = math.pi * angles.astype(jnp.float32) / VIEWS_ALL
    step_width = length / bins
    deviation = 0.25 * step_width
    spacing = step_width * (0.75 + 0.25 * jnp.cos(2.0 * view_angle))
    offset = 1.5 * step_width * jnp.sin(view_angle)
    centres = (jnp.arange(bins, dtype=jnp.float32) + 0.5 - bins / 2)[None, :] * spacing[
        :, None
    ] + offset[:, None]
    voxel_pos = jnp.arange(length, dtype=jnp.float32) + 0.5 - length / 2
    distance = voxel_pos[None, None, :] - centres[:, :, None]
    values = jnp.exp(-distance * distance / (2.0 * deviation * deviation)) / (
        deviation * math.sqrt(2.0 * math.pi)
    )
    return values.astype(jnp.bfloat16)


def ring_gather_kernel(payload, out, send_sems, recv_sems):
    count = lax.axis_size("view")
    me = lax.axis_index("view")
    slab = lax.axis_index("slab")
    left = lax.rem(me + count - 1, count)
    right = lax.rem(me + 1, count)
    half = payload.shape[0] // 2
    rest = payload.shape[0] - half

    barrier = pltpu.get_barrier_semaphore()
    for neighbour in (left, right):
        pl.semaphore_signal(barrier, inc=1, device_id=(slab, neighbour), device_id_type=MESH)
    pl.semaphore_wait(barrier, 2)

    to_left = pltpu.make_async_remote_copy(
        src_ref=payload, dst_ref=out.at[1], send_sem=send_sems.at[0], recv_sem=recv_sems.at[1],
        device_id=(slab, left), device_id_type=MESH,
    )
    to_right = pltpu.make_async_remote_copy(
        src_ref=payload, dst_ref=out.at[0], send_sem=send_sems.at[1], recv_sem=recv_sems.at[0],
        device_id=(slab, right), device_id_type=MESH,
    )
    to_left.start()
    to_right.start()
    to_right.wait_recv()
    onward_right = pltpu.make_async_remote_copy(
        src_ref=out.at[0, pl.ds(0, half)], dst_ref=out.at[2, pl.ds(0, half)],
        send_sem=send_sems.at[2], recv_sem=recv_sems.at[2],
        device_id=(slab, right), device_id_type=MESH,
    )
    onward_right.start()
    to_left.wait_recv()
    onward_left = pltpu.make_async_remote_copy(
        src_ref=out.at[1, pl.ds(half, rest)], dst_ref=out.at[2, pl.ds(half, rest)],
        send_sem=send_sems.at[3], recv_sem=recv_sems.at[3],
        device_id=(slab, left), device_id_type=MESH,
    )
    onward_left.start()
    to_left.wait_send()
    to_right.wait_send()
    onward_right.wait_send()
    onward_left.wait_send()
    onward_right.wait_recv()
    onward_left.wait_recv()


def ring_gather(payload):
    return pl.pallas_call(
        ring_gather_kernel,
        out_shape=jax.ShapeDtypeStruct((3,) + payload.shape, payload.dtype),
        in_specs=[pl.BlockSpec(memory_space=pl.ANY)],
        out_specs=pl.BlockSpec(memory_space=pl.ANY),
        scratch_shapes=[pltpu.SemaphoreType.DMA((4,)), pltpu.SemaphoreType.DMA((4,))],
        compiler_params=pltpu.CompilerParams(collective_id=0, has_side_effects=True),
    )(payload)


def exchange_kernel(send, out, local_sem, send_sems, recv_sems):
    count = lax.axis_size("slab")
    me = lax.axis_index("slab")
    view = lax.axis_index("view")

    barrier = pltpu.get_barrier_semaphore()

    def greet(step, carry):
        peer = lax.rem(me + step, count)
        pl.semaphore_signal(barrier, inc=1, device_id=(peer, view), device_id_type=MESH)
        return carry

    lax.fori_loop(1, count, greet, 0)
    pl.semaphore_wait(barrier, count - 1)

    local = pltpu.make_async_copy(send.at[me], out.at[me], local_sem)
    local.start()

    def copy_to(step):
        peer = lax.rem(me + step, count)
        return pltpu.make_async_remote_copy(
            src_ref=send.at[peer], dst_ref=out.at[me],
            send_sem=send_sems.at[step], recv_sem=recv_sems.at[step],
            device_id=(peer, view), device_id_type=MESH,
        )

    def start(step, carry):
        copy_to(step).start()
        return carry

    def finish(step, carry):
        copy = copy_to(step)
        copy.wait_send()
        copy.wait_recv()
        return carry

    lax.fori_loop(1, count, start, 0)
    lax.fori_loop(1, count, finish, 0)
    local.wait()


def exchange(send):
    count = send.shape[0]
    return pl.pallas_call(
        exchange_kernel,
        out_shape=jax.ShapeDtypeStruct(send.shape, send.dtype),
        in_specs=[pl.BlockSpec(memory_space=pl.ANY)],
        out_specs=pl.BlockSpec(memory_space=pl.ANY),
        scratch_shapes=[
            pltpu.SemaphoreType.DMA(()),
            pltpu.SemaphoreType.DMA((count,)),
            pltpu.SemaphoreType.DMA((count,)),
        ],
        compiler_params=pltpu.CompilerParams(collective_id=1, has_side_effects=True),
    )(send)


def on_device(
    activity, sensitivity, psf_width, measured, block_slab, block_line, block_angle, subset_views
):
    weight = psf_width[:, None, None]
    padded = with_halo(activity, (("slab", 0),), 1)
    blurred = ((1.0 - 2.0 * weight) * activity + weight * (padded[:-2] + padded[2:])).astype(
        jnp.bfloat16
    )
    planes, lines_here, length = activity.shape
    bins = measured.shape[3]
    row = planes * bins
    tof_kernel = kernels(subset_views[0], bins, length)
    angle_count = tof_kernel.shape[0]
    pairs = angle_count * lines_here
    projected = jnp.einsum("zlv,atv->zalt", blurred, tof_kernel, preferred_element_type=jnp.float32)
    projected = projected.reshape(planes, pairs, bins)

    slab_count = lax.axis_size("slab")
    block_total = measured.shape[1]
    capacity = 2 * block_total // slab_count
    slots = slab_count * capacity
    targets = block_slab[0, :, 0]
    onehot = (targets[:, None] == jnp.arange(slab_count, dtype=jnp.int32)[None, :]).astype(
        jnp.int32
    )
    slot_pos = jnp.sum((jnp.cumsum(onehot, axis=0) - onehot) * onehot, axis=1)
    flat_slot = targets * capacity + slot_pos
    place = (jnp.arange(slots, dtype=jnp.int32)[:, None] == flat_slot[None, :]).astype(
        jnp.bfloat16
    )
    pair_id = block_angle[0] * lines_here + block_line[0]
    extra = 128
    tag = jnp.broadcast_to(pair_id.astype(jnp.bfloat16)[:, None], (block_total, extra))
    outgoing = jnp.concatenate([measured[0].reshape(block_total, row), tag], axis=1)
    send = jnp.dot(place, outgoing, preferred_element_type=jnp.float32).astype(jnp.bfloat16)
    recv = exchange(send.reshape(slab_count, capacity, row + extra)).reshape(slots, row + extra)
    index = recv[:, row].astype(jnp.int32)
    rows = recv[:, :row].reshape(slots, planes, bins).transpose(1, 0, 2)
    pick = (index[:, None] == jnp.arange(pairs, dtype=jnp.int32)[None, :]).astype(jnp.float32)
    pick = jnp.broadcast_to(pick[None], (planes, slots, pairs))
    estimate = jnp.einsum("zjp,zpt->zjt", pick, projected, precision=lax.Precision.HIGH)
    ratios = rows.astype(jnp.float32) / (estimate + BACKGROUND)

    same = index[:, None] == index[None, :]
    earlier = jnp.arange(slots)[None, :] < jnp.arange(slots)[:, None]
    first = ~jnp.any(same & earlier, axis=1)
    merge = jnp.broadcast_to((same & first[:, None]).astype(jnp.float32)[None], (planes, slots, slots))
    merged = jnp.einsum(
        "zij,zjt->zit", merge, ratios, precision=lax.Precision.HIGH
    ).astype(jnp.bfloat16)

    views = subset_views[0]
    info = jnp.zeros((slots, bins), jnp.float32)
    info = info.at[:, 0].set(index.astype(jnp.float32))
    info = info.at[:, 1 : 1 + angle_count].set((views // 16).astype(jnp.float32)[None, :])
    info = info.at[:, 1 + angle_count : 1 + 2 * angle_count].set(
        (views % 16).astype(jnp.float32)[None, :]
    )
    payload = jnp.concatenate([merged, info.astype(jnp.bfloat16)[None]], axis=0)
    def back_project(got, kernel_k):
        index_k = got[planes, :, 0].astype(jnp.int32)
        order = jnp.arange(pairs, dtype=jnp.int32)
        wanted = (order % angle_count) * lines_here + order // angle_count
        scatter = (wanted[:, None] == index_k[None, :]).astype(jnp.bfloat16)
        scatter = jnp.broadcast_to(scatter[None], (planes, pairs, slots))
        dense = jnp.einsum(
            "zpi,zit->zpt", scatter, got[:planes], preferred_element_type=jnp.float32
        ).astype(jnp.bfloat16)
        dense = dense.reshape(planes, lines_here, angle_count, bins)
        return jnp.einsum("zlat,atv->zlv", dense, kernel_k, preferred_element_type=jnp.float32)

    def kernel_of(got):
        tail = got[planes, 0].astype(jnp.int32)
        views_k = tail[1 : 1 + angle_count] * 16 + tail[1 + angle_count : 1 + 2 * angle_count]
        return kernels(views_k, bins, length)

    view_count = lax.axis_size("view")
    rightward = [(i, (i + 1) % view_count) for i in range(view_count)]
    leftward = [(i, (i + view_count - 1) % view_count) for i in range(view_count)]
    half = (planes + 1) // 2
    from_left = lax.ppermute(payload, "view", rightward)
    from_right = lax.ppermute(payload, "view", leftward)
    total = back_project(payload, tof_kernel)
    total, from_left, from_right = lax.optimization_barrier((total, from_left, from_right))
    far_low = lax.ppermute(from_left[:half], "view", rightward)
    far_high = lax.ppermute(from_right[half:], "view", leftward)
    total = total + back_project(from_left, kernel_of(from_left))
    total = total + back_project(from_right, kernel_of(from_right))
    far = jnp.concatenate([far_low, far_high], axis=0)
    total = total + back_project(far, kernel_of(far))
    edges = with_halo(weight * total, (("slab", 0),), 1)
    smoothed = (1.0 - 2.0 * weight) * total + edges[:-2] + edges[2:]
    return activity * smoothed / sensitivity


def solution(mesh):
    in_specs = (
        P("slab", None, None),
        P("slab", None, None),
        P("slab"),
        P("view", "slab", None, None),
        P("view", "slab", None),
        P("view", "slab"),
        P("view", "slab"),
        P("view", None),
    )
    out_specs = P("slab", None, None)
    return jax.shard_map(
        on_device, mesh=mesh, in_specs=in_specs, out_specs=out_specs, check_vma=False
    )
```

```python
import math

import jax
import jax.numpy as jnp
from jax import lax
from jax.experimental import pallas as pl
from jax.experimental.pallas import tpu as pltpu
from jax.sharding import PartitionSpec as P

MESH = pl.DeviceIdType.MESH

VIEWS_ALL = 336


BACKGROUND = 0.05


def with_halo(value, sides, width):
    for axis, dim in sides:
        size, length = (lax.axis_size(axis), value.shape[dim])
        up = [(i, (i + 1) % size) for i in range(size - 1)]
        down = [(j, i) for i, j in up]
        last = lax.slice_in_dim(value, length - width, length, axis=dim)
        leading = lax.slice_in_dim(value, 0, width, axis=dim)
        before = lax.ppermute(last, axis, up)
        after = lax.ppermute(leading, axis, down)
        value = jnp.concatenate([before, value, after], axis=dim)
    return value


def kernels(angles, bins, length):
    view_angle = math.pi * angles.astype(jnp.float32) / VIEWS_ALL
    step_width = length / bins
    deviation = 0.25 * step_width
    spacing = step_width * (0.75 + 0.25 * jnp.cos(2.0 * view_angle))
    offset = 1.5 * step_width * jnp.sin(view_angle)
    centres = (jnp.arange(bins, dtype=jnp.float32) + 0.5 - bins / 2)[None, :] * spacing[
        :, None
    ] + offset[:, None]
    voxel_pos = jnp.arange(length, dtype=jnp.float32) + 0.5 - length / 2
    distance = voxel_pos[None, None, :] - centres[:, :, None]
    values = jnp.exp(-distance * distance / (2.0 * deviation * deviation)) / (
        deviation * math.sqrt(2.0 * math.pi)
    )
    return values.astype(jnp.bfloat16)


def ring_gather_kernel(payload, out, send_sems, recv_sems):
    count = lax.axis_size("view")
    me = lax.axis_index("view")
    slab = lax.axis_index("slab")
    left = lax.rem(me + count - 1, count)
    right = lax.rem(me + 1, count)
    half = payload.shape[0] // 2
    rest = payload.shape[0] - half

    barrier = pltpu.get_barrier_semaphore()
    for neighbour in (left, right):
        pl.semaphore_signal(barrier, inc=1, device_id=(slab, neighbour), device_id_type=MESH)
    pl.semaphore_wait(barrier, 2)

    to_left = pltpu.make_async_remote_copy(
        src_ref=payload, dst_ref=out.at[1], send_sem=send_sems.at[0], recv_sem=recv_sems.at[1],
        device_id=(slab, left), device_id_type=MESH,
    )
    to_right = pltpu.make_async_remote_copy(
        src_ref=payload, dst_ref=out.at[0], send_sem=send_sems.at[1], recv_sem=recv_sems.at[0],
        device_id=(slab, right), device_id_type=MESH,
    )
    to_left.start()
    to_right.start()
    to_right.wait_recv()
    onward_right = pltpu.make_async_remote_copy(
        src_ref=out.at[0, pl.ds(0, half)], dst_ref=out.at[2, pl.ds(0, half)],
        send_sem=send_sems.at[2], recv_sem=recv_sems.at[2],
        device_id=(slab, right), device_id_type=MESH,
    )
    onward_right.start()
    to_left.wait_recv()
    onward_left = pltpu.make_async_remote_copy(
        src_ref=out.at[1, pl.ds(half, rest)], dst_ref=out.at[2, pl.ds(half, rest)],
        send_sem=send_sems.at[3], recv_sem=recv_sems.at[3],
        device_id=(slab, left), device_id_type=MESH,
    )
    onward_left.start()
    to_left.wait_send()
    to_right.wait_send()
    onward_right.wait_send()
    onward_left.wait_send()
    onward_right.wait_recv()
    onward_left.wait_recv()


def ring_gather(payload):
    return pl.pallas_call(
        ring_gather_kernel,
        out_shape=jax.ShapeDtypeStruct((3,) + payload.shape, payload.dtype),
        in_specs=[pl.BlockSpec(memory_space=pl.ANY)],
        out_specs=pl.BlockSpec(memory_space=pl.ANY),
        scratch_shapes=[pltpu.SemaphoreType.DMA((4,)), pltpu.SemaphoreType.DMA((4,))],
        compiler_params=pltpu.CompilerParams(collective_id=0, has_side_effects=True),
    )(payload)


def exchange_kernel(send, out, local_sem, send_sems, recv_sems):
    count = lax.axis_size("slab")
    me = lax.axis_index("slab")
    view = lax.axis_index("view")

    barrier = pltpu.get_barrier_semaphore()

    def greet(step, carry):
        peer = lax.rem(me + step, count)
        pl.semaphore_signal(barrier, inc=1, device_id=(peer, view), device_id_type=MESH)
        return carry

    lax.fori_loop(1, count, greet, 0)
    pl.semaphore_wait(barrier, count - 1)

    local = pltpu.make_async_copy(send.at[me], out.at[me], local_sem)
    local.start()

    def copy_to(step):
        peer = lax.rem(me + step, count)
        return pltpu.make_async_remote_copy(
            src_ref=send.at[peer], dst_ref=out.at[me],
            send_sem=send_sems.at[step], recv_sem=recv_sems.at[step],
            device_id=(peer, view), device_id_type=MESH,
        )

    def start(step, carry):
        copy_to(step).start()
        return carry

    def finish(step, carry):
        copy = copy_to(step)
        copy.wait_send()
        copy.wait_recv()
        return carry

    lax.fori_loop(1, count, start, 0)
    lax.fori_loop(1, count, finish, 0)
    local.wait()


def exchange(send):
    count = send.shape[0]
    return pl.pallas_call(
        exchange_kernel,
        out_shape=jax.ShapeDtypeStruct(send.shape, send.dtype),
        in_specs=[pl.BlockSpec(memory_space=pl.ANY)],
        out_specs=pl.BlockSpec(memory_space=pl.ANY),
        scratch_shapes=[
            pltpu.SemaphoreType.DMA(()),
            pltpu.SemaphoreType.DMA((count,)),
            pltpu.SemaphoreType.DMA((count,)),
        ],
        compiler_params=pltpu.CompilerParams(collective_id=1, has_side_effects=True),
    )(send)


def on_device(
    activity, sensitivity, psf_width, measured, block_slab, block_line, block_angle, subset_views
):
    weight = psf_width[:, None, None]
    view_table = lax.all_gather(subset_views[0], "view")
    padded = with_halo(activity, (("slab", 0),), 1)
    blurred = ((1.0 - 2.0 * weight) * activity + weight * (padded[:-2] + padded[2:])).astype(
        jnp.bfloat16
    )
    planes, lines_here, length = activity.shape
    bins = measured.shape[3]
    row = planes * bins
    tof_kernel = kernels(subset_views[0], bins, length)
    angle_count = tof_kernel.shape[0]
    pairs = angle_count * lines_here
    projected = jnp.einsum("zlv,atv->zalt", blurred, tof_kernel, preferred_element_type=jnp.float32)
    projected = projected.reshape(planes, pairs, bins)

    slab_count = lax.axis_size("slab")
    block_total = measured.shape[1]
    capacity = 2 * block_total // slab_count
    slots = slab_count * capacity
    targets = block_slab[0, :, 0]
    onehot = (targets[:, None] == jnp.arange(slab_count, dtype=jnp.int32)[None, :]).astype(
        jnp.int32
    )
    slot_pos = jnp.sum((jnp.cumsum(onehot, axis=0) - onehot) * onehot, axis=1)
    flat_slot = targets * capacity + slot_pos
    place = (jnp.arange(slots, dtype=jnp.int32)[:, None] == flat_slot[None, :]).astype(
        jnp.bfloat16
    )
    pair_id = block_angle[0] * lines_here + block_line[0]
    extra = 128
    tag = jnp.broadcast_to(pair_id.astype(jnp.bfloat16)[:, None], (block_total, extra))
    outgoing = jnp.concatenate([measured[0].reshape(block_total, row), tag], axis=1)
    send = jnp.dot(place, outgoing, preferred_element_type=jnp.float32).astype(jnp.bfloat16)
    recv = exchange(send.reshape(slab_count, capacity, row + extra)).reshape(slots, row + extra)
    index = recv[:, row].astype(jnp.int32)
    rows = recv[:, :row].reshape(slots, planes, bins).transpose(1, 0, 2)
    pick = (index[:, None] == jnp.arange(pairs, dtype=jnp.int32)[None, :]).astype(jnp.float32)
    pick = jnp.broadcast_to(pick[None], (planes, slots, pairs))
    estimate = jnp.einsum("zjp,zpt->zjt", pick, projected, precision=lax.Precision.HIGH)
    ratios = rows.astype(jnp.float32) / (estimate + BACKGROUND)

    same = index[:, None] == index[None, :]
    earlier = jnp.arange(slots)[None, :] < jnp.arange(slots)[:, None]
    first = ~jnp.any(same & earlier, axis=1)
    merge = jnp.broadcast_to((same & first[:, None]).astype(jnp.float32)[None], (planes, slots, slots))
    merged = jnp.einsum(
        "zij,zjt->zit", merge, ratios, precision=lax.Precision.HIGH
    ).astype(jnp.bfloat16)

    views = subset_views[0]
    info = jnp.zeros((slots, bins), jnp.float32)
    info = info.at[:, 0].set(index.astype(jnp.float32))
    info = info.at[:, 1 : 1 + angle_count].set((views // 16).astype(jnp.float32)[None, :])
    info = info.at[:, 1 + angle_count : 1 + 2 * angle_count].set(
        (views % 16).astype(jnp.float32)[None, :]
    )
    payload = jnp.concatenate([merged, info.astype(jnp.bfloat16)[None]], axis=0)
    def back_project(got, kernel_k):
        index_k = got[planes, :, 0].astype(jnp.int32)
        order = jnp.arange(pairs, dtype=jnp.int32)
        wanted = (order % angle_count) * lines_here + order // angle_count
        scatter = (wanted[:, None] == index_k[None, :]).astype(jnp.bfloat16)
        scatter = jnp.broadcast_to(scatter[None], (planes, pairs, slots))
        dense = jnp.einsum(
            "zpi,zit->zpt", scatter, got[:planes], preferred_element_type=jnp.float32
        ).astype(jnp.bfloat16)
        dense = dense.reshape(planes, lines_here, angle_count, bins)
        return jnp.einsum("zlat,atv->zlv", dense, kernel_k, preferred_element_type=jnp.float32)

    def kernel_of(got):
        tail = got[planes, 0].astype(jnp.int32)
        views_k = tail[1 : 1 + angle_count] * 16 + tail[1 + angle_count : 1 + 2 * angle_count]
        return kernels(views_k, bins, length)

    view_count = lax.axis_size("view")
    rightward = [(i, (i + 1) % view_count) for i in range(view_count)]
    leftward = [(i, (i + view_count - 1) % view_count) for i in range(view_count)]
    half = (planes + 1) // 2
    from_left = lax.ppermute(payload, "view", rightward)
    from_right = lax.ppermute(payload, "view", leftward)
    me = lax.axis_index("view")
    payload, view_table = lax.optimization_barrier((payload, view_table))
    kernel_left = kernels(view_table[lax.rem(me + view_count - 1, view_count)], bins, length)
    kernel_right = kernels(view_table[lax.rem(me + 1, view_count)], bins, length)
    kernel_far = kernels(view_table[lax.rem(me + 2, view_count)], bins, length)
    total = back_project(payload, tof_kernel)
    total, from_left, from_right, kernel_left, kernel_right, kernel_far = lax.optimization_barrier(
        (total, from_left, from_right, kernel_left, kernel_right, kernel_far)
    )
    far_low = lax.ppermute(from_left[:half], "view", rightward)
    far_high = lax.ppermute(from_right[half:], "view", leftward)
    total = total + back_project(from_left, kernel_left)
    total = total + back_project(from_right, kernel_right)
    total, far_low, far_high = lax.optimization_barrier((total, far_low, far_high))
    far = jnp.concatenate([far_low, far_high], axis=0)
    total = total + back_project(far, kernel_far)
    edges = with_halo(weight * total, (("slab", 0),), 1)
    smoothed = (1.0 - 2.0 * weight) * total + edges[:-2] + edges[2:]
    return activity * smoothed / sensitivity


def solution(mesh):
    in_specs = (
        P("slab", None, None),
        P("slab", None, None),
        P("slab"),
        P("view", "slab", None, None),
        P("view", "slab", None),
        P("view", "slab"),
        P("view", "slab"),
        P("view", None),
    )
    out_specs = P("slab", None, None)
    return jax.shard_map(
        on_device, mesh=mesh, in_specs=in_specs, out_specs=out_specs, check_vma=False
    )
```

```python
import math

import jax
import jax.numpy as jnp
from jax import lax
from jax.experimental import pallas as pl
from jax.experimental.pallas import tpu as pltpu
from jax.sharding import PartitionSpec as P

MESH = pl.DeviceIdType.MESH

VIEWS_ALL = 336


BACKGROUND = 0.05


def with_halo(value, sides, width):
    for axis, dim in sides:
        size, length = (lax.axis_size(axis), value.shape[dim])
        up = [(i, (i + 1) % size) for i in range(size - 1)]
        down = [(j, i) for i, j in up]
        last = lax.slice_in_dim(value, length - width, length, axis=dim)
        leading = lax.slice_in_dim(value, 0, width, axis=dim)
        before = lax.ppermute(last, axis, up)
        after = lax.ppermute(leading, axis, down)
        value = jnp.concatenate([before, value, after], axis=dim)
    return value


def kernels(angles, bins, length):
    view_angle = math.pi * angles.astype(jnp.float32) / VIEWS_ALL
    step_width = length / bins
    deviation = 0.25 * step_width
    spacing = step_width * (0.75 + 0.25 * jnp.cos(2.0 * view_angle))
    offset = 1.5 * step_width * jnp.sin(view_angle)
    centres = (jnp.arange(bins, dtype=jnp.float32) + 0.5 - bins / 2)[None, :] * spacing[
        :, None
    ] + offset[:, None]
    voxel_pos = jnp.arange(length, dtype=jnp.float32) + 0.5 - length / 2
    distance = voxel_pos[None, None, :] - centres[:, :, None]
    values = jnp.exp(-distance * distance / (2.0 * deviation * deviation)) / (
        deviation * math.sqrt(2.0 * math.pi)
    )
    return values.astype(jnp.bfloat16)


def ring_gather_kernel(payload, out, send_sems, recv_sems):
    count = lax.axis_size("view")
    me = lax.axis_index("view")
    slab = lax.axis_index("slab")
    left = lax.rem(me + count - 1, count)
    right = lax.rem(me + 1, count)
    half = payload.shape[0] // 2
    rest = payload.shape[0] - half

    barrier = pltpu.get_barrier_semaphore()
    for neighbour in (left, right):
        pl.semaphore_signal(barrier, inc=1, device_id=(slab, neighbour), device_id_type=MESH)
    pl.semaphore_wait(barrier, 2)

    to_left = pltpu.make_async_remote_copy(
        src_ref=payload, dst_ref=out.at[1], send_sem=send_sems.at[0], recv_sem=recv_sems.at[1],
        device_id=(slab, left), device_id_type=MESH,
    )
    to_right = pltpu.make_async_remote_copy(
        src_ref=payload, dst_ref=out.at[0], send_sem=send_sems.at[1], recv_sem=recv_sems.at[0],
        device_id=(slab, right), device_id_type=MESH,
    )
    to_left.start()
    to_right.start()
    to_right.wait_recv()
    onward_right = pltpu.make_async_remote_copy(
        src_ref=out.at[0, pl.ds(0, half)], dst_ref=out.at[2, pl.ds(0, half)],
        send_sem=send_sems.at[2], recv_sem=recv_sems.at[2],
        device_id=(slab, right), device_id_type=MESH,
    )
    onward_right.start()
    to_left.wait_recv()
    onward_left = pltpu.make_async_remote_copy(
        src_ref=out.at[1, pl.ds(half, rest)], dst_ref=out.at[2, pl.ds(half, rest)],
        send_sem=send_sems.at[3], recv_sem=recv_sems.at[3],
        device_id=(slab, left), device_id_type=MESH,
    )
    onward_left.start()
    to_left.wait_send()
    to_right.wait_send()
    onward_right.wait_send()
    onward_left.wait_send()
    onward_right.wait_recv()
    onward_left.wait_recv()


def ring_gather(payload):
    return pl.pallas_call(
        ring_gather_kernel,
        out_shape=jax.ShapeDtypeStruct((3,) + payload.shape, payload.dtype),
        in_specs=[pl.BlockSpec(memory_space=pl.ANY)],
        out_specs=pl.BlockSpec(memory_space=pl.ANY),
        scratch_shapes=[pltpu.SemaphoreType.DMA((4,)), pltpu.SemaphoreType.DMA((4,))],
        compiler_params=pltpu.CompilerParams(collective_id=0, has_side_effects=True),
    )(payload)


def exchange_kernel(send, out, local_sem, send_sems, recv_sems):
    count = lax.axis_size("slab")
    me = lax.axis_index("slab")
    view = lax.axis_index("view")

    barrier = pltpu.get_barrier_semaphore()

    def greet(step, carry):
        peer = lax.rem(me + step, count)
        pl.semaphore_signal(barrier, inc=1, device_id=(peer, view), device_id_type=MESH)
        return carry

    lax.fori_loop(1, count, greet, 0)
    pl.semaphore_wait(barrier, count - 1)

    local = pltpu.make_async_copy(send.at[me], out.at[me], local_sem)
    local.start()

    def copy_to(step):
        peer = lax.rem(me + step, count)
        return pltpu.make_async_remote_copy(
            src_ref=send.at[peer], dst_ref=out.at[me],
            send_sem=send_sems.at[step], recv_sem=recv_sems.at[step],
            device_id=(peer, view), device_id_type=MESH,
        )

    def start(step, carry):
        copy_to(step).start()
        return carry

    def finish(step, carry):
        copy = copy_to(step)
        copy.wait_send()
        copy.wait_recv()
        return carry

    lax.fori_loop(1, count, start, 0)
    lax.fori_loop(1, count, finish, 0)
    local.wait()


def exchange(send):
    count = send.shape[0]
    return pl.pallas_call(
        exchange_kernel,
        out_shape=jax.ShapeDtypeStruct(send.shape, send.dtype),
        in_specs=[pl.BlockSpec(memory_space=pl.ANY)],
        out_specs=pl.BlockSpec(memory_space=pl.ANY),
        scratch_shapes=[
            pltpu.SemaphoreType.DMA(()),
            pltpu.SemaphoreType.DMA((count,)),
            pltpu.SemaphoreType.DMA((count,)),
        ],
        compiler_params=pltpu.CompilerParams(collective_id=1, has_side_effects=True),
    )(send)


def on_device(
    activity, sensitivity, psf_width, measured, block_slab, block_line, block_angle, subset_views
):
    weight = psf_width[:, None, None]
    padded = with_halo(activity, (("slab", 0),), 1)
    blurred = ((1.0 - 2.0 * weight) * activity + weight * (padded[:-2] + padded[2:])).astype(
        jnp.bfloat16
    )
    planes, lines_here, length = activity.shape
    bins = measured.shape[3]
    row = planes * bins
    tof_kernel = kernels(subset_views[0], bins, length)
    angle_count = tof_kernel.shape[0]
    pairs = angle_count * lines_here
    projected = jnp.einsum("zlv,atv->zalt", blurred, tof_kernel, preferred_element_type=jnp.float32)
    projected = projected.reshape(planes, pairs, bins)

    slab_count = lax.axis_size("slab")
    block_total = measured.shape[1]
    capacity = 2 * block_total // slab_count
    slots = slab_count * capacity
    targets = block_slab[0, :, 0]
    onehot = (targets[:, None] == jnp.arange(slab_count, dtype=jnp.int32)[None, :]).astype(
        jnp.int32
    )
    slot_pos = jnp.sum((jnp.cumsum(onehot, axis=0) - onehot) * onehot, axis=1)
    flat_slot = targets * capacity + slot_pos
    place = (jnp.arange(slots, dtype=jnp.int32)[:, None] == flat_slot[None, :]).astype(
        jnp.bfloat16
    )
    pair_id = block_angle[0] * lines_here + block_line[0]
    extra = 128
    tag = jnp.broadcast_to(pair_id.astype(jnp.bfloat16)[:, None], (block_total, extra))
    outgoing = jnp.concatenate([measured[0].reshape(block_total, row), tag], axis=1)
    send = jnp.dot(place, outgoing, preferred_element_type=jnp.float32).astype(jnp.bfloat16)
    recv = exchange(send.reshape(slab_count, capacity, row + extra)).reshape(slots, row + extra)
    index = recv[:, row].astype(jnp.int32)
    rows = recv[:, :row].reshape(slots, planes, bins).transpose(1, 0, 2)
    pick = (index[:, None] == jnp.arange(pairs, dtype=jnp.int32)[None, :]).astype(jnp.float32)
    pick = jnp.broadcast_to(pick[None], (planes, slots, pairs))
    estimate = jnp.einsum("zjp,zpt->zjt", pick, projected, precision=lax.Precision.HIGH)
    ratios = rows.astype(jnp.float32) / (estimate + BACKGROUND)

    same = index[:, None] == index[None, :]
    earlier = jnp.arange(slots)[None, :] < jnp.arange(slots)[:, None]
    first = ~jnp.any(same & earlier, axis=1)
    merge = jnp.broadcast_to((same & first[:, None]).astype(jnp.float32)[None], (planes, slots, slots))
    merged = jnp.einsum(
        "zij,zjt->zit", merge, ratios, precision=lax.Precision.HIGH
    ).astype(jnp.bfloat16)

    views = subset_views[0]
    info = jnp.zeros((slots, bins), jnp.float32)
    info = info.at[:, 0].set(index.astype(jnp.float32))
    info = info.at[:, 1 : 1 + angle_count].set((views // 16).astype(jnp.float32)[None, :])
    info = info.at[:, 1 + angle_count : 1 + 2 * angle_count].set(
        (views % 16).astype(jnp.float32)[None, :]
    )
    payload = jnp.concatenate([merged, info.astype(jnp.bfloat16)[None]], axis=0)
    def back_project(got, kernel_k):
        index_k = got[planes, :, 0].astype(jnp.int32)
        order = jnp.arange(pairs, dtype=jnp.int32)
        wanted = (order % angle_count) * lines_here + order // angle_count
        scatter = (wanted[:, None] == index_k[None, :]).astype(jnp.bfloat16)
        scatter = jnp.broadcast_to(scatter[None], (planes, pairs, slots))
        dense = jnp.einsum(
            "zpi,zit->zpt", scatter, got[:planes], preferred_element_type=jnp.float32
        ).astype(jnp.bfloat16)
        dense = dense.reshape(planes, lines_here, angle_count, bins)
        return jnp.einsum("zlat,atv->zlv", dense, kernel_k, preferred_element_type=jnp.float32)

    def kernel_of(got):
        tail = got[planes, 0].astype(jnp.int32)
        views_k = tail[1 : 1 + angle_count] * 16 + tail[1 + angle_count : 1 + 2 * angle_count]
        return kernels(views_k, bins, length)

    view_count = lax.axis_size("view")
    rightward = [(i, (i + 1) % view_count) for i in range(view_count)]
    leftward = [(i, (i + view_count - 1) % view_count) for i in range(view_count)]
    half = (planes + 1) // 2
    from_left = lax.ppermute(payload, "view", rightward)
    from_right = lax.ppermute(payload, "view", leftward)
    total = back_project(payload, tof_kernel)
    total, from_left, from_right = lax.optimization_barrier((total, from_left, from_right))
    far_low = lax.ppermute(from_left[:half], "view", rightward)
    far_high = lax.ppermute(from_right[half:], "view", leftward)
    total = total + back_project(from_left, kernel_of(from_left))
    total = total + back_project(from_right, kernel_of(from_right))
    total, far_low, far_high = lax.optimization_barrier((total, far_low, far_high))
    far = jnp.concatenate([far_low, far_high], axis=0)
    total = total + back_project(far, kernel_of(far))
    edges = with_halo(weight * total, (("slab", 0),), 1)
    smoothed = (1.0 - 2.0 * weight) * total + edges[:-2] + edges[2:]
    return activity * smoothed / sensitivity


def solution(mesh):
    in_specs = (
        P("slab", None, None),
        P("slab", None, None),
        P("slab"),
        P("view", "slab", None, None),
        P("view", "slab", None),
        P("view", "slab"),
        P("view", "slab"),
        P("view", None),
    )
    out_specs = P("slab", None, None)
    return jax.shard_map(
        on_device, mesh=mesh, in_specs=in_specs, out_specs=out_specs, check_vma=False
    )
```

```python
import math

import jax
import jax.numpy as jnp
from jax import lax
from jax.experimental import pallas as pl
from jax.experimental.pallas import tpu as pltpu
from jax.sharding import PartitionSpec as P

MESH = pl.DeviceIdType.MESH

VIEWS_ALL = 336


BACKGROUND = 0.05


def with_halo(value, sides, width):
    for axis, dim in sides:
        size, length = (lax.axis_size(axis), value.shape[dim])
        up = [(i, (i + 1) % size) for i in range(size - 1)]
        down = [(j, i) for i, j in up]
        last = lax.slice_in_dim(value, length - width, length, axis=dim)
        leading = lax.slice_in_dim(value, 0, width, axis=dim)
        before = lax.ppermute(last, axis, up)
        after = lax.ppermute(leading, axis, down)
        value = jnp.concatenate([before, value, after], axis=dim)
    return value


def kernels(angles, bins, length):
    view_angle = math.pi * angles.astype(jnp.float32) / VIEWS_ALL
    step_width = length / bins
    deviation = 0.25 * step_width
    spacing = step_width * (0.75 + 0.25 * jnp.cos(2.0 * view_angle))
    offset = 1.5 * step_width * jnp.sin(view_angle)
    centres = (jnp.arange(bins, dtype=jnp.float32) + 0.5 - bins / 2)[None, :] * spacing[
        :, None
    ] + offset[:, None]
    voxel_pos = jnp.arange(length, dtype=jnp.float32) + 0.5 - length / 2
    distance = voxel_pos[None, None, :] - centres[:, :, None]
    values = jnp.exp(-distance * distance / (2.0 * deviation * deviation)) / (
        deviation * math.sqrt(2.0 * math.pi)
    )
    return values.astype(jnp.bfloat16)


def ring_gather_kernel(payload, out, send_sems, recv_sems):
    count = lax.axis_size("view")
    me = lax.axis_index("view")
    slab = lax.axis_index("slab")
    left = lax.rem(me + count - 1, count)
    right = lax.rem(me + 1, count)
    half = payload.shape[0] // 2
    rest = payload.shape[0] - half

    barrier = pltpu.get_barrier_semaphore()
    for neighbour in (left, right):
        pl.semaphore_signal(barrier, inc=1, device_id=(slab, neighbour), device_id_type=MESH)
    pl.semaphore_wait(barrier, 2)

    to_left = pltpu.make_async_remote_copy(
        src_ref=payload, dst_ref=out.at[1], send_sem=send_sems.at[0], recv_sem=recv_sems.at[1],
        device_id=(slab, left), device_id_type=MESH,
    )
    to_right = pltpu.make_async_remote_copy(
        src_ref=payload, dst_ref=out.at[0], send_sem=send_sems.at[1], recv_sem=recv_sems.at[0],
        device_id=(slab, right), device_id_type=MESH,
    )
    to_left.start()
    to_right.start()
    to_right.wait_recv()
    onward_right = pltpu.make_async_remote_copy(
        src_ref=out.at[0, pl.ds(0, half)], dst_ref=out.at[2, pl.ds(0, half)],
        send_sem=send_sems.at[2], recv_sem=recv_sems.at[2],
        device_id=(slab, right), device_id_type=MESH,
    )
    onward_right.start()
    to_left.wait_recv()
    onward_left = pltpu.make_async_remote_copy(
        src_ref=out.at[1, pl.ds(half, rest)], dst_ref=out.at[2, pl.ds(half, rest)],
        send_sem=send_sems.at[3], recv_sem=recv_sems.at[3],
        device_id=(slab, left), device_id_type=MESH,
    )
    onward_left.start()
    to_left.wait_send()
    to_right.wait_send()
    onward_right.wait_send()
    onward_left.wait_send()
    onward_right.wait_recv()
    onward_left.wait_recv()


def ring_gather(payload):
    return pl.pallas_call(
        ring_gather_kernel,
        out_shape=jax.ShapeDtypeStruct((3,) + payload.shape, payload.dtype),
        in_specs=[pl.BlockSpec(memory_space=pl.ANY)],
        out_specs=pl.BlockSpec(memory_space=pl.ANY),
        scratch_shapes=[pltpu.SemaphoreType.DMA((4,)), pltpu.SemaphoreType.DMA((4,))],
        compiler_params=pltpu.CompilerParams(collective_id=0, has_side_effects=True),
    )(payload)


def exchange_kernel(send, image, spread, out, projected, local_sem, send_sems, recv_sems):
    count = lax.axis_size("slab")
    me = lax.axis_index("slab")
    view = lax.axis_index("view")

    barrier = pltpu.get_barrier_semaphore()

    def greet(step, carry):
        peer = lax.rem(me + step, count)
        pl.semaphore_signal(barrier, inc=1, device_id=(peer, view), device_id_type=MESH)
        return carry

    lax.fori_loop(1, count, greet, 0)
    pl.semaphore_wait(barrier, count - 1)

    local = pltpu.make_async_copy(send.at[me], out.at[me], local_sem)
    local.start()

    def copy_to(step):
        peer = lax.rem(me + step, count)
        return pltpu.make_async_remote_copy(
            src_ref=send.at[peer], dst_ref=out.at[me],
            send_sem=send_sems.at[step], recv_sem=recv_sems.at[step],
            device_id=(peer, view), device_id_type=MESH,
        )

    def start(step, carry):
        copy_to(step).start()
        return carry

    def finish(step, carry):
        copy = copy_to(step)
        copy.wait_send()
        copy.wait_recv()
        return carry

    lax.fori_loop(1, count, start, 0)

    tile = 128

    @pl.loop(0, image.shape[0] // tile)
    def _(step):
        rows = pl.ds(pl.multiple_of(step * tile, tile), tile)
        projected[rows, :] = lax.dot_general(
            image[rows, :], spread[...], (((1,), (1,)), ((), ())),
            preferred_element_type=jnp.float32,
        )

    lax.fori_loop(1, count, finish, 0)
    local.wait()


def exchange(send, image, spread):
    count = send.shape[0]
    vmem = pl.BlockSpec(memory_space=pltpu.VMEM)
    return pl.pallas_call(
        exchange_kernel,
        out_shape=(
            jax.ShapeDtypeStruct(send.shape, send.dtype),
            jax.ShapeDtypeStruct((image.shape[0], spread.shape[0]), jnp.float32),
        ),
        in_specs=[pl.BlockSpec(memory_space=pl.ANY), vmem, vmem],
        out_specs=(pl.BlockSpec(memory_space=pl.ANY), vmem),
        scratch_shapes=[
            pltpu.SemaphoreType.DMA(()),
            pltpu.SemaphoreType.DMA((count,)),
            pltpu.SemaphoreType.DMA((count,)),
        ],
        compiler_params=pltpu.CompilerParams(collective_id=1, has_side_effects=True),
    )(send, image, spread)


def on_device(
    activity, sensitivity, psf_width, measured, block_slab, block_line, block_angle, subset_views
):
    weight = psf_width[:, None, None]
    padded = with_halo(activity, (("slab", 0),), 1)
    blurred = ((1.0 - 2.0 * weight) * activity + weight * (padded[:-2] + padded[2:])).astype(
        jnp.bfloat16
    )
    planes, lines_here, length = activity.shape
    bins = measured.shape[3]
    row = planes * bins
    tof_kernel = kernels(subset_views[0], bins, length)
    angle_count = tof_kernel.shape[0]
    pairs = angle_count * lines_here

    slab_count = lax.axis_size("slab")
    block_total = measured.shape[1]
    capacity = 2 * block_total // slab_count
    slots = slab_count * capacity
    targets = block_slab[0, :, 0]
    onehot = (targets[:, None] == jnp.arange(slab_count, dtype=jnp.int32)[None, :]).astype(
        jnp.int32
    )
    slot_pos = jnp.sum((jnp.cumsum(onehot, axis=0) - onehot) * onehot, axis=1)
    flat_slot = targets * capacity + slot_pos
    place = (jnp.arange(slots, dtype=jnp.int32)[:, None] == flat_slot[None, :]).astype(
        jnp.bfloat16
    )
    pair_id = block_line[0] * angle_count + block_angle[0]
    extra = 128
    tag = jnp.broadcast_to(pair_id.astype(jnp.bfloat16)[:, None], (block_total, extra))
    outgoing = jnp.concatenate([measured[0].reshape(block_total, row), tag], axis=1)
    send = jnp.dot(place, outgoing, preferred_element_type=jnp.float32).astype(jnp.bfloat16)
    recv, projected = exchange(
        send.reshape(slab_count, capacity, row + extra),
        blurred.reshape(planes * lines_here, length),
        tof_kernel.reshape(pairs // lines_here * bins, length),
    )
    recv = recv.reshape(slots, row + extra)
    projected = projected.reshape(planes, pairs, bins)
    index = recv[:, row].astype(jnp.int32)
    rows = recv[:, :row].reshape(slots, planes, bins).transpose(1, 0, 2)
    pick = (index[:, None] == jnp.arange(pairs, dtype=jnp.int32)[None, :]).astype(jnp.float32)
    pick = jnp.broadcast_to(pick[None], (planes, slots, pairs))
    estimate = jnp.einsum("zjp,zpt->zjt", pick, projected, precision=lax.Precision.HIGH)
    ratios = rows.astype(jnp.float32) / (estimate + BACKGROUND)

    same = index[:, None] == index[None, :]
    earlier = jnp.arange(slots)[None, :] < jnp.arange(slots)[:, None]
    first = ~jnp.any(same & earlier, axis=1)
    merge = jnp.broadcast_to((same & first[:, None]).astype(jnp.float32)[None], (planes, slots, slots))
    merged = jnp.einsum(
        "zij,zjt->zit", merge, ratios, precision=lax.Precision.HIGH
    ).astype(jnp.bfloat16)

    views = subset_views[0]
    info = jnp.zeros((slots, bins), jnp.float32)
    info = info.at[:, 0].set(index.astype(jnp.float32))
    info = info.at[:, 1 : 1 + angle_count].set((views // 16).astype(jnp.float32)[None, :])
    info = info.at[:, 1 + angle_count : 1 + 2 * angle_count].set(
        (views % 16).astype(jnp.float32)[None, :]
    )
    payload = jnp.concatenate([merged, info.astype(jnp.bfloat16)[None]], axis=0)
    def back_project(got, kernel_k):
        index_k = got[planes, :, 0].astype(jnp.int32)
        order = jnp.arange(pairs, dtype=jnp.int32)
        scatter = (order[:, None] == index_k[None, :]).astype(jnp.bfloat16)
        scatter = jnp.broadcast_to(scatter[None], (planes, pairs, slots))
        dense = jnp.einsum(
            "zpi,zit->zpt", scatter, got[:planes], preferred_element_type=jnp.float32
        ).astype(jnp.bfloat16)
        dense = dense.reshape(planes, lines_here, angle_count, bins)
        return jnp.einsum("zlat,atv->zlv", dense, kernel_k, preferred_element_type=jnp.float32)

    def kernel_of(got):
        tail = got[planes, 0].astype(jnp.int32)
        views_k = tail[1 : 1 + angle_count] * 16 + tail[1 + angle_count : 1 + 2 * angle_count]
        return kernels(views_k, bins, length)

    view_count = lax.axis_size("view")
    rightward = [(i, (i + 1) % view_count) for i in range(view_count)]
    leftward = [(i, (i + view_count - 1) % view_count) for i in range(view_count)]
    half = (planes + 1) // 2
    from_left = lax.ppermute(payload, "view", rightward)
    from_right = lax.ppermute(payload, "view", leftward)
    total = back_project(payload, tof_kernel)
    total, from_left, from_right = lax.optimization_barrier((total, from_left, from_right))
    far_low = lax.ppermute(from_left[:half], "view", rightward)
    far_high = lax.ppermute(from_right[half:], "view", leftward)
    total = total + back_project(from_left, kernel_of(from_left))
    total = total + back_project(from_right, kernel_of(from_right))
    total, far_low, far_high = lax.optimization_barrier((total, far_low, far_high))
    far = jnp.concatenate([far_low, far_high], axis=0)
    total = total + back_project(far, kernel_of(far))
    edges = with_halo(weight * total, (("slab", 0),), 1)
    smoothed = (1.0 - 2.0 * weight) * total + edges[:-2] + edges[2:]
    return activity * smoothed / sensitivity


def solution(mesh):
    in_specs = (
        P("slab", None, None),
        P("slab", None, None),
        P("slab"),
        P("view", "slab", None, None),
        P("view", "slab", None),
        P("view", "slab"),
        P("view", "slab"),
        P("view", None),
    )
    out_specs = P("slab", None, None)
    return jax.shard_map(
        on_device, mesh=mesh, in_specs=in_specs, out_specs=out_specs, check_vma=False
    )
```

```python
import math

import jax
import jax.numpy as jnp
from jax import lax
from jax.experimental import pallas as pl
from jax.experimental.pallas import tpu as pltpu
from jax.sharding import PartitionSpec as P

MESH = pl.DeviceIdType.MESH

VIEWS_ALL = 336


BACKGROUND = 0.05


def with_halo(value, sides, width):
    for axis, dim in sides:
        size, length = (lax.axis_size(axis), value.shape[dim])
        up = [(i, (i + 1) % size) for i in range(size - 1)]
        down = [(j, i) for i, j in up]
        last = lax.slice_in_dim(value, length - width, length, axis=dim)
        leading = lax.slice_in_dim(value, 0, width, axis=dim)
        before = lax.ppermute(last, axis, up)
        after = lax.ppermute(leading, axis, down)
        value = jnp.concatenate([before, value, after], axis=dim)
    return value


def kernels(angles, bins, length):
    view_angle = math.pi * angles.astype(jnp.float32) / VIEWS_ALL
    step_width = length / bins
    deviation = 0.25 * step_width
    spacing = step_width * (0.75 + 0.25 * jnp.cos(2.0 * view_angle))
    offset = 1.5 * step_width * jnp.sin(view_angle)
    centres = (jnp.arange(bins, dtype=jnp.float32) + 0.5 - bins / 2)[None, :] * spacing[
        :, None
    ] + offset[:, None]
    voxel_pos = jnp.arange(length, dtype=jnp.float32) + 0.5 - length / 2
    distance = voxel_pos[None, None, :] - centres[:, :, None]
    values = jnp.exp(-distance * distance / (2.0 * deviation * deviation)) / (
        deviation * math.sqrt(2.0 * math.pi)
    )
    return values.astype(jnp.bfloat16)


def ring_gather_kernel(payload, out, send_sems, recv_sems):
    count = lax.axis_size("view")
    me = lax.axis_index("view")
    slab = lax.axis_index("slab")
    left = lax.rem(me + count - 1, count)
    right = lax.rem(me + 1, count)
    half = payload.shape[0] // 2
    rest = payload.shape[0] - half

    barrier = pltpu.get_barrier_semaphore()
    for neighbour in (left, right):
        pl.semaphore_signal(barrier, inc=1, device_id=(slab, neighbour), device_id_type=MESH)
    pl.semaphore_wait(barrier, 2)

    to_left = pltpu.make_async_remote_copy(
        src_ref=payload, dst_ref=out.at[1], send_sem=send_sems.at[0], recv_sem=recv_sems.at[1],
        device_id=(slab, left), device_id_type=MESH,
    )
    to_right = pltpu.make_async_remote_copy(
        src_ref=payload, dst_ref=out.at[0], send_sem=send_sems.at[1], recv_sem=recv_sems.at[0],
        device_id=(slab, right), device_id_type=MESH,
    )
    to_left.start()
    to_right.start()
    to_right.wait_recv()
    onward_right = pltpu.make_async_remote_copy(
        src_ref=out.at[0, pl.ds(0, half)], dst_ref=out.at[2, pl.ds(0, half)],
        send_sem=send_sems.at[2], recv_sem=recv_sems.at[2],
        device_id=(slab, right), device_id_type=MESH,
    )
    onward_right.start()
    to_left.wait_recv()
    onward_left = pltpu.make_async_remote_copy(
        src_ref=out.at[1, pl.ds(half, rest)], dst_ref=out.at[2, pl.ds(half, rest)],
        send_sem=send_sems.at[3], recv_sem=recv_sems.at[3],
        device_id=(slab, left), device_id_type=MESH,
    )
    onward_left.start()
    to_left.wait_send()
    to_right.wait_send()
    onward_right.wait_send()
    onward_left.wait_send()
    onward_right.wait_recv()
    onward_left.wait_recv()


def ring_gather(payload):
    return pl.pallas_call(
        ring_gather_kernel,
        out_shape=jax.ShapeDtypeStruct((3,) + payload.shape, payload.dtype),
        in_specs=[pl.BlockSpec(memory_space=pl.ANY)],
        out_specs=pl.BlockSpec(memory_space=pl.ANY),
        scratch_shapes=[pltpu.SemaphoreType.DMA((4,)), pltpu.SemaphoreType.DMA((4,))],
        compiler_params=pltpu.CompilerParams(collective_id=0, has_side_effects=True),
    )(payload)


def exchange_kernel(send, out, local_sem, send_sems, recv_sems):
    count = lax.axis_size("slab")
    me = lax.axis_index("slab")
    view = lax.axis_index("view")

    barrier = pltpu.get_barrier_semaphore()

    def greet(step, carry):
        peer = lax.rem(me + step, count)
        pl.semaphore_signal(barrier, inc=1, device_id=(peer, view), device_id_type=MESH)
        return carry

    lax.fori_loop(1, count, greet, 0)
    pl.semaphore_wait(barrier, count - 1)

    local = pltpu.make_async_copy(send.at[me], out.at[me], local_sem)
    local.start()

    def copy_to(step):
        peer = lax.rem(me + step, count)
        return pltpu.make_async_remote_copy(
            src_ref=send.at[peer], dst_ref=out.at[me],
            send_sem=send_sems.at[step], recv_sem=recv_sems.at[step],
            device_id=(peer, view), device_id_type=MESH,
        )

    def start(step, carry):
        copy_to(step).start()
        return carry

    def finish(step, carry):
        copy = copy_to(step)
        copy.wait_send()
        copy.wait_recv()
        return carry

    lax.fori_loop(1, count, start, 0)
    lax.fori_loop(1, count, finish, 0)
    local.wait()


def exchange(send):
    count = send.shape[0]
    return pl.pallas_call(
        exchange_kernel,
        out_shape=jax.ShapeDtypeStruct(send.shape, send.dtype),
        in_specs=[pl.BlockSpec(memory_space=pl.ANY)],
        out_specs=pl.BlockSpec(memory_space=pl.ANY),
        scratch_shapes=[
            pltpu.SemaphoreType.DMA(()),
            pltpu.SemaphoreType.DMA((count,)),
            pltpu.SemaphoreType.DMA((count,)),
        ],
        compiler_params=pltpu.CompilerParams(collective_id=1, has_side_effects=True),
    )(send)


def on_device(
    activity, sensitivity, psf_width, measured, block_slab, block_line, block_angle, subset_views
):
    weight = psf_width[:, None, None]
    padded = with_halo(activity, (("slab", 0),), 1)
    blurred = ((1.0 - 2.0 * weight) * activity + weight * (padded[:-2] + padded[2:])).astype(
        jnp.bfloat16
    )
    planes, lines_here, length = activity.shape
    bins = measured.shape[3]
    row = planes * bins
    tof_kernel = kernels(subset_views[0], bins, length)
    angle_count = tof_kernel.shape[0]
    pairs = angle_count * lines_here
    projected = jnp.einsum("zlv,atv->zalt", blurred, tof_kernel, preferred_element_type=jnp.float32)
    projected = projected.reshape(planes, pairs, bins)

    slab_count = lax.axis_size("slab")
    block_total = measured.shape[1]
    capacity = 2 * block_total // slab_count
    slots = slab_count * capacity
    targets = block_slab[0, :, 0]
    onehot = (targets[:, None] == jnp.arange(slab_count, dtype=jnp.int32)[None, :]).astype(
        jnp.int32
    )
    slot_pos = jnp.sum((jnp.cumsum(onehot, axis=0) - onehot) * onehot, axis=1)
    flat_slot = targets * capacity + slot_pos
    place = (jnp.arange(slots, dtype=jnp.int32)[:, None] == flat_slot[None, :]).astype(
        jnp.bfloat16
    )
    pair_id = block_angle[0] * lines_here + block_line[0]
    extra = 128
    tag = jnp.broadcast_to(pair_id.astype(jnp.bfloat16)[:, None], (block_total, extra))
    outgoing = jnp.concatenate([measured[0].reshape(block_total, row), tag], axis=1)
    send = jnp.dot(place, outgoing, preferred_element_type=jnp.float32).astype(jnp.bfloat16)
    recv = lax.all_to_all(
        send.reshape(slab_count, capacity, row + extra), "slab", 0, 0, tiled=True
    ).reshape(slots, row + extra)
    index = recv[:, row].astype(jnp.int32)
    rows = recv[:, :row].reshape(slots, planes, bins).transpose(1, 0, 2)
    pick = (index[:, None] == jnp.arange(pairs, dtype=jnp.int32)[None, :]).astype(jnp.float32)
    pick = jnp.broadcast_to(pick[None], (planes, slots, pairs))
    estimate = jnp.einsum("zjp,zpt->zjt", pick, projected, precision=lax.Precision.HIGH)
    ratios = rows.astype(jnp.float32) / (estimate + BACKGROUND)

    same = index[:, None] == index[None, :]
    earlier = jnp.arange(slots)[None, :] < jnp.arange(slots)[:, None]
    first = ~jnp.any(same & earlier, axis=1)
    merge = jnp.broadcast_to((same & first[:, None]).astype(jnp.float32)[None], (planes, slots, slots))
    merged = jnp.einsum(
        "zij,zjt->zit", merge, ratios, precision=lax.Precision.HIGH
    ).astype(jnp.bfloat16)

    views = subset_views[0]
    info = jnp.zeros((slots, bins), jnp.float32)
    info = info.at[:, 0].set(index.astype(jnp.float32))
    info = info.at[:, 1 : 1 + angle_count].set((views // 16).astype(jnp.float32)[None, :])
    info = info.at[:, 1 + angle_count : 1 + 2 * angle_count].set(
        (views % 16).astype(jnp.float32)[None, :]
    )
    payload = jnp.concatenate([merged, info.astype(jnp.bfloat16)[None]], axis=0)
    def back_project(got, kernel_k):
        index_k = got[planes, :, 0].astype(jnp.int32)
        order = jnp.arange(pairs, dtype=jnp.int32)
        wanted = (order % angle_count) * lines_here + order // angle_count
        scatter = (wanted[:, None] == index_k[None, :]).astype(jnp.bfloat16)
        scatter = jnp.broadcast_to(scatter[None], (planes, pairs, slots))
        dense = jnp.einsum(
            "zpi,zit->zpt", scatter, got[:planes], preferred_element_type=jnp.float32
        ).astype(jnp.bfloat16)
        dense = dense.reshape(planes, lines_here, angle_count, bins)
        return jnp.einsum("zlat,atv->zlv", dense, kernel_k, preferred_element_type=jnp.float32)

    def kernel_of(got):
        tail = got[planes, 0].astype(jnp.int32)
        views_k = tail[1 : 1 + angle_count] * 16 + tail[1 + angle_count : 1 + 2 * angle_count]
        return kernels(views_k, bins, length)

    view_count = lax.axis_size("view")
    rightward = [(i, (i + 1) % view_count) for i in range(view_count)]
    leftward = [(i, (i + view_count - 1) % view_count) for i in range(view_count)]
    half = (planes + 1) // 2
    from_left = lax.ppermute(payload, "view", rightward)
    from_right = lax.ppermute(payload, "view", leftward)
    total = back_project(payload, tof_kernel)
    total, from_left, from_right = lax.optimization_barrier((total, from_left, from_right))
    far_low = lax.ppermute(from_left[:half], "view", rightward)
    far_high = lax.ppermute(from_right[half:], "view", leftward)
    total = total + back_project(from_left, kernel_of(from_left))
    total = total + back_project(from_right, kernel_of(from_right))
    total, far_low, far_high = lax.optimization_barrier((total, far_low, far_high))
    far = jnp.concatenate([far_low, far_high], axis=0)
    total = total + back_project(far, kernel_of(far))
    edges = with_halo(weight * total, (("slab", 0),), 1)
    smoothed = (1.0 - 2.0 * weight) * total + edges[:-2] + edges[2:]
    return activity * smoothed / sensitivity


def solution(mesh):
    in_specs = (
        P("slab", None, None),
        P("slab", None, None),
        P("slab"),
        P("view", "slab", None, None),
        P("view", "slab", None),
        P("view", "slab"),
        P("view", "slab"),
        P("view", None),
    )
    out_specs = P("slab", None, None)
    return jax.shard_map(
        on_device, mesh=mesh, in_specs=in_specs, out_specs=out_specs, check_vma=False
    )
```

```python
import math

import jax
import jax.numpy as jnp
from jax import lax
from jax.experimental import pallas as pl
from jax.experimental.pallas import tpu as pltpu
from jax.sharding import PartitionSpec as P

MESH = pl.DeviceIdType.MESH

VIEWS_ALL = 336


BACKGROUND = 0.05


def with_halo(value, sides, width):
    for axis, dim in sides:
        size, length = (lax.axis_size(axis), value.shape[dim])
        up = [(i, (i + 1) % size) for i in range(size - 1)]
        down = [(j, i) for i, j in up]
        last = lax.slice_in_dim(value, length - width, length, axis=dim)
        leading = lax.slice_in_dim(value, 0, width, axis=dim)
        before = lax.ppermute(last, axis, up)
        after = lax.ppermute(leading, axis, down)
        value = jnp.concatenate([before, value, after], axis=dim)
    return value


def kernels(angles, bins, length):
    view_angle = math.pi * angles.astype(jnp.float32) / VIEWS_ALL
    step_width = length / bins
    deviation = 0.25 * step_width
    spacing = step_width * (0.75 + 0.25 * jnp.cos(2.0 * view_angle))
    offset = 1.5 * step_width * jnp.sin(view_angle)
    centres = (jnp.arange(bins, dtype=jnp.float32) + 0.5 - bins / 2)[None, :] * spacing[
        :, None
    ] + offset[:, None]
    voxel_pos = jnp.arange(length, dtype=jnp.float32) + 0.5 - length / 2
    distance = voxel_pos[None, None, :] - centres[:, :, None]
    values = jnp.exp(-distance * distance / (2.0 * deviation * deviation)) / (
        deviation * math.sqrt(2.0 * math.pi)
    )
    return values.astype(jnp.bfloat16)


def ring_gather_kernel(payload, out, send_sems, recv_sems):
    count = lax.axis_size("view")
    me = lax.axis_index("view")
    slab = lax.axis_index("slab")
    left = lax.rem(me + count - 1, count)
    right = lax.rem(me + 1, count)
    half = payload.shape[0] // 2
    rest = payload.shape[0] - half

    barrier = pltpu.get_barrier_semaphore()
    for neighbour in (left, right):
        pl.semaphore_signal(barrier, inc=1, device_id=(slab, neighbour), device_id_type=MESH)
    pl.semaphore_wait(barrier, 2)

    to_left = pltpu.make_async_remote_copy(
        src_ref=payload, dst_ref=out.at[1], send_sem=send_sems.at[0], recv_sem=recv_sems.at[1],
        device_id=(slab, left), device_id_type=MESH,
    )
    to_right = pltpu.make_async_remote_copy(
        src_ref=payload, dst_ref=out.at[0], send_sem=send_sems.at[1], recv_sem=recv_sems.at[0],
        device_id=(slab, right), device_id_type=MESH,
    )
    to_left.start()
    to_right.start()
    to_right.wait_recv()
    onward_right = pltpu.make_async_remote_copy(
        src_ref=out.at[0, pl.ds(0, half)], dst_ref=out.at[2, pl.ds(0, half)],
        send_sem=send_sems.at[2], recv_sem=recv_sems.at[2],
        device_id=(slab, right), device_id_type=MESH,
    )
    onward_right.start()
    to_left.wait_recv()
    onward_left = pltpu.make_async_remote_copy(
        src_ref=out.at[1, pl.ds(half, rest)], dst_ref=out.at[2, pl.ds(half, rest)],
        send_sem=send_sems.at[3], recv_sem=recv_sems.at[3],
        device_id=(slab, left), device_id_type=MESH,
    )
    onward_left.start()
    to_left.wait_send()
    to_right.wait_send()
    onward_right.wait_send()
    onward_left.wait_send()
    onward_right.wait_recv()
    onward_left.wait_recv()


def ring_gather(payload):
    return pl.pallas_call(
        ring_gather_kernel,
        out_shape=jax.ShapeDtypeStruct((3,) + payload.shape, payload.dtype),
        in_specs=[pl.BlockSpec(memory_space=pl.ANY)],
        out_specs=pl.BlockSpec(memory_space=pl.ANY),
        scratch_shapes=[pltpu.SemaphoreType.DMA((4,)), pltpu.SemaphoreType.DMA((4,))],
        compiler_params=pltpu.CompilerParams(collective_id=0, has_side_effects=True),
    )(payload)


def exchange_kernel(send, out, local_sem, send_sems, recv_sems):
    count = lax.axis_size("slab")
    me = lax.axis_index("slab")
    view = lax.axis_index("view")

    barrier = pltpu.get_barrier_semaphore()

    def greet(step, carry):
        peer = lax.rem(me + step, count)
        pl.semaphore_signal(barrier, inc=1, device_id=(peer, view), device_id_type=MESH)
        return carry

    lax.fori_loop(1, count, greet, 0)
    pl.semaphore_wait(barrier, count - 1)

    local = pltpu.make_async_copy(send.at[me], out.at[me], local_sem)
    local.start()

    def copy_to(step):
        peer = lax.rem(me + step, count)
        return pltpu.make_async_remote_copy(
            src_ref=send.at[peer], dst_ref=out.at[me],
            send_sem=send_sems.at[step], recv_sem=recv_sems.at[step],
            device_id=(peer, view), device_id_type=MESH,
        )

    def start(step, carry):
        copy_to(step).start()
        return carry

    def finish(step, carry):
        copy = copy_to(step)
        copy.wait_send()
        copy.wait_recv()
        return carry

    lax.fori_loop(1, count, start, 0)
    lax.fori_loop(1, count, finish, 0)
    local.wait()


def exchange(send):
    count = send.shape[0]
    return pl.pallas_call(
        exchange_kernel,
        out_shape=jax.ShapeDtypeStruct(send.shape, send.dtype),
        in_specs=[pl.BlockSpec(memory_space=pl.ANY)],
        out_specs=pl.BlockSpec(memory_space=pl.ANY),
        scratch_shapes=[
            pltpu.SemaphoreType.DMA(()),
            pltpu.SemaphoreType.DMA((count,)),
            pltpu.SemaphoreType.DMA((count,)),
        ],
        compiler_params=pltpu.CompilerParams(collective_id=1, has_side_effects=True),
    )(send)


def on_device(
    activity, sensitivity, psf_width, measured, block_slab, block_line, block_angle, subset_views
):
    weight = psf_width[:, None, None]
    padded = with_halo(activity, (("slab", 0),), 1)
    blurred = ((1.0 - 2.0 * weight) * activity + weight * (padded[:-2] + padded[2:])).astype(
        jnp.bfloat16
    )
    planes, lines_here, length = activity.shape
    bins = measured.shape[3]
    row = planes * bins
    tof_kernel = kernels(subset_views[0], bins, length)
    angle_count = tof_kernel.shape[0]
    pairs = angle_count * lines_here
    projected = jnp.einsum("zlv,atv->zalt", blurred, tof_kernel, preferred_element_type=jnp.float32)
    projected = projected.reshape(planes, pairs, bins)

    slab_count = lax.axis_size("slab")
    block_total = measured.shape[1]
    capacity = 2 * block_total // slab_count
    slots = slab_count * capacity
    targets = block_slab[0, :, 0]
    onehot = (targets[:, None] == jnp.arange(slab_count, dtype=jnp.int32)[None, :]).astype(
        jnp.int32
    )
    slot_pos = jnp.sum((jnp.cumsum(onehot, axis=0) - onehot) * onehot, axis=1)
    flat_slot = targets * capacity + slot_pos
    place = (jnp.arange(slots, dtype=jnp.int32)[:, None] == flat_slot[None, :]).astype(
        jnp.bfloat16
    )
    pair_id = block_angle[0] * lines_here + block_line[0]
    extra = 128
    tag = jnp.broadcast_to(pair_id.astype(jnp.bfloat16)[:, None], (block_total, extra))
    outgoing = jnp.concatenate([measured[0].reshape(block_total, row), tag], axis=1)
    send = jnp.dot(place, outgoing, preferred_element_type=jnp.float32).astype(jnp.bfloat16)
    recv = lax.all_to_all(
        send.reshape(slab_count, capacity, row + extra), "slab", 0, 0, tiled=True
    ).reshape(slots, row + extra)
    index = recv[:, row].astype(jnp.int32)
    rows = recv[:, :row].reshape(slots, planes, bins).transpose(1, 0, 2)
    pick = (index[:, None] == jnp.arange(pairs, dtype=jnp.int32)[None, :]).astype(jnp.float32)
    pick = jnp.broadcast_to(pick[None], (planes, slots, pairs))
    estimate = jnp.einsum("zjp,zpt->zjt", pick, projected, precision=lax.Precision.HIGH)
    ratios = rows.astype(jnp.float32) / (estimate + BACKGROUND)

    same = index[:, None] == index[None, :]
    earlier = jnp.arange(slots)[None, :] < jnp.arange(slots)[:, None]
    first = ~jnp.any(same & earlier, axis=1)
    merge = jnp.broadcast_to((same & first[:, None]).astype(jnp.float32)[None], (planes, slots, slots))
    merged = jnp.einsum(
        "zij,zjt->zit", merge, ratios, precision=lax.Precision.HIGH
    ).astype(jnp.bfloat16)

    views = subset_views[0]
    info = jnp.zeros((slots, bins), jnp.float32)
    info = info.at[:, 0].set(index.astype(jnp.float32))
    info = info.at[:, 1 : 1 + angle_count].set((views // 16).astype(jnp.float32)[None, :])
    info = info.at[:, 1 + angle_count : 1 + 2 * angle_count].set(
        (views % 16).astype(jnp.float32)[None, :]
    )
    payload = jnp.concatenate([merged, info.astype(jnp.bfloat16)[None]], axis=0)
    def spread_out(got):
        index_k = got[planes, :, 0].astype(jnp.int32)
        order = jnp.arange(pairs, dtype=jnp.int32)
        wanted = (order % angle_count) * lines_here + order // angle_count
        scatter = (wanted[:, None] == index_k[None, :]).astype(jnp.bfloat16)
        scatter = jnp.broadcast_to(scatter[None], (planes, pairs, slots))
        dense = jnp.einsum(
            "zpi,zit->zpt", scatter, got[:planes], preferred_element_type=jnp.float32
        ).astype(jnp.bfloat16)
        return dense.reshape(planes, lines_here, angle_count, bins)

    def back_project(got, kernel_k):
        return jnp.einsum(
            "zlat,atv->zlv", spread_out(got), kernel_k, preferred_element_type=jnp.float32
        )

    def kernel_of(got):
        tail = got[planes, 0].astype(jnp.int32)
        views_k = tail[1 : 1 + angle_count] * 16 + tail[1 + angle_count : 1 + 2 * angle_count]
        return kernels(views_k, bins, length)

    view_count = lax.axis_size("view")
    rightward = [(i, (i + 1) % view_count) for i in range(view_count)]
    leftward = [(i, (i + view_count - 1) % view_count) for i in range(view_count)]
    half = (planes + 1) // 2
    from_left = lax.ppermute(payload, "view", rightward)
    from_right = lax.ppermute(payload, "view", leftward)
    total = back_project(payload, tof_kernel)
    total, from_left, from_right = lax.optimization_barrier((total, from_left, from_right))
    far_low = lax.ppermute(from_left[:half], "view", rightward)
    far_high = lax.ppermute(from_right[half:], "view", leftward)
    total = total + back_project(from_left, kernel_of(from_left))
    total = total + back_project(from_right, kernel_of(from_right))
    total, far_low, far_high = lax.optimization_barrier((total, far_low, far_high))
    far = jnp.concatenate([far_low, far_high], axis=0)
    kernel_far = kernel_of(far)
    dense_far = spread_out(far)
    low, high = (
        total[plane] + jnp.einsum("lat,atv->lv", dense_far[plane], kernel_far,
                                  preferred_element_type=jnp.float32)
        for plane in (0, planes - 1)
    )
    size = lax.axis_size("slab")
    up = [(i, (i + 1) % size) for i in range(size - 1)]
    down = [(j, i) for i, j in up]
    from_below = lax.ppermute((weight[planes - 1] * high)[None], "slab", up)
    from_above = lax.ppermute((weight[0] * low)[None], "slab", down)
    total = total + jnp.einsum(
        "zlat,atv->zlv", dense_far, kernel_far, preferred_element_type=jnp.float32
    )
    weighted = weight * total
    below = jnp.concatenate([from_below, weighted[: planes - 1]], axis=0)
    above = jnp.concatenate([weighted[1:], from_above], axis=0)
    smoothed = (1.0 - 2.0 * weight) * total + below + above
    return activity * smoothed / sensitivity


def solution(mesh):
    in_specs = (
        P("slab", None, None),
        P("slab", None, None),
        P("slab"),
        P("view", "slab", None, None),
        P("view", "slab", None),
        P("view", "slab"),
        P("view", "slab"),
        P("view", None),
    )
    out_specs = P("slab", None, None)
    return jax.shard_map(
        on_device, mesh=mesh, in_specs=in_specs, out_specs=out_specs, check_vma=False
    )
```

```python
import math

import jax
import jax.numpy as jnp
from jax import lax
from jax.experimental import pallas as pl
from jax.experimental.pallas import tpu as pltpu
from jax.sharding import PartitionSpec as P

MESH = pl.DeviceIdType.MESH

VIEWS_ALL = 336


BACKGROUND = 0.05


def with_halo(value, sides, width):
    for axis, dim in sides:
        size, length = (lax.axis_size(axis), value.shape[dim])
        up = [(i, (i + 1) % size) for i in range(size - 1)]
        down = [(j, i) for i, j in up]
        last = lax.slice_in_dim(value, length - width, length, axis=dim)
        leading = lax.slice_in_dim(value, 0, width, axis=dim)
        before = lax.ppermute(last, axis, up)
        after = lax.ppermute(leading, axis, down)
        value = jnp.concatenate([before, value, after], axis=dim)
    return value


def kernels(angles, bins, length):
    view_angle = math.pi * angles.astype(jnp.float32) / VIEWS_ALL
    step_width = length / bins
    deviation = 0.25 * step_width
    spacing = step_width * (0.75 + 0.25 * jnp.cos(2.0 * view_angle))
    offset = 1.5 * step_width * jnp.sin(view_angle)
    centres = (jnp.arange(bins, dtype=jnp.float32) + 0.5 - bins / 2)[None, :] * spacing[
        :, None
    ] + offset[:, None]
    voxel_pos = jnp.arange(length, dtype=jnp.float32) + 0.5 - length / 2
    distance = voxel_pos[None, None, :] - centres[:, :, None]
    values = jnp.exp(-distance * distance / (2.0 * deviation * deviation)) / (
        deviation * math.sqrt(2.0 * math.pi)
    )
    return values.astype(jnp.bfloat16)


def ring_gather_kernel(payload, out, send_sems, recv_sems):
    count = lax.axis_size("view")
    me = lax.axis_index("view")
    slab = lax.axis_index("slab")
    left = lax.rem(me + count - 1, count)
    right = lax.rem(me + 1, count)
    half = payload.shape[0] // 2
    rest = payload.shape[0] - half

    barrier = pltpu.get_barrier_semaphore()
    for neighbour in (left, right):
        pl.semaphore_signal(barrier, inc=1, device_id=(slab, neighbour), device_id_type=MESH)
    pl.semaphore_wait(barrier, 2)

    to_left = pltpu.make_async_remote_copy(
        src_ref=payload, dst_ref=out.at[1], send_sem=send_sems.at[0], recv_sem=recv_sems.at[1],
        device_id=(slab, left), device_id_type=MESH,
    )
    to_right = pltpu.make_async_remote_copy(
        src_ref=payload, dst_ref=out.at[0], send_sem=send_sems.at[1], recv_sem=recv_sems.at[0],
        device_id=(slab, right), device_id_type=MESH,
    )
    to_left.start()
    to_right.start()
    to_right.wait_recv()
    onward_right = pltpu.make_async_remote_copy(
        src_ref=out.at[0, pl.ds(0, half)], dst_ref=out.at[2, pl.ds(0, half)],
        send_sem=send_sems.at[2], recv_sem=recv_sems.at[2],
        device_id=(slab, right), device_id_type=MESH,
    )
    onward_right.start()
    to_left.wait_recv()
    onward_left = pltpu.make_async_remote_copy(
        src_ref=out.at[1, pl.ds(half, rest)], dst_ref=out.at[2, pl.ds(half, rest)],
        send_sem=send_sems.at[3], recv_sem=recv_sems.at[3],
        device_id=(slab, left), device_id_type=MESH,
    )
    onward_left.start()
    to_left.wait_send()
    to_right.wait_send()
    onward_right.wait_send()
    onward_left.wait_send()
    onward_right.wait_recv()
    onward_left.wait_recv()


def ring_gather(payload):
    return pl.pallas_call(
        ring_gather_kernel,
        out_shape=jax.ShapeDtypeStruct((3,) + payload.shape, payload.dtype),
        in_specs=[pl.BlockSpec(memory_space=pl.ANY)],
        out_specs=pl.BlockSpec(memory_space=pl.ANY),
        scratch_shapes=[pltpu.SemaphoreType.DMA((4,)), pltpu.SemaphoreType.DMA((4,))],
        compiler_params=pltpu.CompilerParams(collective_id=0, has_side_effects=True),
    )(payload)


def exchange_kernel(send, out, local_sem, send_sems, recv_sems):
    count = lax.axis_size("slab")
    me = lax.axis_index("slab")
    view = lax.axis_index("view")

    barrier = pltpu.get_barrier_semaphore()

    def greet(step, carry):
        peer = lax.rem(me + step, count)
        pl.semaphore_signal(barrier, inc=1, device_id=(peer, view), device_id_type=MESH)
        return carry

    lax.fori_loop(1, count, greet, 0)
    pl.semaphore_wait(barrier, count - 1)

    local = pltpu.make_async_copy(send.at[me], out.at[me], local_sem)
    local.start()

    def copy_to(step):
        peer = lax.rem(me + step, count)
        return pltpu.make_async_remote_copy(
            src_ref=send.at[peer], dst_ref=out.at[me],
            send_sem=send_sems.at[step], recv_sem=recv_sems.at[step],
            device_id=(peer, view), device_id_type=MESH,
        )

    def start(step, carry):
        copy_to(step).start()
        return carry

    def finish(step, carry):
        copy = copy_to(step)
        copy.wait_send()
        copy.wait_recv()
        return carry

    lax.fori_loop(1, count, start, 0)
    lax.fori_loop(1, count, finish, 0)
    local.wait()


def exchange(send):
    count = send.shape[0]
    return pl.pallas_call(
        exchange_kernel,
        out_shape=jax.ShapeDtypeStruct(send.shape, send.dtype),
        in_specs=[pl.BlockSpec(memory_space=pl.ANY)],
        out_specs=pl.BlockSpec(memory_space=pl.ANY),
        scratch_shapes=[
            pltpu.SemaphoreType.DMA(()),
            pltpu.SemaphoreType.DMA((count,)),
            pltpu.SemaphoreType.DMA((count,)),
        ],
        compiler_params=pltpu.CompilerParams(collective_id=1, has_side_effects=True),
    )(send)


def split_bf16(value):
    high = value.astype(jnp.bfloat16)
    low = (value - high.astype(jnp.float32)).astype(jnp.bfloat16)
    return high, low


def on_device(
    activity, sensitivity, psf_width, measured, block_slab, block_line, block_angle, subset_views
):
    weight = psf_width[:, None, None]
    padded = with_halo(activity, (("slab", 0),), 1)
    blurred = ((1.0 - 2.0 * weight) * activity + weight * (padded[:-2] + padded[2:])).astype(
        jnp.bfloat16
    )
    planes, lines_here, length = activity.shape
    bins = measured.shape[3]
    row = planes * bins
    tof_kernel = kernels(subset_views[0], bins, length)
    angle_count = tof_kernel.shape[0]
    pairs = angle_count * lines_here
    projected = jnp.einsum("zlv,atv->zalt", blurred, tof_kernel, preferred_element_type=jnp.float32)
    projected = projected.reshape(planes, pairs, bins)

    slab_count = lax.axis_size("slab")
    block_total = measured.shape[1]
    capacity = 2 * block_total // slab_count
    slots = slab_count * capacity
    targets = block_slab[0, :, 0]
    onehot = (targets[:, None] == jnp.arange(slab_count, dtype=jnp.int32)[None, :]).astype(
        jnp.int32
    )
    slot_pos = jnp.sum((jnp.cumsum(onehot, axis=0) - onehot) * onehot, axis=1)
    flat_slot = targets * capacity + slot_pos
    place = (jnp.arange(slots, dtype=jnp.int32)[:, None] == flat_slot[None, :]).astype(
        jnp.bfloat16
    )
    pair_id = block_angle[0] * lines_here + block_line[0]
    extra = 128
    tag = jnp.broadcast_to(pair_id.astype(jnp.bfloat16)[:, None], (block_total, extra))
    outgoing = jnp.concatenate([measured[0].reshape(block_total, row), tag], axis=1)
    send = jnp.dot(place, outgoing, preferred_element_type=jnp.float32).astype(jnp.bfloat16)
    recv = lax.all_to_all(
        send.reshape(slab_count, capacity, row + extra), "slab", 0, 0, tiled=True
    ).reshape(slots, row + extra)
    index = recv[:, row].astype(jnp.int32)
    rows = recv[:, :row].reshape(slots, planes, bins).transpose(1, 0, 2)
    pick = (index[:, None] == jnp.arange(pairs, dtype=jnp.int32)[None, :]).astype(jnp.bfloat16)
    pick = jnp.broadcast_to(pick[None], (planes, slots, pairs))
    estimate = sum(
        jnp.einsum("zjp,zpt->zjt", pick, piece, preferred_element_type=jnp.float32)
        for piece in split_bf16(projected)
    )
    ratios = rows.astype(jnp.float32) / (estimate + BACKGROUND)

    same = index[:, None] == index[None, :]
    earlier = jnp.arange(slots)[None, :] < jnp.arange(slots)[:, None]
    first = ~jnp.any(same & earlier, axis=1)
    merge = jnp.broadcast_to((same & first[:, None]).astype(jnp.bfloat16)[None], (planes, slots, slots))
    merged = sum(
        jnp.einsum("zij,zjt->zit", merge, piece, preferred_element_type=jnp.float32)
        for piece in split_bf16(ratios)
    ).astype(jnp.bfloat16)

    views = subset_views[0]
    info = jnp.zeros((slots, bins), jnp.float32)
    info = info.at[:, 0].set(index.astype(jnp.float32))
    info = info.at[:, 1 : 1 + angle_count].set((views // 16).astype(jnp.float32)[None, :])
    info = info.at[:, 1 + angle_count : 1 + 2 * angle_count].set(
        (views % 16).astype(jnp.float32)[None, :]
    )
    payload = jnp.concatenate([merged, info.astype(jnp.bfloat16)[None]], axis=0)
    def back_project(got, kernel_k):
        index_k = got[planes, :, 0].astype(jnp.int32)
        order = jnp.arange(pairs, dtype=jnp.int32)
        wanted = (order % angle_count) * lines_here + order // angle_count
        scatter = (wanted[:, None] == index_k[None, :]).astype(jnp.bfloat16)
        scatter = jnp.broadcast_to(scatter[None], (planes, pairs, slots))
        dense = jnp.einsum(
            "zpi,zit->zpt", scatter, got[:planes], preferred_element_type=jnp.float32
        ).astype(jnp.bfloat16)
        dense = dense.reshape(planes, lines_here, angle_count, bins)
        return jnp.einsum("zlat,atv->zlv", dense, kernel_k, preferred_element_type=jnp.float32)

    def kernel_of(got):
        tail = got[planes, 0].astype(jnp.int32)
        views_k = tail[1 : 1 + angle_count] * 16 + tail[1 + angle_count : 1 + 2 * angle_count]
        return kernels(views_k, bins, length)

    view_count = lax.axis_size("view")
    rightward = [(i, (i + 1) % view_count) for i in range(view_count)]
    leftward = [(i, (i + view_count - 1) % view_count) for i in range(view_count)]
    half = (planes + 1) // 2
    from_left = lax.ppermute(payload, "view", rightward)
    from_right = lax.ppermute(payload, "view", leftward)
    total = back_project(payload, tof_kernel)
    total, from_left, from_right = lax.optimization_barrier((total, from_left, from_right))
    far_low = lax.ppermute(from_left[:half], "view", rightward)
    far_high = lax.ppermute(from_right[half:], "view", leftward)
    total = total + back_project(from_left, kernel_of(from_left))
    total = total + back_project(from_right, kernel_of(from_right))
    total, far_low, far_high = lax.optimization_barrier((total, far_low, far_high))
    far = jnp.concatenate([far_low, far_high], axis=0)
    total = total + back_project(far, kernel_of(far))
    edges = with_halo(weight * total, (("slab", 0),), 1)
    smoothed = (1.0 - 2.0 * weight) * total + edges[:-2] + edges[2:]
    return activity * smoothed / sensitivity


def solution(mesh):
    in_specs = (
        P("slab", None, None),
        P("slab", None, None),
        P("slab"),
        P("view", "slab", None, None),
        P("view", "slab", None),
        P("view", "slab"),
        P("view", "slab"),
        P("view", None),
    )
    out_specs = P("slab", None, None)
    return jax.shard_map(
        on_device, mesh=mesh, in_specs=in_specs, out_specs=out_specs, check_vma=False
    )
```

```python
import math

import jax
import jax.numpy as jnp
from jax import lax
from jax.experimental import pallas as pl
from jax.experimental.pallas import tpu as pltpu
from jax.sharding import PartitionSpec as P

MESH = pl.DeviceIdType.MESH

VIEWS_ALL = 336


BACKGROUND = 0.05


def with_halo(value, sides, width):
    for axis, dim in sides:
        size, length = (lax.axis_size(axis), value.shape[dim])
        up = [(i, (i + 1) % size) for i in range(size - 1)]
        down = [(j, i) for i, j in up]
        last = lax.slice_in_dim(value, length - width, length, axis=dim)
        leading = lax.slice_in_dim(value, 0, width, axis=dim)
        before = lax.ppermute(last, axis, up)
        after = lax.ppermute(leading, axis, down)
        value = jnp.concatenate([before, value, after], axis=dim)
    return value


def kernels(angles, bins, length):
    view_angle = math.pi * angles.astype(jnp.float32) / VIEWS_ALL
    step_width = length / bins
    deviation = 0.25 * step_width
    spacing = step_width * (0.75 + 0.25 * jnp.cos(2.0 * view_angle))
    offset = 1.5 * step_width * jnp.sin(view_angle)
    centres = (jnp.arange(bins, dtype=jnp.float32) + 0.5 - bins / 2)[None, :] * spacing[
        :, None
    ] + offset[:, None]
    voxel_pos = jnp.arange(length, dtype=jnp.float32) + 0.5 - length / 2
    distance = voxel_pos[None, None, :] - centres[:, :, None]
    values = jnp.exp(-distance * distance / (2.0 * deviation * deviation)) / (
        deviation * math.sqrt(2.0 * math.pi)
    )
    return values.astype(jnp.bfloat16)


def ring_gather_kernel(payload, out, send_sems, recv_sems):
    count = lax.axis_size("view")
    me = lax.axis_index("view")
    slab = lax.axis_index("slab")
    left = lax.rem(me + count - 1, count)
    right = lax.rem(me + 1, count)
    half = payload.shape[0] // 2
    rest = payload.shape[0] - half

    barrier = pltpu.get_barrier_semaphore()
    for neighbour in (left, right):
        pl.semaphore_signal(barrier, inc=1, device_id=(slab, neighbour), device_id_type=MESH)
    pl.semaphore_wait(barrier, 2)

    to_left = pltpu.make_async_remote_copy(
        src_ref=payload, dst_ref=out.at[1], send_sem=send_sems.at[0], recv_sem=recv_sems.at[1],
        device_id=(slab, left), device_id_type=MESH,
    )
    to_right = pltpu.make_async_remote_copy(
        src_ref=payload, dst_ref=out.at[0], send_sem=send_sems.at[1], recv_sem=recv_sems.at[0],
        device_id=(slab, right), device_id_type=MESH,
    )
    to_left.start()
    to_right.start()
    to_right.wait_recv()
    onward_right = pltpu.make_async_remote_copy(
        src_ref=out.at[0, pl.ds(0, half)], dst_ref=out.at[2, pl.ds(0, half)],
        send_sem=send_sems.at[2], recv_sem=recv_sems.at[2],
        device_id=(slab, right), device_id_type=MESH,
    )
    onward_right.start()
    to_left.wait_recv()
    onward_left = pltpu.make_async_remote_copy(
        src_ref=out.at[1, pl.ds(half, rest)], dst_ref=out.at[2, pl.ds(half, rest)],
        send_sem=send_sems.at[3], recv_sem=recv_sems.at[3],
        device_id=(slab, left), device_id_type=MESH,
    )
    onward_left.start()
    to_left.wait_send()
    to_right.wait_send()
    onward_right.wait_send()
    onward_left.wait_send()
    onward_right.wait_recv()
    onward_left.wait_recv()


def ring_gather(payload):
    return pl.pallas_call(
        ring_gather_kernel,
        out_shape=jax.ShapeDtypeStruct((3,) + payload.shape, payload.dtype),
        in_specs=[pl.BlockSpec(memory_space=pl.ANY)],
        out_specs=pl.BlockSpec(memory_space=pl.ANY),
        scratch_shapes=[pltpu.SemaphoreType.DMA((4,)), pltpu.SemaphoreType.DMA((4,))],
        compiler_params=pltpu.CompilerParams(collective_id=0, has_side_effects=True),
    )(payload)


def exchange_kernel(send, out, local_sem, send_sems, recv_sems):
    count = lax.axis_size("slab")
    me = lax.axis_index("slab")
    view = lax.axis_index("view")

    barrier = pltpu.get_barrier_semaphore()

    def greet(step, carry):
        peer = lax.rem(me + step, count)
        pl.semaphore_signal(barrier, inc=1, device_id=(peer, view), device_id_type=MESH)
        return carry

    lax.fori_loop(1, count, greet, 0)
    pl.semaphore_wait(barrier, count - 1)

    local = pltpu.make_async_copy(send.at[me], out.at[me], local_sem)
    local.start()

    def copy_to(step):
        peer = lax.rem(me + step, count)
        return pltpu.make_async_remote_copy(
            src_ref=send.at[peer], dst_ref=out.at[me],
            send_sem=send_sems.at[step], recv_sem=recv_sems.at[step],
            device_id=(peer, view), device_id_type=MESH,
        )

    def start(step, carry):
        copy_to(step).start()
        return carry

    def finish(step, carry):
        copy = copy_to(step)
        copy.wait_send()
        copy.wait_recv()
        return carry

    lax.fori_loop(1, count, start, 0)
    lax.fori_loop(1, count, finish, 0)
    local.wait()


def exchange(send):
    count = send.shape[0]
    return pl.pallas_call(
        exchange_kernel,
        out_shape=jax.ShapeDtypeStruct(send.shape, send.dtype),
        in_specs=[pl.BlockSpec(memory_space=pl.ANY)],
        out_specs=pl.BlockSpec(memory_space=pl.ANY),
        scratch_shapes=[
            pltpu.SemaphoreType.DMA(()),
            pltpu.SemaphoreType.DMA((count,)),
            pltpu.SemaphoreType.DMA((count,)),
        ],
        compiler_params=pltpu.CompilerParams(collective_id=1, has_side_effects=True),
    )(send)


def on_device(
    activity, sensitivity, psf_width, measured, block_slab, block_line, block_angle, subset_views
):
    weight = psf_width[:, None, None]
    padded = with_halo(activity, (("slab", 0),), 1)
    blurred = ((1.0 - 2.0 * weight) * activity + weight * (padded[:-2] + padded[2:])).astype(
        jnp.bfloat16
    )
    planes, lines_here, length = activity.shape
    bins = measured.shape[3]
    row = planes * bins
    tof_kernel = kernels(subset_views[0], bins, length)
    angle_count = tof_kernel.shape[0]
    pairs = angle_count * lines_here
    projected = jnp.einsum("zlv,atv->zalt", blurred, tof_kernel, preferred_element_type=jnp.float32)
    projected = projected.reshape(planes, pairs, bins)

    slab_count = lax.axis_size("slab")
    block_total = measured.shape[1]
    capacity = 2 * block_total // slab_count
    slots = slab_count * capacity
    targets = block_slab[0, :, 0]
    onehot = (targets[:, None] == jnp.arange(slab_count, dtype=jnp.int32)[None, :]).astype(
        jnp.int32
    )
    slot_pos = jnp.sum((jnp.cumsum(onehot, axis=0) - onehot) * onehot, axis=1)
    flat_slot = targets * capacity + slot_pos
    place = (jnp.arange(slots, dtype=jnp.int32)[:, None] == flat_slot[None, :]).astype(
        jnp.bfloat16
    )
    pair_id = block_angle[0] * lines_here + block_line[0]
    extra = 128
    tag = jnp.broadcast_to(pair_id.astype(jnp.bfloat16)[:, None], (block_total, extra))
    outgoing = jnp.concatenate([measured[0].reshape(block_total, row), tag], axis=1)
    send = jnp.dot(place, outgoing, preferred_element_type=jnp.float32).astype(jnp.bfloat16)
    recv = lax.all_to_all(
        send.reshape(slab_count, capacity, row + extra), "slab", 0, 0, tiled=True
    ).reshape(slots, row + extra)
    index = recv[:, row].astype(jnp.int32)
    rows = recv[:, :row].reshape(slots, planes, bins).transpose(1, 0, 2)
    pick = (index[:, None] == jnp.arange(pairs, dtype=jnp.int32)[None, :]).astype(jnp.float32)
    pick = jnp.broadcast_to(pick[None], (planes, slots, pairs))
    estimate = jnp.einsum("zjp,zpt->zjt", pick, projected, precision=lax.Precision.HIGH)
    ratios = rows.astype(jnp.float32) / (estimate + BACKGROUND)

    same = index[:, None] == index[None, :]
    earlier = jnp.arange(slots)[None, :] < jnp.arange(slots)[:, None]
    first = ~jnp.any(same & earlier, axis=1)
    merge = jnp.broadcast_to((same & first[:, None]).astype(jnp.float32)[None], (planes, slots, slots))
    merged = jnp.einsum(
        "zij,zjt->zit", merge, ratios, precision=lax.Precision.HIGH
    ).astype(jnp.bfloat16)

    views = subset_views[0]
    info = jnp.zeros((slots, bins), jnp.float32)
    info = info.at[:, 0].set(index.astype(jnp.float32))
    info = info.at[:, 1 : 1 + angle_count].set((views // 16).astype(jnp.float32)[None, :])
    info = info.at[:, 1 + angle_count : 1 + 2 * angle_count].set(
        (views % 16).astype(jnp.float32)[None, :]
    )
    payload = jnp.concatenate([merged, info.astype(jnp.bfloat16)[None]], axis=0)
    def back_project(got, kernel_k):
        index_k = got[planes, :, 0].astype(jnp.int32)
        order = jnp.arange(pairs, dtype=jnp.int32)
        wanted = (order % angle_count) * lines_here + order // angle_count
        scatter = (wanted[:, None] == index_k[None, :]).astype(jnp.bfloat16)
        scatter = jnp.broadcast_to(scatter[None], (planes, pairs, slots))
        dense = jnp.einsum(
            "zpi,zit->zpt", scatter, got[:planes], preferred_element_type=jnp.float32
        ).astype(jnp.bfloat16)
        dense = dense.reshape(planes, lines_here, angle_count, bins)
        return jnp.einsum("zlat,atv->zlv", dense, kernel_k, preferred_element_type=jnp.float32)

    def kernel_of(got):
        tail = got[planes, 0].astype(jnp.int32)
        views_k = tail[1 : 1 + angle_count] * 16 + tail[1 + angle_count : 1 + 2 * angle_count]
        return kernels(views_k, bins, length)

    view_count = lax.axis_size("view")
    rightward = [(i, (i + 1) % view_count) for i in range(view_count)]
    leftward = [(i, (i + view_count - 1) % view_count) for i in range(view_count)]
    half = (planes + 1) // 2
    from_left = lax.ppermute(payload, "view", rightward)
    from_right = lax.ppermute(payload, "view", leftward)
    payload, activity, sensitivity = lax.optimization_barrier((payload, activity, sensitivity))
    scale = activity / sensitivity
    total = back_project(payload, tof_kernel)
    total, from_left, from_right, scale = lax.optimization_barrier(
        (total, from_left, from_right, scale)
    )
    far_low = lax.ppermute(from_left[:half], "view", rightward)
    far_high = lax.ppermute(from_right[half:], "view", leftward)
    total = total + back_project(from_left, kernel_of(from_left))
    total = total + back_project(from_right, kernel_of(from_right))
    total, far_low, far_high = lax.optimization_barrier((total, far_low, far_high))
    far = jnp.concatenate([far_low, far_high], axis=0)
    total = total + back_project(far, kernel_of(far))
    edges = with_halo(weight * total, (("slab", 0),), 1)
    smoothed = (1.0 - 2.0 * weight) * total + edges[:-2] + edges[2:]
    return smoothed * scale


def solution(mesh):
    in_specs = (
        P("slab", None, None),
        P("slab", None, None),
        P("slab"),
        P("view", "slab", None, None),
        P("view", "slab", None),
        P("view", "slab"),
        P("view", "slab"),
        P("view", None),
    )
    out_specs = P("slab", None, None)
    return jax.shard_map(
        on_device, mesh=mesh, in_specs=in_specs, out_specs=out_specs, check_vma=False
    )
```

```python
import math

import jax
import jax.numpy as jnp
from jax import lax
from jax.experimental import pallas as pl
from jax.experimental.pallas import tpu as pltpu
from jax.sharding import PartitionSpec as P

MESH = pl.DeviceIdType.MESH

VIEWS_ALL = 336


BACKGROUND = 0.05


def with_halo(value, sides, width):
    for axis, dim in sides:
        size, length = (lax.axis_size(axis), value.shape[dim])
        up = [(i, (i + 1) % size) for i in range(size - 1)]
        down = [(j, i) for i, j in up]
        last = lax.slice_in_dim(value, length - width, length, axis=dim)
        leading = lax.slice_in_dim(value, 0, width, axis=dim)
        before = lax.ppermute(last, axis, up)
        after = lax.ppermute(leading, axis, down)
        value = jnp.concatenate([before, value, after], axis=dim)
    return value


def kernels(angles, bins, length):
    view_angle = math.pi * angles.astype(jnp.float32) / VIEWS_ALL
    step_width = length / bins
    deviation = 0.25 * step_width
    spacing = step_width * (0.75 + 0.25 * jnp.cos(2.0 * view_angle))
    offset = 1.5 * step_width * jnp.sin(view_angle)
    centres = (jnp.arange(bins, dtype=jnp.float32) + 0.5 - bins / 2)[None, :] * spacing[
        :, None
    ] + offset[:, None]
    voxel_pos = jnp.arange(length, dtype=jnp.float32) + 0.5 - length / 2
    distance = voxel_pos[None, None, :] - centres[:, :, None]
    values = jnp.exp(-distance * distance / (2.0 * deviation * deviation)) / (
        deviation * math.sqrt(2.0 * math.pi)
    )
    return values.astype(jnp.bfloat16)


def ring_gather_kernel(payload, out, send_sems, recv_sems):
    count = lax.axis_size("view")
    me = lax.axis_index("view")
    slab = lax.axis_index("slab")
    left = lax.rem(me + count - 1, count)
    right = lax.rem(me + 1, count)
    half = payload.shape[0] // 2
    rest = payload.shape[0] - half

    barrier = pltpu.get_barrier_semaphore()
    for neighbour in (left, right):
        pl.semaphore_signal(barrier, inc=1, device_id=(slab, neighbour), device_id_type=MESH)
    pl.semaphore_wait(barrier, 2)

    to_left = pltpu.make_async_remote_copy(
        src_ref=payload, dst_ref=out.at[1], send_sem=send_sems.at[0], recv_sem=recv_sems.at[1],
        device_id=(slab, left), device_id_type=MESH,
    )
    to_right = pltpu.make_async_remote_copy(
        src_ref=payload, dst_ref=out.at[0], send_sem=send_sems.at[1], recv_sem=recv_sems.at[0],
        device_id=(slab, right), device_id_type=MESH,
    )
    to_left.start()
    to_right.start()
    to_right.wait_recv()
    onward_right = pltpu.make_async_remote_copy(
        src_ref=out.at[0, pl.ds(0, half)], dst_ref=out.at[2, pl.ds(0, half)],
        send_sem=send_sems.at[2], recv_sem=recv_sems.at[2],
        device_id=(slab, right), device_id_type=MESH,
    )
    onward_right.start()
    to_left.wait_recv()
    onward_left = pltpu.make_async_remote_copy(
        src_ref=out.at[1, pl.ds(half, rest)], dst_ref=out.at[2, pl.ds(half, rest)],
        send_sem=send_sems.at[3], recv_sem=recv_sems.at[3],
        device_id=(slab, left), device_id_type=MESH,
    )
    onward_left.start()
    to_left.wait_send()
    to_right.wait_send()
    onward_right.wait_send()
    onward_left.wait_send()
    onward_right.wait_recv()
    onward_left.wait_recv()


def ring_gather(payload):
    return pl.pallas_call(
        ring_gather_kernel,
        out_shape=jax.ShapeDtypeStruct((3,) + payload.shape, payload.dtype),
        in_specs=[pl.BlockSpec(memory_space=pl.ANY)],
        out_specs=pl.BlockSpec(memory_space=pl.ANY),
        scratch_shapes=[pltpu.SemaphoreType.DMA((4,)), pltpu.SemaphoreType.DMA((4,))],
        compiler_params=pltpu.CompilerParams(collective_id=0, has_side_effects=True),
    )(payload)


def exchange_kernel(send, out, local_sem, send_sems, recv_sems):
    count = lax.axis_size("slab")
    me = lax.axis_index("slab")
    view = lax.axis_index("view")

    barrier = pltpu.get_barrier_semaphore()

    def greet(step, carry):
        peer = lax.rem(me + step, count)
        pl.semaphore_signal(barrier, inc=1, device_id=(peer, view), device_id_type=MESH)
        return carry

    lax.fori_loop(1, count, greet, 0)
    pl.semaphore_wait(barrier, count - 1)

    local = pltpu.make_async_copy(send.at[me], out.at[me], local_sem)
    local.start()

    def copy_to(step):
        peer = lax.rem(me + step, count)
        return pltpu.make_async_remote_copy(
            src_ref=send.at[peer], dst_ref=out.at[me],
            send_sem=send_sems.at[step], recv_sem=recv_sems.at[step],
            device_id=(peer, view), device_id_type=MESH,
        )

    def start(step, carry):
        copy_to(step).start()
        return carry

    def finish(step, carry):
        copy = copy_to(step)
        copy.wait_send()
        copy.wait_recv()
        return carry

    lax.fori_loop(1, count, start, 0)
    lax.fori_loop(1, count, finish, 0)
    local.wait()


def exchange(send):
    count = send.shape[0]
    return pl.pallas_call(
        exchange_kernel,
        out_shape=jax.ShapeDtypeStruct(send.shape, send.dtype),
        in_specs=[pl.BlockSpec(memory_space=pl.ANY)],
        out_specs=pl.BlockSpec(memory_space=pl.ANY),
        scratch_shapes=[
            pltpu.SemaphoreType.DMA(()),
            pltpu.SemaphoreType.DMA((count,)),
            pltpu.SemaphoreType.DMA((count,)),
        ],
        compiler_params=pltpu.CompilerParams(collective_id=1, has_side_effects=True),
    )(send)


def on_device(
    activity, sensitivity, psf_width, measured, block_slab, block_line, block_angle, subset_views
):
    weight = psf_width[:, None, None]
    views = subset_views[0]
    angle_total = views.shape[0]
    column = jnp.arange(measured.shape[3], dtype=jnp.int32)
    digits = jnp.concatenate([views // 16, views % 16])
    fixed = jnp.zeros(column.shape, jnp.int32).at[1 : 1 + 2 * angle_total].set(digits)
    fixed = fixed.astype(jnp.bfloat16)

    def info_row(index_column):
        return jnp.where(column[None, :] == 0, index_column[:, None], fixed[None, :])

    planes, lines_here, length = activity.shape
    bins = measured.shape[3]
    row = planes * bins
    tof_kernel = kernels(subset_views[0], bins, length)
    angle_count = tof_kernel.shape[0]
    pairs = angle_count * lines_here

    slab_count = lax.axis_size("slab")
    block_total = measured.shape[1]
    capacity = 2 * block_total // slab_count
    slots = slab_count * capacity
    targets = block_slab[0, :, 0]
    onehot = (targets[:, None] == jnp.arange(slab_count, dtype=jnp.int32)[None, :]).astype(
        jnp.int32
    )
    slot_pos = jnp.sum((jnp.cumsum(onehot, axis=0) - onehot) * onehot, axis=1)
    flat_slot = targets * capacity + slot_pos
    place = (jnp.arange(slots, dtype=jnp.int32)[:, None] == flat_slot[None, :]).astype(
        jnp.bfloat16
    )
    pair_id = block_angle[0] * lines_here + block_line[0]
    extra = 128
    tag = jnp.broadcast_to(pair_id.astype(jnp.bfloat16)[:, None], (block_total, extra))
    outgoing = jnp.concatenate([measured[0].reshape(block_total, row), tag], axis=1)
    send = jnp.dot(place, outgoing, preferred_element_type=jnp.float32).astype(jnp.bfloat16)
    send, activity_late = lax.optimization_barrier((send, activity))
    padded = with_halo(activity_late, (("slab", 0),), 1)
    blurred = ((1.0 - 2.0 * weight) * activity + weight * (padded[:-2] + padded[2:])).astype(
        jnp.bfloat16
    )
    projected = jnp.einsum("zlv,atv->zalt", blurred, tof_kernel, preferred_element_type=jnp.float32)
    projected = projected.reshape(planes, pairs, bins)
    recv = lax.all_to_all(
        send.reshape(slab_count, capacity, row + extra), "slab", 0, 0, tiled=True
    ).reshape(slots, row + extra)
    index = recv[:, row].astype(jnp.int32)
    rows = recv[:, :row].reshape(slots, planes, bins).transpose(1, 0, 2)
    pick = (index[:, None] == jnp.arange(pairs, dtype=jnp.int32)[None, :]).astype(jnp.float32)
    pick = jnp.broadcast_to(pick[None], (planes, slots, pairs))
    estimate = jnp.einsum("zjp,zpt->zjt", pick, projected, precision=lax.Precision.HIGH)
    ratios = rows.astype(jnp.float32) / (estimate + BACKGROUND)

    same = index[:, None] == index[None, :]
    earlier = jnp.arange(slots)[None, :] < jnp.arange(slots)[:, None]
    first = ~jnp.any(same & earlier, axis=1)
    merge = jnp.broadcast_to((same & first[:, None]).astype(jnp.float32)[None], (planes, slots, slots))
    merged = jnp.einsum(
        "zij,zjt->zit", merge, ratios, precision=lax.Precision.HIGH
    ).astype(jnp.bfloat16)

    payload = jnp.concatenate([merged, info_row(recv[:, row])[None]], axis=0)
    def back_project(got, kernel_k):
        index_k = got[planes, :, 0].astype(jnp.int32)
        order = jnp.arange(pairs, dtype=jnp.int32)
        wanted = (order % angle_count) * lines_here + order // angle_count
        scatter = (wanted[:, None] == index_k[None, :]).astype(jnp.bfloat16)
        scatter = jnp.broadcast_to(scatter[None], (planes, pairs, slots))
        dense = jnp.einsum(
            "zpi,zit->zpt", scatter, got[:planes], preferred_element_type=jnp.float32
        ).astype(jnp.bfloat16)
        dense = dense.reshape(planes, lines_here, angle_count, bins)
        return jnp.einsum("zlat,atv->zlv", dense, kernel_k, preferred_element_type=jnp.float32)

    def kernel_of(got):
        tail = got[planes, 0].astype(jnp.int32)
        views_k = tail[1 : 1 + angle_count] * 16 + tail[1 + angle_count : 1 + 2 * angle_count]
        return kernels(views_k, bins, length)

    view_count = lax.axis_size("view")
    rightward = [(i, (i + 1) % view_count) for i in range(view_count)]
    leftward = [(i, (i + view_count - 1) % view_count) for i in range(view_count)]
    half = (planes + 1) // 2
    from_left = lax.ppermute(payload, "view", rightward)
    from_right = lax.ppermute(payload, "view", leftward)
    total = back_project(payload, tof_kernel)
    total, from_left, from_right = lax.optimization_barrier((total, from_left, from_right))
    far_low = lax.ppermute(from_left[:half], "view", rightward)
    far_high = lax.ppermute(from_right[half:], "view", leftward)
    total = total + back_project(from_left, kernel_of(from_left))
    total = total + back_project(from_right, kernel_of(from_right))
    total, far_low, far_high = lax.optimization_barrier((total, far_low, far_high))
    far = jnp.concatenate([far_low, far_high], axis=0)
    total = total + back_project(far, kernel_of(far))
    edges = with_halo(weight * total, (("slab", 0),), 1)
    smoothed = (1.0 - 2.0 * weight) * total + edges[:-2] + edges[2:]
    return activity * smoothed / sensitivity


def solution(mesh):
    in_specs = (
        P("slab", None, None),
        P("slab", None, None),
        P("slab"),
        P("view", "slab", None, None),
        P("view", "slab", None),
        P("view", "slab"),
        P("view", "slab"),
        P("view", None),
    )
    out_specs = P("slab", None, None)
    return jax.shard_map(
        on_device, mesh=mesh, in_specs=in_specs, out_specs=out_specs, check_vma=False
    )
```

```python
import math

import jax
import jax.numpy as jnp
from jax import lax
from jax.experimental import pallas as pl
from jax.experimental.pallas import tpu as pltpu
from jax.sharding import PartitionSpec as P

MESH = pl.DeviceIdType.MESH

VIEWS_ALL = 336


BACKGROUND = 0.05


def with_halo(value, sides, width):
    for axis, dim in sides:
        size, length = (lax.axis_size(axis), value.shape[dim])
        up = [(i, (i + 1) % size) for i in range(size - 1)]
        down = [(j, i) for i, j in up]
        last = lax.slice_in_dim(value, length - width, length, axis=dim)
        leading = lax.slice_in_dim(value, 0, width, axis=dim)
        before = lax.ppermute(last, axis, up)
        after = lax.ppermute(leading, axis, down)
        value = jnp.concatenate([before, value, after], axis=dim)
    return value


def kernels(angles, bins, length):
    view_angle = math.pi * angles.astype(jnp.float32) / VIEWS_ALL
    step_width = length / bins
    deviation = 0.25 * step_width
    spacing = step_width * (0.75 + 0.25 * jnp.cos(2.0 * view_angle))
    offset = 1.5 * step_width * jnp.sin(view_angle)
    centres = (jnp.arange(bins, dtype=jnp.float32) + 0.5 - bins / 2)[None, :] * spacing[
        :, None
    ] + offset[:, None]
    voxel_pos = jnp.arange(length, dtype=jnp.float32) + 0.5 - length / 2
    distance = voxel_pos[None, None, :] - centres[:, :, None]
    values = jnp.exp(-distance * distance / (2.0 * deviation * deviation)) / (
        deviation * math.sqrt(2.0 * math.pi)
    )
    return values.astype(jnp.bfloat16)


def ring_gather_kernel(payload, out, send_sems, recv_sems):
    count = lax.axis_size("view")
    me = lax.axis_index("view")
    slab = lax.axis_index("slab")
    left = lax.rem(me + count - 1, count)
    right = lax.rem(me + 1, count)
    half = payload.shape[0] // 2
    rest = payload.shape[0] - half

    barrier = pltpu.get_barrier_semaphore()
    for neighbour in (left, right):
        pl.semaphore_signal(barrier, inc=1, device_id=(slab, neighbour), device_id_type=MESH)
    pl.semaphore_wait(barrier, 2)

    to_left = pltpu.make_async_remote_copy(
        src_ref=payload, dst_ref=out.at[1], send_sem=send_sems.at[0], recv_sem=recv_sems.at[1],
        device_id=(slab, left), device_id_type=MESH,
    )
    to_right = pltpu.make_async_remote_copy(
        src_ref=payload, dst_ref=out.at[0], send_sem=send_sems.at[1], recv_sem=recv_sems.at[0],
        device_id=(slab, right), device_id_type=MESH,
    )
    to_left.start()
    to_right.start()
    to_right.wait_recv()
    onward_right = pltpu.make_async_remote_copy(
        src_ref=out.at[0, pl.ds(0, half)], dst_ref=out.at[2, pl.ds(0, half)],
        send_sem=send_sems.at[2], recv_sem=recv_sems.at[2],
        device_id=(slab, right), device_id_type=MESH,
    )
    onward_right.start()
    to_left.wait_recv()
    onward_left = pltpu.make_async_remote_copy(
        src_ref=out.at[1, pl.ds(half, rest)], dst_ref=out.at[2, pl.ds(half, rest)],
        send_sem=send_sems.at[3], recv_sem=recv_sems.at[3],
        device_id=(slab, left), device_id_type=MESH,
    )
    onward_left.start()
    to_left.wait_send()
    to_right.wait_send()
    onward_right.wait_send()
    onward_left.wait_send()
    onward_right.wait_recv()
    onward_left.wait_recv()


def ring_gather(payload):
    return pl.pallas_call(
        ring_gather_kernel,
        out_shape=jax.ShapeDtypeStruct((3,) + payload.shape, payload.dtype),
        in_specs=[pl.BlockSpec(memory_space=pl.ANY)],
        out_specs=pl.BlockSpec(memory_space=pl.ANY),
        scratch_shapes=[pltpu.SemaphoreType.DMA((4,)), pltpu.SemaphoreType.DMA((4,))],
        compiler_params=pltpu.CompilerParams(collective_id=0, has_side_effects=True),
    )(payload)


def exchange_kernel(send, out, local_sem, send_sems, recv_sems):
    count = lax.axis_size("slab")
    me = lax.axis_index("slab")
    view = lax.axis_index("view")

    barrier = pltpu.get_barrier_semaphore()

    def greet(step, carry):
        peer = lax.rem(me + step, count)
        pl.semaphore_signal(barrier, inc=1, device_id=(peer, view), device_id_type=MESH)
        return carry

    lax.fori_loop(1, count, greet, 0)
    pl.semaphore_wait(barrier, count - 1)

    local = pltpu.make_async_copy(send.at[me], out.at[me], local_sem)
    local.start()

    def copy_to(step):
        peer = lax.rem(me + step, count)
        return pltpu.make_async_remote_copy(
            src_ref=send.at[peer], dst_ref=out.at[me],
            send_sem=send_sems.at[step], recv_sem=recv_sems.at[step],
            device_id=(peer, view), device_id_type=MESH,
        )

    def start(step, carry):
        copy_to(step).start()
        return carry

    def finish(step, carry):
        copy = copy_to(step)
        copy.wait_send()
        copy.wait_recv()
        return carry

    lax.fori_loop(1, count, start, 0)
    lax.fori_loop(1, count, finish, 0)
    local.wait()


def exchange(send):
    count = send.shape[0]
    return pl.pallas_call(
        exchange_kernel,
        out_shape=jax.ShapeDtypeStruct(send.shape, send.dtype),
        in_specs=[pl.BlockSpec(memory_space=pl.ANY)],
        out_specs=pl.BlockSpec(memory_space=pl.ANY),
        scratch_shapes=[
            pltpu.SemaphoreType.DMA(()),
            pltpu.SemaphoreType.DMA((count,)),
            pltpu.SemaphoreType.DMA((count,)),
        ],
        compiler_params=pltpu.CompilerParams(collective_id=1, has_side_effects=True),
    )(send)


def on_device(
    activity, sensitivity, psf_width, measured, block_slab, block_line, block_angle, subset_views
):
    weight = psf_width[:, None, None]
    views = subset_views[0]
    angle_total = views.shape[0]
    column = jnp.arange(measured.shape[3], dtype=jnp.int32)
    digits = jnp.concatenate([views // 16, views % 16])
    fixed = jnp.zeros(column.shape, jnp.int32).at[1 : 1 + 2 * angle_total].set(digits)
    fixed = fixed.astype(jnp.bfloat16)

    def info_row(index_column):
        return jnp.where(column[None, :] == 0, index_column[:, None], fixed[None, :])

    planes, lines_here, length = activity.shape
    bins = measured.shape[3]
    row = planes * bins
    tof_kernel = kernels(subset_views[0], bins, length)
    angle_count = tof_kernel.shape[0]
    pairs = angle_count * lines_here

    slab_count = lax.axis_size("slab")
    block_total = measured.shape[1]
    capacity = 2 * block_total // slab_count
    slots = slab_count * capacity
    targets = block_slab[0, :, 0]
    onehot = (targets[:, None] == jnp.arange(slab_count, dtype=jnp.int32)[None, :]).astype(
        jnp.int32
    )
    slot_pos = jnp.sum((jnp.cumsum(onehot, axis=0) - onehot) * onehot, axis=1)
    flat_slot = targets * capacity + slot_pos
    place = (jnp.arange(slots, dtype=jnp.int32)[:, None] == flat_slot[None, :]).astype(
        jnp.bfloat16
    )
    pair_id = block_angle[0] * lines_here + block_line[0]
    extra = 128
    tag = jnp.broadcast_to(pair_id.astype(jnp.bfloat16)[:, None], (block_total, extra))
    outgoing = jnp.concatenate([measured[0].reshape(block_total, row), tag], axis=1)
    send = jnp.dot(place, outgoing, preferred_element_type=jnp.float32).astype(jnp.bfloat16)
    send, activity_late = lax.optimization_barrier((send, activity))
    padded = with_halo(activity_late, (("slab", 0),), 1)
    blurred = ((1.0 - 2.0 * weight) * activity + weight * (padded[:-2] + padded[2:])).astype(
        jnp.bfloat16
    )
    projected = jnp.einsum("zlv,atv->zalt", blurred, tof_kernel, preferred_element_type=jnp.float32)
    projected = projected.reshape(planes, pairs, bins)
    recv = lax.all_to_all(
        send.reshape(slab_count, capacity, row + extra), "slab", 0, 0, tiled=True
    ).reshape(slots, row + extra)
    index = recv[:, row].astype(jnp.int32)
    rows = recv[:, :row].reshape(slots, planes, bins).transpose(1, 0, 2)
    rows = lax.optimization_barrier(rows)
    pick = (index[:, None] == jnp.arange(pairs, dtype=jnp.int32)[None, :]).astype(jnp.float32)
    pick = jnp.broadcast_to(pick[None], (planes, slots, pairs))
    estimate = jnp.einsum("zjp,zpt->zjt", pick, projected, precision=lax.Precision.HIGH)
    ratios = rows.astype(jnp.float32) / (estimate + BACKGROUND)

    same = index[:, None] == index[None, :]
    earlier = jnp.arange(slots)[None, :] < jnp.arange(slots)[:, None]
    first = ~jnp.any(same & earlier, axis=1)
    merge = jnp.broadcast_to((same & first[:, None]).astype(jnp.float32)[None], (planes, slots, slots))
    merged = jnp.einsum(
        "zij,zjt->zit", merge, ratios, precision=lax.Precision.HIGH
    ).astype(jnp.bfloat16)

    payload = jnp.concatenate([merged, info_row(recv[:, row])[None]], axis=0)
    def back_project(got, kernel_k):
        index_k = got[planes, :, 0].astype(jnp.int32)
        order = jnp.arange(pairs, dtype=jnp.int32)
        wanted = (order % angle_count) * lines_here + order // angle_count
        scatter = (wanted[:, None] == index_k[None, :]).astype(jnp.bfloat16)
        scatter = jnp.broadcast_to(scatter[None], (planes, pairs, slots))
        dense = jnp.einsum(
            "zpi,zit->zpt", scatter, got[:planes], preferred_element_type=jnp.float32
        ).astype(jnp.bfloat16)
        dense = dense.reshape(planes, lines_here, angle_count, bins)
        return jnp.einsum("zlat,atv->zlv", dense, kernel_k, preferred_element_type=jnp.float32)

    def kernel_of(got):
        tail = got[planes, 0].astype(jnp.int32)
        views_k = tail[1 : 1 + angle_count] * 16 + tail[1 + angle_count : 1 + 2 * angle_count]
        return kernels(views_k, bins, length)

    view_count = lax.axis_size("view")
    rightward = [(i, (i + 1) % view_count) for i in range(view_count)]
    leftward = [(i, (i + view_count - 1) % view_count) for i in range(view_count)]
    half = (planes + 1) // 2
    from_left = lax.ppermute(payload, "view", rightward)
    from_right = lax.ppermute(payload, "view", leftward)
    total = back_project(payload, tof_kernel)
    total, from_left, from_right = lax.optimization_barrier((total, from_left, from_right))
    far_low = lax.ppermute(from_left[:half], "view", rightward)
    far_high = lax.ppermute(from_right[half:], "view", leftward)
    total = total + back_project(from_left, kernel_of(from_left))
    total = total + back_project(from_right, kernel_of(from_right))
    total, far_low, far_high = lax.optimization_barrier((total, far_low, far_high))
    far = jnp.concatenate([far_low, far_high], axis=0)
    total = total + back_project(far, kernel_of(far))
    edges = with_halo(weight * total, (("slab", 0),), 1)
    smoothed = (1.0 - 2.0 * weight) * total + edges[:-2] + edges[2:]
    return activity * smoothed / sensitivity


def solution(mesh):
    in_specs = (
        P("slab", None, None),
        P("slab", None, None),
        P("slab"),
        P("view", "slab", None, None),
        P("view", "slab", None),
        P("view", "slab"),
        P("view", "slab"),
        P("view", None),
    )
    out_specs = P("slab", None, None)
    return jax.shard_map(
        on_device, mesh=mesh, in_specs=in_specs, out_specs=out_specs, check_vma=False
    )
```

```python
import math

import jax
import jax.numpy as jnp
from jax import lax
from jax.experimental import pallas as pl
from jax.experimental.pallas import tpu as pltpu
from jax.sharding import PartitionSpec as P

MESH = pl.DeviceIdType.MESH

VIEWS_ALL = 336


BACKGROUND = 0.05


def with_halo(value, sides, width):
    for axis, dim in sides:
        size, length = (lax.axis_size(axis), value.shape[dim])
        up = [(i, (i + 1) % size) for i in range(size - 1)]
        down = [(j, i) for i, j in up]
        last = lax.slice_in_dim(value, length - width, length, axis=dim)
        leading = lax.slice_in_dim(value, 0, width, axis=dim)
        before = lax.ppermute(last, axis, up)
        after = lax.ppermute(leading, axis, down)
        value = jnp.concatenate([before, value, after], axis=dim)
    return value


def kernels(angles, bins, length):
    view_angle = math.pi * angles.astype(jnp.float32) / VIEWS_ALL
    step_width = length / bins
    deviation = 0.25 * step_width
    spacing = step_width * (0.75 + 0.25 * jnp.cos(2.0 * view_angle))
    offset = 1.5 * step_width * jnp.sin(view_angle)
    centres = (jnp.arange(bins, dtype=jnp.float32) + 0.5 - bins / 2)[None, :] * spacing[
        :, None
    ] + offset[:, None]
    voxel_pos = jnp.arange(length, dtype=jnp.float32) + 0.5 - length / 2
    distance = voxel_pos[None, None, :] - centres[:, :, None]
    values = jnp.exp(-distance * distance / (2.0 * deviation * deviation)) / (
        deviation * math.sqrt(2.0 * math.pi)
    )
    return values.astype(jnp.bfloat16)


def ring_gather_kernel(payload, out, send_sems, recv_sems):
    count = lax.axis_size("view")
    me = lax.axis_index("view")
    slab = lax.axis_index("slab")
    left = lax.rem(me + count - 1, count)
    right = lax.rem(me + 1, count)
    half = payload.shape[0] // 2
    rest = payload.shape[0] - half

    barrier = pltpu.get_barrier_semaphore()
    for neighbour in (left, right):
        pl.semaphore_signal(barrier, inc=1, device_id=(slab, neighbour), device_id_type=MESH)
    pl.semaphore_wait(barrier, 2)

    to_left = pltpu.make_async_remote_copy(
        src_ref=payload, dst_ref=out.at[1], send_sem=send_sems.at[0], recv_sem=recv_sems.at[1],
        device_id=(slab, left), device_id_type=MESH,
    )
    to_right = pltpu.make_async_remote_copy(
        src_ref=payload, dst_ref=out.at[0], send_sem=send_sems.at[1], recv_sem=recv_sems.at[0],
        device_id=(slab, right), device_id_type=MESH,
    )
    to_left.start()
    to_right.start()
    to_right.wait_recv()
    onward_right = pltpu.make_async_remote_copy(
        src_ref=out.at[0, pl.ds(0, half)], dst_ref=out.at[2, pl.ds(0, half)],
        send_sem=send_sems.at[2], recv_sem=recv_sems.at[2],
        device_id=(slab, right), device_id_type=MESH,
    )
    onward_right.start()
    to_left.wait_recv()
    onward_left = pltpu.make_async_remote_copy(
        src_ref=out.at[1, pl.ds(half, rest)], dst_ref=out.at[2, pl.ds(half, rest)],
        send_sem=send_sems.at[3], recv_sem=recv_sems.at[3],
        device_id=(slab, left), device_id_type=MESH,
    )
    onward_left.start()
    to_left.wait_send()
    to_right.wait_send()
    onward_right.wait_send()
    onward_left.wait_send()
    onward_right.wait_recv()
    onward_left.wait_recv()


def ring_gather(payload):
    return pl.pallas_call(
        ring_gather_kernel,
        out_shape=jax.ShapeDtypeStruct((3,) + payload.shape, payload.dtype),
        in_specs=[pl.BlockSpec(memory_space=pl.ANY)],
        out_specs=pl.BlockSpec(memory_space=pl.ANY),
        scratch_shapes=[pltpu.SemaphoreType.DMA((4,)), pltpu.SemaphoreType.DMA((4,))],
        compiler_params=pltpu.CompilerParams(collective_id=0, has_side_effects=True),
    )(payload)


def exchange_kernel(send, out, local_sem, send_sems, recv_sems):
    count = lax.axis_size("slab")
    me = lax.axis_index("slab")
    view = lax.axis_index("view")

    barrier = pltpu.get_barrier_semaphore()

    def greet(step, carry):
        peer = lax.rem(me + step, count)
        pl.semaphore_signal(barrier, inc=1, device_id=(peer, view), device_id_type=MESH)
        return carry

    lax.fori_loop(1, count, greet, 0)
    pl.semaphore_wait(barrier, count - 1)

    local = pltpu.make_async_copy(send.at[me], out.at[me], local_sem)
    local.start()

    def copy_to(step):
        peer = lax.rem(me + step, count)
        return pltpu.make_async_remote_copy(
            src_ref=send.at[peer], dst_ref=out.at[me],
            send_sem=send_sems.at[step], recv_sem=recv_sems.at[step],
            device_id=(peer, view), device_id_type=MESH,
        )

    def start(step, carry):
        copy_to(step).start()
        return carry

    def finish(step, carry):
        copy = copy_to(step)
        copy.wait_send()
        copy.wait_recv()
        return carry

    lax.fori_loop(1, count, start, 0)
    lax.fori_loop(1, count, finish, 0)
    local.wait()


def exchange(send):
    count = send.shape[0]
    return pl.pallas_call(
        exchange_kernel,
        out_shape=jax.ShapeDtypeStruct(send.shape, send.dtype),
        in_specs=[pl.BlockSpec(memory_space=pl.ANY)],
        out_specs=pl.BlockSpec(memory_space=pl.ANY),
        scratch_shapes=[
            pltpu.SemaphoreType.DMA(()),
            pltpu.SemaphoreType.DMA((count,)),
            pltpu.SemaphoreType.DMA((count,)),
        ],
        compiler_params=pltpu.CompilerParams(collective_id=1, has_side_effects=True),
    )(send)


def on_device(
    activity, sensitivity, psf_width, measured, block_slab, block_line, block_angle, subset_views
):
    weight = psf_width[:, None, None]
    views = subset_views[0]
    angle_total = views.shape[0]
    column = jnp.arange(measured.shape[3], dtype=jnp.int32)
    digits = jnp.concatenate([views // 16, views % 16])
    fixed = jnp.zeros(column.shape, jnp.int32).at[1 : 1 + 2 * angle_total].set(digits)
    fixed = fixed.astype(jnp.bfloat16)

    def info_row(index_column):
        return jnp.where(column[None, :] == 0, index_column[:, None], fixed[None, :])

    planes, lines_here, length = activity.shape
    bins = measured.shape[3]
    row = planes * bins
    tof_kernel = kernels(subset_views[0], bins, length)
    angle_count = tof_kernel.shape[0]
    pairs = angle_count * lines_here

    slab_count = lax.axis_size("slab")
    block_total = measured.shape[1]
    capacity = 2 * block_total // slab_count
    slots = slab_count * capacity
    targets = block_slab[0, :, 0]
    onehot = (targets[:, None] == jnp.arange(slab_count, dtype=jnp.int32)[None, :]).astype(
        jnp.int32
    )
    slot_pos = jnp.sum((jnp.cumsum(onehot, axis=0) - onehot) * onehot, axis=1)
    flat_slot = targets * capacity + slot_pos
    place = (jnp.arange(slots, dtype=jnp.int32)[:, None] == flat_slot[None, :]).astype(
        jnp.bfloat16
    )
    pair_id = block_angle[0] * lines_here + block_line[0]
    extra = 128
    tag = jnp.broadcast_to(pair_id.astype(jnp.bfloat16)[:, None], (block_total, extra))
    outgoing = jnp.concatenate([measured[0].reshape(block_total, row), tag], axis=1)
    send = jnp.dot(place, outgoing, preferred_element_type=jnp.float32).astype(jnp.bfloat16)
    send, activity_late = lax.optimization_barrier((send, activity))
    padded = with_halo(activity_late, (("slab", 0),), 1)
    blurred = ((1.0 - 2.0 * weight) * activity + weight * (padded[:-2] + padded[2:])).astype(
        jnp.bfloat16
    )
    projected = jnp.einsum("zlv,atv->zalt", blurred, tof_kernel, preferred_element_type=jnp.float32)
    projected = projected.reshape(planes, pairs, bins)
    recv = lax.all_to_all(
        send.reshape(slab_count, capacity, row + extra), "slab", 0, 0, tiled=True
    ).reshape(slots, row + extra)
    index = recv[:, row].astype(jnp.int32)
    rows = recv[:, :row].reshape(slots, planes, bins).transpose(1, 0, 2)
    rows = lax.optimization_barrier(rows)
    pick = (index[:, None] == jnp.arange(pairs, dtype=jnp.int32)[None, :]).astype(jnp.float32)
    pick = jnp.broadcast_to(pick[None], (planes, slots, pairs))
    high = lax.reduce_precision(projected, exponent_bits=8, mantissa_bits=7)
    parts = (high.astype(jnp.bfloat16), (projected - high).astype(jnp.bfloat16))
    estimate = sum(
        jnp.einsum("zjp,zpt->zjt", pick.astype(jnp.bfloat16), piece,
                   preferred_element_type=jnp.float32)
        for piece in parts
    )
    ratios = rows.astype(jnp.float32) / (estimate + BACKGROUND)

    same = index[:, None] == index[None, :]
    earlier = jnp.arange(slots)[None, :] < jnp.arange(slots)[:, None]
    first = ~jnp.any(same & earlier, axis=1)
    merge = jnp.broadcast_to((same & first[:, None]).astype(jnp.float32)[None], (planes, slots, slots))
    merged = jnp.einsum(
        "zij,zjt->zit", merge, ratios, precision=lax.Precision.HIGH
    ).astype(jnp.bfloat16)

    payload = jnp.concatenate([merged, info_row(recv[:, row])[None]], axis=0)
    def back_project(got, kernel_k):
        index_k = got[planes, :, 0].astype(jnp.int32)
        order = jnp.arange(pairs, dtype=jnp.int32)
        wanted = (order % angle_count) * lines_here + order // angle_count
        scatter = (wanted[:, None] == index_k[None, :]).astype(jnp.bfloat16)
        scatter = jnp.broadcast_to(scatter[None], (planes, pairs, slots))
        dense = jnp.einsum(
            "zpi,zit->zpt", scatter, got[:planes], preferred_element_type=jnp.float32
        ).astype(jnp.bfloat16)
        dense = dense.reshape(planes, lines_here, angle_count, bins)
        return jnp.einsum("zlat,atv->zlv", dense, kernel_k, preferred_element_type=jnp.float32)

    def kernel_of(got):
        tail = got[planes, 0].astype(jnp.int32)
        views_k = tail[1 : 1 + angle_count] * 16 + tail[1 + angle_count : 1 + 2 * angle_count]
        return kernels(views_k, bins, length)

    view_count = lax.axis_size("view")
    rightward = [(i, (i + 1) % view_count) for i in range(view_count)]
    leftward = [(i, (i + view_count - 1) % view_count) for i in range(view_count)]
    half = (planes + 1) // 2
    from_left = lax.ppermute(payload, "view", rightward)
    from_right = lax.ppermute(payload, "view", leftward)
    total = back_project(payload, tof_kernel)
    total, from_left, from_right = lax.optimization_barrier((total, from_left, from_right))
    far_low = lax.ppermute(from_left[:half], "view", rightward)
    far_high = lax.ppermute(from_right[half:], "view", leftward)
    total = total + back_project(from_left, kernel_of(from_left))
    total = total + back_project(from_right, kernel_of(from_right))
    total, far_low, far_high = lax.optimization_barrier((total, far_low, far_high))
    far = jnp.concatenate([far_low, far_high], axis=0)
    total = total + back_project(far, kernel_of(far))
    edges = with_halo(weight * total, (("slab", 0),), 1)
    smoothed = (1.0 - 2.0 * weight) * total + edges[:-2] + edges[2:]
    return activity * smoothed / sensitivity


def solution(mesh):
    in_specs = (
        P("slab", None, None),
        P("slab", None, None),
        P("slab"),
        P("view", "slab", None, None),
        P("view", "slab", None),
        P("view", "slab"),
        P("view", "slab"),
        P("view", None),
    )
    out_specs = P("slab", None, None)
    return jax.shard_map(
        on_device, mesh=mesh, in_specs=in_specs, out_specs=out_specs, check_vma=False
    )
```

```python
import math

import jax
import jax.numpy as jnp
from jax import lax
from jax.experimental import pallas as pl
from jax.experimental.pallas import tpu as pltpu
from jax.sharding import PartitionSpec as P

MESH = pl.DeviceIdType.MESH

VIEWS_ALL = 336


BACKGROUND = 0.05


def with_halo(value, sides, width):
    for axis, dim in sides:
        size, length = (lax.axis_size(axis), value.shape[dim])
        up = [(i, (i + 1) % size) for i in range(size - 1)]
        down = [(j, i) for i, j in up]
        last = lax.slice_in_dim(value, length - width, length, axis=dim)
        leading = lax.slice_in_dim(value, 0, width, axis=dim)
        before = lax.ppermute(last, axis, up)
        after = lax.ppermute(leading, axis, down)
        value = jnp.concatenate([before, value, after], axis=dim)
    return value


def kernels(angles, bins, length):
    view_angle = math.pi * angles.astype(jnp.float32) / VIEWS_ALL
    step_width = length / bins
    deviation = 0.25 * step_width
    spacing = step_width * (0.75 + 0.25 * jnp.cos(2.0 * view_angle))
    offset = 1.5 * step_width * jnp.sin(view_angle)
    centres = (jnp.arange(bins, dtype=jnp.float32) + 0.5 - bins / 2)[None, :] * spacing[
        :, None
    ] + offset[:, None]
    voxel_pos = jnp.arange(length, dtype=jnp.float32) + 0.5 - length / 2
    distance = voxel_pos[None, None, :] - centres[:, :, None]
    values = jnp.exp(-distance * distance / (2.0 * deviation * deviation)) / (
        deviation * math.sqrt(2.0 * math.pi)
    )
    return values.astype(jnp.bfloat16)


def ring_gather_kernel(payload, out, send_sems, recv_sems):
    count = lax.axis_size("view")
    me = lax.axis_index("view")
    slab = lax.axis_index("slab")
    left = lax.rem(me + count - 1, count)
    right = lax.rem(me + 1, count)
    half = payload.shape[0] // 2
    rest = payload.shape[0] - half

    barrier = pltpu.get_barrier_semaphore()
    for neighbour in (left, right):
        pl.semaphore_signal(barrier, inc=1, device_id=(slab, neighbour), device_id_type=MESH)
    pl.semaphore_wait(barrier, 2)

    to_left = pltpu.make_async_remote_copy(
        src_ref=payload, dst_ref=out.at[1], send_sem=send_sems.at[0], recv_sem=recv_sems.at[1],
        device_id=(slab, left), device_id_type=MESH,
    )
    to_right = pltpu.make_async_remote_copy(
        src_ref=payload, dst_ref=out.at[0], send_sem=send_sems.at[1], recv_sem=recv_sems.at[0],
        device_id=(slab, right), device_id_type=MESH,
    )
    to_left.start()
    to_right.start()
    to_right.wait_recv()
    onward_right = pltpu.make_async_remote_copy(
        src_ref=out.at[0, pl.ds(0, half)], dst_ref=out.at[2, pl.ds(0, half)],
        send_sem=send_sems.at[2], recv_sem=recv_sems.at[2],
        device_id=(slab, right), device_id_type=MESH,
    )
    onward_right.start()
    to_left.wait_recv()
    onward_left = pltpu.make_async_remote_copy(
        src_ref=out.at[1, pl.ds(half, rest)], dst_ref=out.at[2, pl.ds(half, rest)],
        send_sem=send_sems.at[3], recv_sem=recv_sems.at[3],
        device_id=(slab, left), device_id_type=MESH,
    )
    onward_left.start()
    to_left.wait_send()
    to_right.wait_send()
    onward_right.wait_send()
    onward_left.wait_send()
    onward_right.wait_recv()
    onward_left.wait_recv()


def ring_gather(payload):
    return pl.pallas_call(
        ring_gather_kernel,
        out_shape=jax.ShapeDtypeStruct((3,) + payload.shape, payload.dtype),
        in_specs=[pl.BlockSpec(memory_space=pl.ANY)],
        out_specs=pl.BlockSpec(memory_space=pl.ANY),
        scratch_shapes=[pltpu.SemaphoreType.DMA((4,)), pltpu.SemaphoreType.DMA((4,))],
        compiler_params=pltpu.CompilerParams(collective_id=0, has_side_effects=True),
    )(payload)


def exchange_kernel(send, out, local_sem, send_sems, recv_sems):
    count = lax.axis_size("slab")
    me = lax.axis_index("slab")
    view = lax.axis_index("view")

    barrier = pltpu.get_barrier_semaphore()

    def greet(step, carry):
        peer = lax.rem(me + step, count)
        pl.semaphore_signal(barrier, inc=1, device_id=(peer, view), device_id_type=MESH)
        return carry

    lax.fori_loop(1, count, greet, 0)
    pl.semaphore_wait(barrier, count - 1)

    local = pltpu.make_async_copy(send.at[me], out.at[me], local_sem)
    local.start()

    def copy_to(step):
        peer = lax.rem(me + step, count)
        return pltpu.make_async_remote_copy(
            src_ref=send.at[peer], dst_ref=out.at[me],
            send_sem=send_sems.at[step], recv_sem=recv_sems.at[step],
            device_id=(peer, view), device_id_type=MESH,
        )

    def start(step, carry):
        copy_to(step).start()
        return carry

    def finish(step, carry):
        copy = copy_to(step)
        copy.wait_send()
        copy.wait_recv()
        return carry

    lax.fori_loop(1, count, start, 0)
    lax.fori_loop(1, count, finish, 0)
    local.wait()


def exchange(send):
    count = send.shape[0]
    return pl.pallas_call(
        exchange_kernel,
        out_shape=jax.ShapeDtypeStruct(send.shape, send.dtype),
        in_specs=[pl.BlockSpec(memory_space=pl.ANY)],
        out_specs=pl.BlockSpec(memory_space=pl.ANY),
        scratch_shapes=[
            pltpu.SemaphoreType.DMA(()),
            pltpu.SemaphoreType.DMA((count,)),
            pltpu.SemaphoreType.DMA((count,)),
        ],
        compiler_params=pltpu.CompilerParams(collective_id=1, has_side_effects=True),
    )(send)


def on_device(
    activity, sensitivity, psf_width, measured, block_slab, block_line, block_angle, subset_views
):
    weight = psf_width[:, None, None]
    views = subset_views[0]
    angle_total = views.shape[0]
    column = jnp.arange(measured.shape[3], dtype=jnp.int32)
    digits = jnp.concatenate([views // 16, views % 16])
    fixed = jnp.zeros(column.shape, jnp.int32).at[1 : 1 + 2 * angle_total].set(digits)
    fixed = fixed.astype(jnp.bfloat16)

    def info_row(index_column):
        return jnp.where(column[None, :] == 0, index_column[:, None], fixed[None, :])

    planes, lines_here, length = activity.shape
    bins = measured.shape[3]
    row = planes * bins
    tof_kernel = kernels(subset_views[0], bins, length)
    angle_count = tof_kernel.shape[0]
    pairs = angle_count * lines_here

    slab_count = lax.axis_size("slab")
    block_total = measured.shape[1]
    capacity = 2 * block_total // slab_count
    slots = slab_count * capacity
    targets = block_slab[0, :, 0]
    onehot = (targets[:, None] == jnp.arange(slab_count, dtype=jnp.int32)[None, :]).astype(
        jnp.int32
    )
    slot_pos = jnp.sum((jnp.cumsum(onehot, axis=0) - onehot) * onehot, axis=1)
    flat_slot = targets * capacity + slot_pos
    place = (jnp.arange(slots, dtype=jnp.int32)[:, None] == flat_slot[None, :]).astype(
        jnp.bfloat16
    )
    pair_id = block_angle[0] * lines_here + block_line[0]
    extra = 128
    tag = jnp.broadcast_to(pair_id.astype(jnp.bfloat16)[:, None], (block_total, extra))
    outgoing = jnp.concatenate([measured[0].reshape(block_total, row), tag], axis=1)
    send = jnp.dot(place, outgoing, preferred_element_type=jnp.float32).astype(jnp.bfloat16)
    send, activity_late = lax.optimization_barrier((send, activity))
    padded = with_halo(activity_late, (("slab", 0),), 1)
    blurred = ((1.0 - 2.0 * weight) * activity + weight * (padded[:-2] + padded[2:])).astype(
        jnp.bfloat16
    )
    projected = jnp.einsum("zlv,atv->zalt", blurred, tof_kernel, preferred_element_type=jnp.float32)
    projected = projected.reshape(planes, pairs, bins)
    recv = lax.all_to_all(
        send.reshape(slab_count, capacity, row + extra), "slab", 0, 0, tiled=True
    ).reshape(slots, row + extra)
    index = recv[:, row].astype(jnp.int32)
    rows = recv[:, :row].reshape(slots, planes, bins)
    by_pair = projected.transpose(1, 0, 2)
    estimate = by_pair[index]
    ratios = (rows.astype(jnp.float32) / (estimate + BACKGROUND)).reshape(slots, row)

    same = index[:, None] == index[None, :]
    earlier = jnp.arange(slots)[None, :] < jnp.arange(slots)[:, None]
    first = ~jnp.any(same & earlier, axis=1)
    merge = (same & first[:, None]).astype(jnp.float32)
    merged = jnp.dot(merge, ratios, precision=lax.Precision.HIGH).astype(jnp.bfloat16)
    merged = merged.reshape(slots, planes, bins).transpose(1, 0, 2)

    payload = jnp.concatenate([merged, info_row(recv[:, row])[None]], axis=0)
    def back_project(got, kernel_k):
        index_k = got[planes, :, 0].astype(jnp.int32)
        order = jnp.arange(pairs, dtype=jnp.int32)
        wanted = (order % angle_count) * lines_here + order // angle_count
        scatter = (wanted[:, None] == index_k[None, :]).astype(jnp.bfloat16)
        scatter = jnp.broadcast_to(scatter[None], (planes, pairs, slots))
        dense = jnp.einsum(
            "zpi,zit->zpt", scatter, got[:planes], preferred_element_type=jnp.float32
        ).astype(jnp.bfloat16)
        dense = dense.reshape(planes, lines_here, angle_count, bins)
        return jnp.einsum("zlat,atv->zlv", dense, kernel_k, preferred_element_type=jnp.float32)

    def kernel_of(got):
        tail = got[planes, 0].astype(jnp.int32)
        views_k = tail[1 : 1 + angle_count] * 16 + tail[1 + angle_count : 1 + 2 * angle_count]
        return kernels(views_k, bins, length)

    view_count = lax.axis_size("view")
    rightward = [(i, (i + 1) % view_count) for i in range(view_count)]
    leftward = [(i, (i + view_count - 1) % view_count) for i in range(view_count)]
    half = (planes + 1) // 2
    from_left = lax.ppermute(payload, "view", rightward)
    from_right = lax.ppermute(payload, "view", leftward)
    total = back_project(payload, tof_kernel)
    total, from_left, from_right = lax.optimization_barrier((total, from_left, from_right))
    far_low = lax.ppermute(from_left[:half], "view", rightward)
    far_high = lax.ppermute(from_right[half:], "view", leftward)
    total = total + back_project(from_left, kernel_of(from_left))
    total = total + back_project(from_right, kernel_of(from_right))
    total, far_low, far_high = lax.optimization_barrier((total, far_low, far_high))
    far = jnp.concatenate([far_low, far_high], axis=0)
    total = total + back_project(far, kernel_of(far))
    edges = with_halo(weight * total, (("slab", 0),), 1)
    smoothed = (1.0 - 2.0 * weight) * total + edges[:-2] + edges[2:]
    return activity * smoothed / sensitivity


def solution(mesh):
    in_specs = (
        P("slab", None, None),
        P("slab", None, None),
        P("slab"),
        P("view", "slab", None, None),
        P("view", "slab", None),
        P("view", "slab"),
        P("view", "slab"),
        P("view", None),
    )
    out_specs = P("slab", None, None)
    return jax.shard_map(
        on_device, mesh=mesh, in_specs=in_specs, out_specs=out_specs, check_vma=False
    )
```

```python
import math

import jax
import jax.numpy as jnp
from jax import lax
from jax.experimental import pallas as pl
from jax.experimental.pallas import tpu as pltpu
from jax.sharding import PartitionSpec as P

MESH = pl.DeviceIdType.MESH

VIEWS_ALL = 336


BACKGROUND = 0.05


def with_halo(value, sides, width):
    for axis, dim in sides:
        size, length = (lax.axis_size(axis), value.shape[dim])
        up = [(i, (i + 1) % size) for i in range(size - 1)]
        down = [(j, i) for i, j in up]
        last = lax.slice_in_dim(value, length - width, length, axis=dim)
        leading = lax.slice_in_dim(value, 0, width, axis=dim)
        before = lax.ppermute(last, axis, up)
        after = lax.ppermute(leading, axis, down)
        value = jnp.concatenate([before, value, after], axis=dim)
    return value


def kernels(angles, bins, length):
    view_angle = math.pi * angles.astype(jnp.float32) / VIEWS_ALL
    step_width = length / bins
    deviation = 0.25 * step_width
    spacing = step_width * (0.75 + 0.25 * jnp.cos(2.0 * view_angle))
    offset = 1.5 * step_width * jnp.sin(view_angle)
    centres = (jnp.arange(bins, dtype=jnp.float32) + 0.5 - bins / 2)[None, :] * spacing[
        :, None
    ] + offset[:, None]
    voxel_pos = jnp.arange(length, dtype=jnp.float32) + 0.5 - length / 2
    distance = voxel_pos[None, None, :] - centres[:, :, None]
    values = jnp.exp(-distance * distance / (2.0 * deviation * deviation)) / (
        deviation * math.sqrt(2.0 * math.pi)
    )
    return values.astype(jnp.bfloat16)


def ring_gather_kernel(payload, out, send_sems, recv_sems):
    count = lax.axis_size("view")
    me = lax.axis_index("view")
    slab = lax.axis_index("slab")
    left = lax.rem(me + count - 1, count)
    right = lax.rem(me + 1, count)
    half = payload.shape[0] // 2
    rest = payload.shape[0] - half

    barrier = pltpu.get_barrier_semaphore()
    for neighbour in (left, right):
        pl.semaphore_signal(barrier, inc=1, device_id=(slab, neighbour), device_id_type=MESH)
    pl.semaphore_wait(barrier, 2)

    to_left = pltpu.make_async_remote_copy(
        src_ref=payload, dst_ref=out.at[1], send_sem=send_sems.at[0], recv_sem=recv_sems.at[1],
        device_id=(slab, left), device_id_type=MESH,
    )
    to_right = pltpu.make_async_remote_copy(
        src_ref=payload, dst_ref=out.at[0], send_sem=send_sems.at[1], recv_sem=recv_sems.at[0],
        device_id=(slab, right), device_id_type=MESH,
    )
    to_left.start()
    to_right.start()
    to_right.wait_recv()
    onward_right = pltpu.make_async_remote_copy(
        src_ref=out.at[0, pl.ds(0, half)], dst_ref=out.at[2, pl.ds(0, half)],
        send_sem=send_sems.at[2], recv_sem=recv_sems.at[2],
        device_id=(slab, right), device_id_type=MESH,
    )
    onward_right.start()
    to_left.wait_recv()
    onward_left = pltpu.make_async_remote_copy(
        src_ref=out.at[1, pl.ds(half, rest)], dst_ref=out.at[2, pl.ds(half, rest)],
        send_sem=send_sems.at[3], recv_sem=recv_sems.at[3],
        device_id=(slab, left), device_id_type=MESH,
    )
    onward_left.start()
    to_left.wait_send()
    to_right.wait_send()
    onward_right.wait_send()
    onward_left.wait_send()
    onward_right.wait_recv()
    onward_left.wait_recv()


def ring_gather(payload):
    return pl.pallas_call(
        ring_gather_kernel,
        out_shape=jax.ShapeDtypeStruct((3,) + payload.shape, payload.dtype),
        in_specs=[pl.BlockSpec(memory_space=pl.ANY)],
        out_specs=pl.BlockSpec(memory_space=pl.ANY),
        scratch_shapes=[pltpu.SemaphoreType.DMA((4,)), pltpu.SemaphoreType.DMA((4,))],
        compiler_params=pltpu.CompilerParams(collective_id=0, has_side_effects=True),
    )(payload)


def exchange_kernel(send, out, local_sem, send_sems, recv_sems):
    count = lax.axis_size("slab")
    me = lax.axis_index("slab")
    view = lax.axis_index("view")

    barrier = pltpu.get_barrier_semaphore()

    def greet(step, carry):
        peer = lax.rem(me + step, count)
        pl.semaphore_signal(barrier, inc=1, device_id=(peer, view), device_id_type=MESH)
        return carry

    lax.fori_loop(1, count, greet, 0)
    pl.semaphore_wait(barrier, count - 1)

    local = pltpu.make_async_copy(send.at[me], out.at[me], local_sem)
    local.start()

    def copy_to(step):
        peer = lax.rem(me + step, count)
        return pltpu.make_async_remote_copy(
            src_ref=send.at[peer], dst_ref=out.at[me],
            send_sem=send_sems.at[step], recv_sem=recv_sems.at[step],
            device_id=(peer, view), device_id_type=MESH,
        )

    def start(step, carry):
        copy_to(step).start()
        return carry

    def finish(step, carry):
        copy = copy_to(step)
        copy.wait_send()
        copy.wait_recv()
        return carry

    lax.fori_loop(1, count, start, 0)
    lax.fori_loop(1, count, finish, 0)
    local.wait()


def exchange(send):
    count = send.shape[0]
    return pl.pallas_call(
        exchange_kernel,
        out_shape=jax.ShapeDtypeStruct(send.shape, send.dtype),
        in_specs=[pl.BlockSpec(memory_space=pl.ANY)],
        out_specs=pl.BlockSpec(memory_space=pl.ANY),
        scratch_shapes=[
            pltpu.SemaphoreType.DMA(()),
            pltpu.SemaphoreType.DMA((count,)),
            pltpu.SemaphoreType.DMA((count,)),
        ],
        compiler_params=pltpu.CompilerParams(collective_id=1, has_side_effects=True),
    )(send)


def on_device(
    activity, sensitivity, psf_width, measured, block_slab, block_line, block_angle, subset_views
):
    weight = psf_width[:, None, None]
    views = subset_views[0]
    angle_total = views.shape[0]
    column = jnp.arange(measured.shape[3], dtype=jnp.int32)
    digits = jnp.concatenate([views // 16, views % 16])
    fixed = jnp.zeros(column.shape, jnp.int32).at[1 : 1 + 2 * angle_total].set(digits)
    fixed = fixed.astype(jnp.bfloat16)

    def info_row(index_column):
        return jnp.where(column[None, :] == 0, index_column[:, None], fixed[None, :])

    planes, lines_here, length = activity.shape
    bins = measured.shape[3]
    row = planes * bins
    tof_kernel = kernels(subset_views[0], bins, length)
    angle_count = tof_kernel.shape[0]
    pairs = angle_count * lines_here

    slab_count = lax.axis_size("slab")
    block_total = measured.shape[1]
    capacity = 2 * block_total // slab_count
    slots = slab_count * capacity
    targets = block_slab[0, :, 0]
    onehot = (targets[:, None] == jnp.arange(slab_count, dtype=jnp.int32)[None, :]).astype(
        jnp.int32
    )
    slot_pos = jnp.sum((jnp.cumsum(onehot, axis=0) - onehot) * onehot, axis=1)
    flat_slot = targets * capacity + slot_pos
    place = (jnp.arange(slots, dtype=jnp.int32)[:, None] == flat_slot[None, :]).astype(
        jnp.bfloat16
    )
    pair_id = block_angle[0] * lines_here + block_line[0]
    extra = 128
    tag = jnp.broadcast_to(pair_id.astype(jnp.bfloat16)[:, None], (block_total, extra))
    outgoing = jnp.concatenate([measured[0].reshape(block_total, row), tag], axis=1)
    send = jnp.concatenate(
        [jnp.dot(place[k::capacity], outgoing, preferred_element_type=jnp.float32)
         for k in range(capacity)], axis=1,
    ).astype(jnp.bfloat16)
    send, activity_late = lax.optimization_barrier((send, activity))
    padded = with_halo(activity_late, (("slab", 0),), 1)
    blurred = ((1.0 - 2.0 * weight) * activity + weight * (padded[:-2] + padded[2:])).astype(
        jnp.bfloat16
    )
    projected = jnp.einsum("zlv,atv->zalt", blurred, tof_kernel, preferred_element_type=jnp.float32)
    projected = projected.reshape(planes, pairs, bins)
    recv = lax.all_to_all(send, "slab", 0, 0, tiled=True)
    recv = jnp.concatenate(
        [recv[:, k * (row + extra) : (k + 1) * (row + extra)] for k in range(capacity)], axis=0
    )
    index = recv[:, row].astype(jnp.int32)
    rows = recv[:, :row].reshape(slots, planes, bins).transpose(1, 0, 2)
    rows = lax.optimization_barrier(rows)
    pick = (index[:, None] == jnp.arange(pairs, dtype=jnp.int32)[None, :]).astype(jnp.float32)
    pick = jnp.broadcast_to(pick[None], (planes, slots, pairs))
    estimate = jnp.einsum("zjp,zpt->zjt", pick, projected, precision=lax.Precision.HIGH)
    ratios = rows.astype(jnp.float32) / (estimate + BACKGROUND)

    same = index[:, None] == index[None, :]
    earlier = jnp.arange(slots)[None, :] < jnp.arange(slots)[:, None]
    first = ~jnp.any(same & earlier, axis=1)
    merge = jnp.broadcast_to((same & first[:, None]).astype(jnp.float32)[None], (planes, slots, slots))
    merged = jnp.einsum(
        "zij,zjt->zit", merge, ratios, precision=lax.Precision.HIGH
    ).astype(jnp.bfloat16)

    payload = jnp.concatenate([merged, info_row(recv[:, row])[None]], axis=0)
    def back_project(got, kernel_k):
        index_k = got[planes, :, 0].astype(jnp.int32)
        order = jnp.arange(pairs, dtype=jnp.int32)
        wanted = (order % angle_count) * lines_here + order // angle_count
        scatter = (wanted[:, None] == index_k[None, :]).astype(jnp.bfloat16)
        scatter = jnp.broadcast_to(scatter[None], (planes, pairs, slots))
        dense = jnp.einsum(
            "zpi,zit->zpt", scatter, got[:planes], preferred_element_type=jnp.float32
        ).astype(jnp.bfloat16)
        dense = dense.reshape(planes, lines_here, angle_count, bins)
        return jnp.einsum("zlat,atv->zlv", dense, kernel_k, preferred_element_type=jnp.float32)

    def kernel_of(got):
        tail = got[planes, 0].astype(jnp.int32)
        views_k = tail[1 : 1 + angle_count] * 16 + tail[1 + angle_count : 1 + 2 * angle_count]
        return kernels(views_k, bins, length)

    view_count = lax.axis_size("view")
    rightward = [(i, (i + 1) % view_count) for i in range(view_count)]
    leftward = [(i, (i + view_count - 1) % view_count) for i in range(view_count)]
    half = (planes + 1) // 2
    from_left = lax.ppermute(payload, "view", rightward)
    from_right = lax.ppermute(payload, "view", leftward)
    total = back_project(payload, tof_kernel)
    total, from_left, from_right = lax.optimization_barrier((total, from_left, from_right))
    far_low = lax.ppermute(from_left[:half], "view", rightward)
    far_high = lax.ppermute(from_right[half:], "view", leftward)
    total = total + back_project(from_left, kernel_of(from_left))
    total = total + back_project(from_right, kernel_of(from_right))
    total, far_low, far_high = lax.optimization_barrier((total, far_low, far_high))
    far = jnp.concatenate([far_low, far_high], axis=0)
    total = total + back_project(far, kernel_of(far))
    edges = with_halo(weight * total, (("slab", 0),), 1)
    smoothed = (1.0 - 2.0 * weight) * total + edges[:-2] + edges[2:]
    return activity * smoothed / sensitivity


def solution(mesh):
    in_specs = (
        P("slab", None, None),
        P("slab", None, None),
        P("slab"),
        P("view", "slab", None, None),
        P("view", "slab", None),
        P("view", "slab"),
        P("view", "slab"),
        P("view", None),
    )
    out_specs = P("slab", None, None)
    return jax.shard_map(
        on_device, mesh=mesh, in_specs=in_specs, out_specs=out_specs, check_vma=False
    )
```
